32 devices in a mesh: fsdp: 4 (over z), ctx: 8 (over y, x, core).
Axes of the slice: x: 2, y: 2, z: 4, core: 2. Of those that a mesh axis runs over, the one named last changes fastest.
Arguments:
- hidden_in: bfloat16 [4, 1024, 1024], P('fsdp', 'ctx'), may hold values from -6 to 6
- pair_table: int32 [8, 2], replicated, may hold values from 0 to 15, as said below
- attn_gain: float32 [1024], replicated, may hold values from 0.5 to 1.5
- query_proj: bfloat16 [1024, 2048], P('fsdp'), may hold values from -0.1875 to 0.1875
- key_proj: bfloat16 [1024, 1024], P('fsdp'), may hold values from -0.1875 to 0.1875
- value_proj: bfloat16 [1024, 1024], P('fsdp'), may hold values from -0.1875 to 0.1875
- query_gain: float32 [128], replicated, may hold values from 0.6 to 5
- key_gain: float32 [128], replicated, may hold values from 0.6 to 5
- output_proj: bfloat16 [1024, 2048], P('fsdp'), may hold values from -2 to 2
- mlp_gain: float32 [1024], replicated, may hold values from 0.5 to 1.5
- gate_proj: bfloat16 [1024, 3072], P('fsdp'), may hold values from -0.1875 to 0.1875
- up_proj: bfloat16 [1024, 3072], P('fsdp'), may hold values from -0.1875 to 0.1875
- down_proj: bfloat16 [1024, 3072], P('fsdp'), may hold values from -0.109375 to 0.109375
- cotangent: bfloat16 [4, 1024, 1024], P('fsdp', 'ctx'), may hold values from -6 to 6
Outputs:
- block_out: bfloat16 [4, 1024, 1024], P('fsdp', 'ctx')
- input_grad: float32 [4, 1024, 1024], P('fsdp', 'ctx')
- attn_gain_grad: float32 [1024], replicated
- query_proj_grad: float32 [1024, 2048], P('fsdp')
- key_proj_grad: float32 [1024, 1024], P('fsdp')
- value_proj_grad: float32 [1024, 1024], P('fsdp')
- query_gain_grad: float32 [128], replicated
- key_gain_grad: float32 [128], replicated
- output_proj_grad: float32 [1024, 2048], P('fsdp')
- mlp_gain_grad: float32 [1024], replicated
- gate_proj_grad: float32 [1024, 3072], P('fsdp')
- up_proj_grad: float32 [1024, 3072], P('fsdp')
- down_proj_grad: float32 [1024, 3072], P('fsdp')
The draws below stay inside these ranges and needn't reach their ends.
Inputs may be any that keep to these rules, and one draw needn't show every extreme that they name: `pair_table`: row c is (p, 15 - p); the p of the rows are 0 to 7, each once.
All inputs are finite; a program needn't handle non-finite values.
Results may differ from the reference program's by a relative error of at most 0.028.
The reference program's roundings to bfloat16 on the way (of `attn_in`, `probs`, `attn_mix`, `mlp_in`, `hidden_act` and `score_grad`) count: a program that leaves them out, or rounds other values in their place, can miss the bound.
Values may be sent and summed in bfloat16 or wider, within the bound.
No kernel may reach another device: no remote copies, remote signals or barrier semaphores. Data moves between devices by JAX's collectives and lax.ppermute only.
A program may use at most 320 MiB of HBM per device.

```python
import math
import jax
import jax.numpy as jnp
from jax import lax

D = 1024
HQ = 16
HK = 8
HD = 128
FF = 3072
BLK = 64
PAIRS = 8
SEQ = 1024
SEQS = 4


def draw_pair_table(key, part):
    order = jax.random.permutation(jax.random.fold_in(key, 13), PAIRS).astype(jnp.int32)
    return jnp.stack([order, 2 * PAIRS - 1 - order], axis=1).astype(jnp.int32)


def draw_query_gain(key, part):
    salted = jax.random.fold_in(key, 11)
    return jnp.exp(jax.random.uniform(salted, (HD,), jnp.float32, -0.51, 0.47))


def draw_key_gain(key, part):
    salted = jax.random.fold_in(key, 12)
    return jnp.exp(jax.random.uniform(salted, (HD,), jnp.float32, -0.51, 0.47))


def spiked(drawn, own_key, source, target, shards_of, factor):
    def block_of(position):
        return (jnp.arange(drawn.shape[position]) // (drawn.shape[position] // shards_of)).reshape((-1,) + (1,) * (drawn.ndim - 1 - position))

    one_side = jax.random.permutation(own_key, shards_of)[block_of(target)]
    other_side = (block_of(target) + shards_of // 2) % shards_of
    return jnp.where((block_of(source) == one_side) | (block_of(source) == other_side), factor * drawn, drawn)


def block_scale(rng, dims, cuts, least, high):
    factor_of = 1.0
    for position, shards_of in cuts:
        draws = jax.random.uniform(jax.random.fold_in(jax.random.fold_in(rng, 6), position), (shards_of,), jnp.float32, least / len(cuts), high / len(cuts))
        factor_of = factor_of * jnp.repeat(jnp.exp(draws), dims[position] // shards_of).reshape((-1,) + (1,) * (len(dims) - 1 - position))
    return factor_of


def centred(stream_key, shape, deviation, limit, pieces=(), kind=jnp.bfloat16):
    level = block_scale(stream_key, shape, pieces, -0.22, 0.18) if pieces else 1.0
    array = jax.random.normal(stream_key, shape, jnp.float32) * deviation * level
    return jnp.minimum(jnp.maximum(array, -limit), limit).astype(kind)


def bell_draw_with(own_key, shape, scale, most, split, heavy, kind=jnp.bfloat16):
    array = scale * jax.random.normal(own_key, shape, jnp.float32)
    if split:
        array = array * block_scale(own_key, shape, split, -0.22, 0.18)
    return jnp.clip(spiked(array, jax.random.fold_in(own_key, 3), *heavy), -most, most).astype(kind)


def setup_inputs(seed: int = 0) -> dict:
    splits = jax.random.split(jax.random.key(seed), 15)
    return {
        "hidden_in": centred(splits[0], (SEQS, SEQ, D), 1.0, 6.0, ((0, 4), (1, 8))),
        "pair_table": draw_pair_table(jax.random.fold_in(splits[14], 71), 0),
        "attn_gain": jnp.clip(1.0 + 0.1 * jax.random.normal(splits[2], (D,), jnp.float32), 0.5, 1.5),
        "query_proj": centred(splits[3], (D, HQ * HD), D ** -0.5, 0.1875, ((0, 4),)),
        "key_proj": centred(splits[4], (D, HK * HD), D ** -0.5, 0.1875, ((0, 4),)),
        "value_proj": centred(splits[5], (D, HK * HD), D ** -0.5, 0.1875, ((0, 4),)),
        "query_gain": draw_query_gain(jax.random.fold_in(splits[14], 71), 0),
        "key_gain": draw_key_gain(jax.random.fold_in(splits[14], 71), 0),
        "output_proj": centred(splits[8], (D, HQ * HD), (max(HQ * HD // 256, 1)) ** -0.5, 2.0, ((0, 4),)),
        "mlp_gain": jnp.clip(1.0 + 0.1 * jax.random.normal(splits[9], (D,), jnp.float32), 0.5, 1.5),
        "gate_proj": centred(splits[10], (D, FF), D ** -0.5, 0.1875, ((0, 4),)),
        "up_proj": centred(splits[11], (D, FF), D ** -0.5, 0.1875, ((0, 4),)),
        "down_proj": centred(splits[12], (D, FF), FF ** -0.5, 0.109375, ((0, 4),)),
        "cotangent": bell_draw_with(splits[13], (SEQS, SEQ, D), 1.0, 6.0, ((0, 4), (1, 8)), (0, 2, 4, 2.0)),
    }


NORM_EPS = 1e-06
ROPE_BASE = 1000000.0
MASKED = -1e+30

def to_bf16(values):
    return lax.optimization_barrier(values.astype(jnp.bfloat16))

def rms_norm(values, gain_vec):
    return values * lax.rsqrt(lax.optimization_barrier(jnp.mean(values * values, axis=-1, keepdims=True)) + NORM_EPS) * gain_vec

def rotate(values, angles):
    half_width = values.shape[-1] // 2
    cosine = jnp.cos(angles)[:, None, :]
    sine_part = jnp.sin(angles)[:, None, :]
    first_half = values[..., :half_width]
    second_half = values[..., half_width:]
    return jnp.concatenate([first_half * cosine - second_half * sine_part, second_half * cosine + first_half * sine_part], axis=-1)

def head_prep(raw_heads, gain_vec, angles):
    return rotate(rms_norm(raw_heads, gain_vec), angles)

def angle_table(positions, head_width):
    half_width = head_width // 2
    frequency = ROPE_BASE ** (-(jnp.arange(half_width, dtype=jnp.float32) * 2.0 / head_width))
    return positions.astype(jnp.float32)[:, None] * frequency[None, :]

def token_positions(pair_table, row_count, block_len):
    index_rows = jnp.arange(row_count, dtype=jnp.int32)
    owners = index_rows // (2 * block_len)
    halves = index_rows // block_len % 2
    return pair_table[owners, halves] * block_len + index_rows % block_len

def times_transposed(lhs_mat, rhs_mat):
    return lax.dot_general(lhs_mat, rhs_mat, (((1,), (1,)), ((), ())), preferred_element_type=jnp.float32)

def transposed_times(lhs_mat, rhs_mat):
    return lax.dot_general(lhs_mat, rhs_mat, (((0,), (0,)), ((), ())), preferred_element_type=jnp.float32)

def grouped_heads(query_heads, kv_count):
    return query_heads.reshape(query_heads.shape[0], kv_count, query_heads.shape[1] // kv_count, query_heads.shape[2])

def masked_scores(query_blk, key_heads, query_pos, key_pos):
    grouped = grouped_heads(query_blk, key_heads.shape[1])
    score_scale = 1.0 / math.sqrt(query_blk.shape[2])
    raw_scores = jnp.einsum('qhgd,khd->hgqk', grouped.astype(jnp.float32), key_heads.astype(jnp.float32)) * score_scale
    allowed = key_pos[None, :] <= query_pos[:, None]
    return jnp.where(allowed[None, None], raw_scores, MASKED)

def attend_block(query_blk, query_pos, key_heads, value_heads, key_pos):
    scores = masked_scores(query_blk, key_heads, query_pos, key_pos)
    row_max = lax.optimization_barrier(jnp.max(scores, axis=-1, keepdims=True))
    row_sum = lax.optimization_barrier(jnp.sum(jnp.exp(scores - row_max), axis=-1, keepdims=True))
    log_total = row_max + jnp.log(row_sum)
    probs = to_bf16(jnp.exp(scores - log_total))
    mixed = jnp.einsum('hgqk,khd->qhgd', probs.astype(jnp.float32), value_heads.astype(jnp.float32))
    return (mixed.reshape(query_blk.shape[0], -1), log_total[..., 0])

def attend_back(query_blk, query_pos, mix_blk, dmix_blk, lse_blk, key_heads, value_heads, key_pos):
    kv_count = key_heads.shape[1]
    score_scale = 1.0 / math.sqrt(query_blk.shape[2])
    scores = masked_scores(query_blk, key_heads, query_pos, key_pos)
    probs = jnp.exp(scores - lse_blk[..., None])
    probs_low = to_bf16(probs)
    dmix_heads = grouped_heads(dmix_blk.reshape(query_blk.shape), kv_count).astype(jnp.float32)
    mix_heads = grouped_heads(mix_blk.reshape(query_blk.shape), kv_count).astype(jnp.float32)
    delta = jnp.einsum('qhgd,qhgd->hgq', dmix_heads, mix_heads)
    value_part = jnp.einsum('hgqk,qhgd->khd', probs_low.astype(jnp.float32), dmix_heads)
    prob_grad = jnp.einsum('qhgd,khd->hgqk', dmix_heads, value_heads.astype(jnp.float32))
    score_grad = to_bf16(probs * (prob_grad - delta[..., None]) * score_scale).astype(jnp.float32)
    query_part = jnp.einsum('hgqk,khd->qhgd', score_grad, key_heads.astype(jnp.float32))
    key_part = jnp.einsum('hgqk,qhgd->khd', score_grad, grouped_heads(query_blk, kv_count).astype(jnp.float32))
    return (query_part.reshape(query_blk.shape), key_part, value_part)

def reference(hidden_in, pair_table, attn_gain, query_proj, key_proj, value_proj, query_gain, key_gain, output_proj, mlp_gain, gate_proj, up_proj, down_proj, cotangent):
    positions = token_positions(pair_table, SEQ, BLK)
    angles = angle_table(positions, HD)
    query_block = math.gcd(SEQ, 512)
    block_count = SEQ // query_block
    pos_blocks = positions.reshape(block_count, query_block)

    def head_query(raw_heads, gain_vec):
        return head_prep(raw_heads, gain_vec, angles)

    def one_sequence(totals, seq_data):
        inputs, cot_low = seq_data
        input_wide = inputs.astype(jnp.float32)
        attn_in = to_bf16(rms_norm(input_wide, attn_gain))
        query_raw = jnp.dot(attn_in, query_proj, preferred_element_type=jnp.float32).reshape(SEQ, HQ, HD)
        key_raw = jnp.dot(attn_in, key_proj, preferred_element_type=jnp.float32).reshape(SEQ, HK, HD)
        value_raw = jnp.dot(attn_in, value_proj, preferred_element_type=jnp.float32).reshape(SEQ, HK, HD)
        query_heads = to_bf16(head_query(query_raw, query_gain))
        key_heads = to_bf16(head_query(key_raw, key_gain))
        value_heads = to_bf16(value_raw)

        def forward_block(state_zero, blk_data):
            query_blk, qpos_blk = blk_data
            return (state_zero, attend_block(query_blk, qpos_blk, key_heads, value_heads, positions))
        unused, (mixed_blocks, lse_blocks) = lax.scan(forward_block, jnp.zeros((), jnp.float32), (query_heads.reshape(block_count, query_block, HQ, HD), pos_blocks))
        attn_mix = to_bf16(mixed_blocks.reshape(SEQ, HQ * HD))
        resid = input_wide + times_transposed(attn_mix, output_proj)
        mlp_in = to_bf16(rms_norm(resid, mlp_gain))
        gate = jnp.dot(mlp_in, gate_proj, preferred_element_type=jnp.float32)
        upper = jnp.dot(mlp_in, up_proj, preferred_element_type=jnp.float32)
        sigma = jax.nn.sigmoid(gate)
        hidden_act = to_bf16(gate * sigma * upper)
        block_out = (resid + times_transposed(hidden_act, down_proj)).astype(jnp.bfloat16)
        hidden_grad = jnp.dot(cot_low, down_proj, preferred_element_type=jnp.float32)
        gate_low = to_bf16(hidden_grad * upper * sigma * (1.0 + gate * (1.0 - sigma)))
        upper_low = to_bf16(hidden_grad * gate * sigma)
        mlp_in_grad = times_transposed(gate_low, gate_proj) + times_transposed(upper_low, up_proj)
        mlp_back = jax.vjp(rms_norm, resid, mlp_gain)[1]
        resid_part, mlp_gain_grad = mlp_back(mlp_in_grad)
        resid_grad = cot_low.astype(jnp.float32) + resid_part
        resid_low = to_bf16(resid_grad)
        mix_grad = to_bf16(jnp.dot(resid_low, output_proj, preferred_element_type=jnp.float32))

        def backward_block(state_pair, blk_data):
            key_total, value_total = state_pair
            query_blk, qpos_blk, mix_blk, dmix_blk, lse_blk = blk_data
            query_part, key_part, value_part = attend_back(query_blk, qpos_blk, mix_blk, dmix_blk, lse_blk, key_heads, value_heads, positions)
            return ((key_total + key_part, value_total + value_part), query_part)
        zero_kv = jnp.zeros((SEQ, HK, HD), jnp.float32)
        (key_grad, value_grad), query_blocks = lax.scan(backward_block, (zero_kv, zero_kv), (query_heads.reshape(block_count, query_block, HQ, HD), pos_blocks, attn_mix.reshape(block_count, query_block, HQ * HD), mix_grad.reshape(block_count, query_block, HQ * HD), lse_blocks))
        query_grad = query_blocks.reshape(SEQ, HQ, HD)
        query_raw_grad, query_gain_grad = jax.vjp(head_query, query_raw, query_gain)[1](query_grad)
        key_raw_grad, key_gain_grad = jax.vjp(head_query, key_raw, key_gain)[1](key_grad)
        query_low = to_bf16(query_raw_grad.reshape(SEQ, HQ * HD))
        key_low = to_bf16(key_raw_grad.reshape(SEQ, HK * HD))
        value_low = to_bf16(value_grad.reshape(SEQ, HK * HD))
        attn_in_grad = times_transposed(query_low, query_proj) + times_transposed(key_low, key_proj) + times_transposed(value_low, value_proj)
        input_back = jax.vjp(rms_norm, input_wide, attn_gain)[1]
        input_part, attn_gain_grad = input_back(attn_in_grad)
        input_grad = resid_grad + input_part
        fresh = (attn_gain_grad, transposed_times(attn_in, query_low), transposed_times(attn_in, key_low), transposed_times(attn_in, value_low), query_gain_grad, key_gain_grad, transposed_times(resid_low, attn_mix), mlp_gain_grad, transposed_times(mlp_in, gate_low), transposed_times(mlp_in, upper_low), transposed_times(cot_low, hidden_act))
        totals = tuple((old + new for old, new in zip(totals, fresh)))
        return (totals, (block_out, input_grad))
    start_totals = (jnp.zeros((D,), jnp.float32), jnp.zeros((D, HQ * HD), jnp.float32), jnp.zeros((D, HK * HD), jnp.float32), jnp.zeros((D, HK * HD), jnp.float32), jnp.zeros((HD,), jnp.float32), jnp.zeros((HD,), jnp.float32), jnp.zeros((D, HQ * HD), jnp.float32), jnp.zeros((D,), jnp.float32), jnp.zeros((D, FF), jnp.float32), jnp.zeros((D, FF), jnp.float32), jnp.zeros((D, FF), jnp.float32))
    totals, (block_out, input_grad) = lax.scan(one_sequence, start_totals, (hidden_in, cotangent))
    return (block_out, input_grad, totals[0], totals[1], totals[2], totals[3], totals[4], totals[5], totals[6], totals[7], totals[8], totals[9], totals[10])
```

```python
import math

import jax
import jax.numpy as jnp
from jax import lax
from jax.sharding import PartitionSpec as P

NORM_EPS = 1e-06
ROPE_BASE = 1000000.0
MASKED = -1e30
F32 = jnp.float32
BF16 = jnp.bfloat16


def rms_norm(values, gain_vec):
    return (
        values * lax.rsqrt(jnp.mean(values * values, axis=-1, keepdims=True) + NORM_EPS) * gain_vec
    )


def rotate(values, cosine, sine_part):
    half_width = values.shape[-1] // 2
    first_half = values[..., :half_width]
    second_half = values[..., half_width:]
    return jnp.concatenate(
        [
            first_half * cosine - second_half * sine_part,
            second_half * cosine + first_half * sine_part,
        ],
        axis=-1,
    )


def times_transposed(lhs_mat, rhs_mat):
    return lax.dot_general(
        lhs_mat, rhs_mat, (((1,), (1,)), ((), ())), preferred_element_type=F32
    )


def transposed_times(lhs_mat, rhs_mat):
    return lax.dot_general(
        lhs_mat, rhs_mat, (((0,), (0,)), ((), ())), preferred_element_type=F32
    )


def times(lhs_mat, rhs_mat):
    return jnp.dot(lhs_mat, rhs_mat, preferred_element_type=F32)


def after(value, *others):
    return lax.optimization_barrier((value,) + others)[0]


def exchange(value, bit, axis):
    count = lax.axis_size(axis)
    return lax.ppermute(value, axis, [(index, index ^ bit) for index in range(count)])


def low_bit(number):
    return number & -number


def top_bit(number):
    return 1 << (number.bit_length() - 1)


def by_bits(numbers, reverse=False):
    return sorted(numbers, key=lambda number: (bin(number).count("1"), number), reverse=reverse)


def gather_ctx(own):
    count = lax.axis_size("ctx")
    half = own.shape[0] // 2
    blocks = {0: own}
    if count > 1:
        blocks[1] = exchange(own, 1, "ctx")
    for number in by_bits(range(2, count, 2)):
        low, top = low_bit(number), top_bit(number)
        if low == top:
            blocks[number] = exchange(own, low, "ctx")
        else:
            blocks[number] = jnp.concatenate(
                [
                    exchange(blocks[number ^ top][:half], top, "ctx"),
                    exchange(blocks[number ^ low][half:], low, "ctx"),
                ],
                axis=0,
            )
        blocks[number + 1] = exchange(blocks[number], 1, "ctx")
    return [blocks[number] for number in range(count)]


def scatter_ctx(blocks):
    count = len(blocks)
    half = blocks[0].shape[0] // 2
    sums = {}
    for number in by_bits(range(0, count, 2), True):
        sums[number] = blocks[number].astype(F32) + exchange(
            blocks[number + 1].astype(BF16), 1, "ctx"
        ).astype(F32)
    halves = {number: [sums[number][:half], sums[number][half:]] for number in sums}
    for number in by_bits(range(2, count, 2), True):
        low, top = low_bit(number), top_bit(number)
        first, second = (part.astype(BF16) for part in halves[number])
        if low == top:
            moved = exchange(jnp.concatenate([first, second], axis=0), low, "ctx").astype(F32)
            halves[0][0] = halves[0][0] + moved[:half]
            halves[0][1] = halves[0][1] + moved[half:]
        else:
            halves[number ^ top][0] = halves[number ^ top][0] + exchange(first, top, "ctx").astype(
                F32
            )
            halves[number ^ low][1] = halves[number ^ low][1] + exchange(
                second, low, "ctx"
            ).astype(F32)
    return jnp.concatenate(halves[0], axis=0)


def gather_fsdp(own):
    count = lax.axis_size("fsdp")
    blocks = {0: own}
    for number in by_bits(range(1, count)):
        low = low_bit(number)
        blocks[number] = exchange(blocks[number ^ low], low, "fsdp")
    return [blocks[number] for number in range(count)]


def scatter_fsdp(blocks):
    sums = {number: block for number, block in enumerate(blocks)}
    for number in by_bits(range(1, len(blocks)), True):
        low = low_bit(number)
        sums[number ^ low] = sums[number ^ low].astype(F32) + exchange(
            sums[number].astype(BF16), low, "fsdp"
        ).astype(F32)
    return sums[0]


def sum_all(value):
    for axis in ("ctx", "fsdp"):
        bit = 1
        while bit < lax.axis_size(axis):
            value = value + exchange(value, bit, axis)
            bit *= 2
    return value


def on_device(
    hidden_in,
    pair_table,
    attn_gain,
    query_proj,
    key_proj,
    value_proj,
    query_gain,
    key_gain,
    output_proj,
    mlp_gain,
    gate_proj,
    up_proj,
    down_proj,
    cotangent,
):
    fsdp_count = lax.axis_size("fsdp")
    fsdp_index = lax.axis_index("fsdp")
    ctx_count = lax.axis_size("ctx")
    ctx_index = lax.axis_index("ctx")
    row_count, width = hidden_in.shape[1:]
    block_len = row_count // 2
    total_rows = ctx_count * row_count
    shard_rows = width // fsdp_count
    head_width = query_gain.shape[0]
    half_head = head_width // 2
    query_total = query_proj.shape[1] // head_width
    kvhead_total = key_proj.shape[1] // head_width
    query_count = query_total // ctx_count
    kv_count = max(1, kvhead_total // ctx_count)
    kv_share = max(1, ctx_count // kvhead_total)
    group_size = query_count // kv_count
    score_scale = 1.0 / math.sqrt(head_width)
    query_width = query_proj.shape[1] // ctx_count
    kv_width = kv_count * head_width
    kv_own = key_proj.shape[1] // ctx_count
    hidden_width = gate_proj.shape[1] // ctx_count

    def block_order(values):
        return jnp.concatenate(
            [
                lax.dynamic_slice_in_dim(
                    values, (fsdp_index ^ number) * shard_rows, shard_rows, axis=values.ndim - 1
                )
                for number in range(fsdp_count)
            ],
            axis=-1,
        )

    def columns(weights, start, size):
        return lax.dynamic_slice_in_dim(weights, start, size, axis=1)

    kv_start = (ctx_index // kv_share) * kv_width
    inputs = block_order(hidden_in[0])
    cot_low = block_order(cotangent[0])
    attn_gain_rel = block_order(attn_gain)
    mlp_gain_rel = block_order(mlp_gain)

    input_blocks = gather_ctx(inputs)
    attn_shard = jnp.concatenate(
        [
            columns(query_proj, ctx_index * query_width, query_width),
            columns(key_proj, kv_start, kv_width),
            columns(value_proj, kv_start, kv_width),
        ],
        axis=1,
    )
    attn_w = jnp.concatenate(gather_fsdp(attn_shard), axis=0)
    output_shard = columns(output_proj, ctx_index * query_width, query_width)
    output_w = jnp.concatenate(gather_fsdp(after(output_shard, attn_w)), axis=0)
    mlp_shard = jnp.concatenate(
        [
            columns(weights, ctx_index * hidden_width, hidden_width)
            for weights in (gate_proj, up_proj, down_proj)
        ],
        axis=1,
    )
    mlp_w = jnp.concatenate(gather_fsdp(after(mlp_shard, output_w)), axis=0)
    gate_upper_w = mlp_w[:, : 2 * hidden_width]
    down_w = mlp_w[:, 2 * hidden_width :]

    owner_ids = ctx_index ^ jnp.arange(ctx_count, dtype=jnp.int32)
    picked = owner_ids[:, None] == jnp.arange(ctx_count, dtype=jnp.int32)[None, :]
    block_ids = jnp.sum(jnp.where(picked[:, :, None], pair_table[None], 0), axis=1)
    positions = (
        block_ids[:, :, None] * block_len + jnp.arange(block_len, dtype=jnp.int32)
    ).reshape(total_rows)
    frequency = ROPE_BASE ** (-(jnp.arange(half_head, dtype=F32) * 2.0 / head_width))
    angles = positions.astype(F32)[:, None] * frequency[None, :]
    cosine = jnp.cos(angles)[:, None, :]
    sine_part = jnp.sin(angles)[:, None, :]

    def head_prep(raw_heads, gain_vec):
        return rotate(rms_norm(raw_heads, gain_vec), cosine, sine_part)

    input_wide = jnp.concatenate(input_blocks, axis=0).astype(F32)
    attn_in = rms_norm(input_wide, attn_gain_rel).astype(BF16)
    attn_raw = times(attn_in, attn_w)
    cot_all = jnp.concatenate(gather_ctx(after(cot_low, attn_raw)), axis=0)
    query_raw = attn_raw[:, :query_width].reshape(total_rows, query_count, head_width)
    key_raw = attn_raw[:, query_width : query_width + kv_width].reshape(
        total_rows, kv_count, head_width
    )
    value_heads = (
        attn_raw[:, query_width + kv_width :].astype(BF16).reshape(total_rows, kv_count, head_width)
    )
    query_heads = head_prep(query_raw, query_gain).astype(BF16)
    key_heads = head_prep(key_raw, key_gain).astype(BF16)
    grouped_query = query_heads.reshape(total_rows, kv_count, group_size, head_width)
    allowed = (positions[None, :] <= positions[:, None])[None, None]
    scores = (
        jnp.einsum("qhgd,khd->hgqk", grouped_query, key_heads, preferred_element_type=F32)
        * score_scale
    )
    scores = jnp.where(allowed, scores, MASKED)
    row_max = jnp.max(scores, axis=-1, keepdims=True)
    row_sum = jnp.sum(jnp.exp(scores - row_max), axis=-1, keepdims=True)
    log_total = row_max + jnp.log(row_sum)
    probs = jnp.exp(scores - log_total)
    probs_low = probs.astype(BF16)
    attn_mix = (
        jnp.einsum("hgqk,khd->qhgd", probs_low, value_heads, preferred_element_type=F32)
        .reshape(total_rows, query_width)
        .astype(BF16)
    )

    def split_rows(values):
        return [
            values[number * row_count : (number + 1) * row_count] for number in range(ctx_count)
        ]

    def split_shards(values):
        return [
            values[number * shard_rows : (number + 1) * shard_rows]
            for number in range(fsdp_count)
        ]

    resid = inputs.astype(F32) + scatter_ctx(
        split_rows(times_transposed(attn_mix, output_w).astype(BF16))
    )
    mlp_in = rms_norm(resid, mlp_gain_rel).astype(BF16)
    mlp_in_all = jnp.concatenate(gather_ctx(mlp_in), axis=0)
    hidden_grad = times(cot_all, down_w)
    gate_upper = times(mlp_in_all, gate_upper_w)
    gate = gate_upper[:, :hidden_width]
    upper = gate_upper[:, hidden_width:]
    sigma = jax.nn.sigmoid(gate)
    hidden_act = (gate * sigma * upper).astype(BF16)
    gate_low = (hidden_grad * upper * sigma * (1.0 + gate * (1.0 - sigma))).astype(BF16)
    upper_low = (hidden_grad * gate * sigma).astype(BF16)
    mlp_right = jnp.concatenate([gate_low, upper_low], axis=1)
    mlp_in_grad = scatter_ctx(split_rows(times_transposed(mlp_right, gate_upper_w).astype(BF16)))
    resid_part, mlp_gain_grad = jax.vjp(rms_norm, resid, mlp_gain_rel)[1](mlp_in_grad)
    resid_grad = cot_low.astype(F32) + resid_part
    resid_low = resid_grad.astype(BF16)
    resid_all = jnp.concatenate(gather_ctx(resid_low), axis=0)

    mlp_grads = scatter_fsdp(
        split_shards(
            jnp.concatenate(
                [
                    transposed_times(mlp_in_all, mlp_right),
                    transposed_times(cot_all, hidden_act),
                ],
                axis=1,
            ).astype(BF16)
        )
    ).astype(BF16)

    mix_grad = times(resid_all, output_w).astype(BF16)
    block_part = times_transposed(hidden_act, down_w).astype(BF16)
    block_sum = scatter_ctx(split_rows(after(block_part, mix_grad)))
    block_out = (resid + block_sum).astype(BF16)
    output_grads = scatter_fsdp(
        split_shards(transposed_times(resid_all, attn_mix).astype(BF16))
    ).astype(BF16)

    dmix_heads = mix_grad.reshape(total_rows, kv_count, group_size, head_width)
    delta = jnp.einsum(
        "qhgd,qhgd->hgq",
        dmix_heads,
        attn_mix.reshape(total_rows, kv_count, group_size, head_width),
        preferred_element_type=F32,
    )
    value_grad = jnp.einsum("hgqk,qhgd->khd", probs_low, dmix_heads, preferred_element_type=F32)
    prob_grad = jnp.einsum("qhgd,khd->hgqk", dmix_heads, value_heads, preferred_element_type=F32)
    score_grad = (probs * (prob_grad - delta[..., None]) * score_scale).astype(BF16)
    query_grad = jnp.einsum("hgqk,khd->qhgd", score_grad, key_heads, preferred_element_type=F32)
    key_grad = jnp.einsum("hgqk,qhgd->khd", score_grad, grouped_query, preferred_element_type=F32)
    bit = 1
    while bit < kv_share:
        both = jnp.concatenate([key_grad, value_grad], axis=1)
        moved = exchange(both, bit, "ctx").reshape((ctx_count, row_count) + both.shape[1:])
        moved = jnp.concatenate([moved[number ^ bit] for number in range(ctx_count)], axis=0)
        key_grad = key_grad + moved[:, :kv_count]
        value_grad = value_grad + moved[:, kv_count:]
        bit *= 2
    query_raw_grad, query_gain_grad = jax.vjp(head_prep, query_raw, query_gain)[1](
        query_grad.reshape(total_rows, query_count, head_width)
    )
    key_raw_grad, key_gain_grad = jax.vjp(head_prep, key_raw, key_gain)[1](key_grad)
    query_low = query_raw_grad.reshape(total_rows, -1).astype(BF16)
    key_low = key_raw_grad.reshape(total_rows, -1).astype(BF16)
    value_low = value_grad.reshape(total_rows, -1).astype(BF16)
    attn_own_w = attn_w
    if kv_share > 1:
        own_start = (ctx_index % kv_share) * kv_own
        key_low = columns(key_low, own_start, kv_own)
        value_low = columns(value_low, own_start, kv_own)
        attn_own_w = jnp.concatenate(
            [
                attn_w[:, :query_width],
                columns(attn_w, query_width + own_start, kv_own),
                columns(attn_w, query_width + kv_width + own_start, kv_own),
            ],
            axis=1,
        )
        key_gain_grad = jnp.where(ctx_index % kv_share == 0, key_gain_grad, 0.0)
    attn_right = jnp.concatenate([query_low, key_low, value_low], axis=1)
    attn_grads = scatter_fsdp(
        split_shards(transposed_times(attn_in, attn_right).astype(BF16))
    ).astype(BF16)
    attn_in_part = times_transposed(attn_right, attn_own_w)
    attn_in_grad = scatter_ctx(split_rows(attn_in_part.astype(BF16)))
    own_wide = inputs.astype(F32)
    input_part = jax.vjp(lambda values: rms_norm(values, attn_gain_rel), own_wide)[1](
        attn_in_grad
    )[0]
    input_grad = resid_grad + input_part
    attn_gain_grad = jnp.sum(
        attn_in_part
        * (
            input_wide
            * lax.rsqrt(jnp.mean(input_wide * input_wide, axis=-1, keepdims=True) + NORM_EPS)
        ),
        axis=0,
    )
    gains = sum_all(
        jnp.concatenate(
            [
                block_order(attn_gain_grad),
                block_order(mlp_gain_grad),
                query_gain_grad,
                key_gain_grad,
            ]
        )
    )

    def natural(blocks, start, size):
        stacked = jnp.stack([block[:, start : start + size] for block in blocks])
        return jnp.concatenate(
            [
                lax.dynamic_index_in_dim(stacked, ctx_index ^ number, 0, keepdims=False)
                for number in range(ctx_count)
            ],
            axis=1,
        ).astype(F32)

    attn_blocks = gather_ctx(attn_grads)
    output_blocks = gather_ctx(output_grads)
    mlp_blocks = gather_ctx(mlp_grads)
    return (
        block_order(block_out)[None],
        block_order(input_grad)[None],
        gains[:width],
        natural(attn_blocks, 0, query_width),
        natural(attn_blocks, query_width, kv_own),
        natural(attn_blocks, query_width + kv_own, kv_own),
        gains[2 * width : 2 * width + head_width],
        gains[2 * width + head_width :],
        natural(output_blocks, 0, query_width),
        gains[width : 2 * width],
        natural(mlp_blocks, 0, hidden_width),
        natural(mlp_blocks, hidden_width, hidden_width),
        natural(mlp_blocks, 2 * hidden_width, hidden_width),
    )


def solution(mesh):
    in_specs = (
        P("fsdp", "ctx", None),
        P(),
        P(),
        P("fsdp", None),
        P("fsdp", None),
        P("fsdp", None),
        P(),
        P(),
        P("fsdp", None),
        P(),
        P("fsdp", None),
        P("fsdp", None),
        P("fsdp", None),
        P("fsdp", "ctx", None),
    )
    out_specs = (
        P("fsdp", "ctx", None),
        P("fsdp", "ctx", None),
        P(),
        P("fsdp", None),
        P("fsdp", None),
        P("fsdp", None),
        P(),
        P(),
        P("fsdp", None),
        P(),
        P("fsdp", None),
        P("fsdp", None),
        P("fsdp", None),
    )
    return jax.shard_map(
        on_device, mesh=mesh, in_specs=in_specs, out_specs=out_specs, check_vma=False
    )
```

```python
import math

import jax
import jax.numpy as jnp
from jax import lax
from jax.experimental import pallas as pl
from jax.experimental.pallas import tpu as pltpu
from jax.sharding import PartitionSpec as P

NORM_EPS = 1e-06
ROPE_BASE = 1000000.0
MASKED = -1e30
F32 = jnp.float32
BF16 = jnp.bfloat16


def rms_norm(values, gain_vec):
    return (
        values * lax.rsqrt(jnp.mean(values * values, axis=-1, keepdims=True) + NORM_EPS) * gain_vec
    )


def rotate(values, cosine, sine_part):
    half_width = values.shape[-1] // 2
    first_half = values[..., :half_width]
    second_half = values[..., half_width:]
    return jnp.concatenate(
        [
            first_half * cosine - second_half * sine_part,
            second_half * cosine + first_half * sine_part,
        ],
        axis=-1,
    )


def times_transposed(lhs_mat, rhs_mat):
    return lax.dot_general(
        lhs_mat, rhs_mat, (((1,), (1,)), ((), ())), preferred_element_type=F32
    )


def transposed_times(lhs_mat, rhs_mat):
    return lax.dot_general(
        lhs_mat, rhs_mat, (((0,), (0,)), ((), ())), preferred_element_type=F32
    )


def times(lhs_mat, rhs_mat):
    return jnp.dot(lhs_mat, rhs_mat, preferred_element_type=F32)


def tie(*values):
    return lax.optimization_barrier(values)


def exchange(value, bit, axis):
    count = lax.axis_size(axis)
    return lax.ppermute(value, axis, [(index, index ^ bit) for index in range(count)])


def low_bit(number):
    return number & -number


def top_bit(number):
    return 1 << (number.bit_length() - 1)


def level_of(number):
    return bin(number).count("1")


def even_numbers(count, level):
    return [number for number in range(0, count, 2) if level_of(number) == level]


def gather_levels(count):
    return (count // 2).bit_length() - 1


def gather_step(blocks, count, level):
    half = blocks[0].shape[0] // 2
    blocks = dict(blocks)
    for number in even_numbers(count, level):
        low, top = low_bit(number), top_bit(number)
        if low == top:
            blocks[number] = exchange(blocks[0], low, "ctx")
        else:
            blocks[number] = jnp.concatenate(
                [
                    exchange(blocks[number ^ top][:half], top, "ctx"),
                    exchange(blocks[number ^ low][half:], low, "ctx"),
                ],
                axis=0,
            )
    return blocks


def gather_last(blocks, count):
    even = jnp.concatenate([blocks[number] for number in range(0, count, 2)], axis=0)
    return even, exchange(even, 1, "ctx")


def gather_ctx(own):
    count = lax.axis_size("ctx")
    blocks = {0: own}
    for level in range(1, gather_levels(count) + 1):
        blocks = gather_step(blocks, count, level)
    return gather_last(blocks, count)


def interleave(even, odd, count):
    rows = even.shape[0] * 2 // count
    both = jnp.stack(
        [even.reshape(count // 2, rows, -1), odd.reshape(count // 2, rows, -1)], axis=1
    )
    return both.reshape(count * rows, -1)


def split_pairs(values, count):
    rows = values.shape[0] // count
    both = values.reshape(count // 2, 2, rows, -1)
    return both[:, 0].reshape(-1, values.shape[1]), both[:, 1].reshape(-1, values.shape[1])


def scatter_ctx(even, odd):
    count = lax.axis_size("ctx")
    rows = even.shape[0] * 2 // count
    half = rows // 2
    moved = exchange(odd, 1, "ctx")

    def piece(number, start, stop):
        base = number // 2 * rows
        return even[base + start : base + stop].astype(F32) + moved[
            base + start : base + stop
        ].astype(F32)

    halves = {
        number: [piece(number, 0, half), piece(number, half, rows)]
        for number in range(0, count, 2)
    }
    for level in range(gather_levels(count), 1, -1):
        for number in even_numbers(count, level):
            low, top = low_bit(number), top_bit(number)
            first, second = (part.astype(BF16) for part in halves[number])
            halves[number ^ top][0] += exchange(first, top, "ctx").astype(F32)
            halves[number ^ low][1] += exchange(second, low, "ctx").astype(F32)
    total = jnp.concatenate(halves[0], axis=0)
    for number in even_numbers(count, 1):
        sent = jnp.concatenate(halves[number], axis=0).astype(BF16)
        total = total + exchange(sent, number, "ctx").astype(F32)
    return total


def gather_fsdp_step(blocks, count, level):
    blocks = dict(blocks)
    for number in range(1, count):
        if level_of(number) == level:
            low = low_bit(number)
            blocks[number] = exchange(blocks[number ^ low], low, "fsdp")
    return blocks


def scatter_fsdp_step(sums, count, level):
    sums = dict(sums)
    for number in range(1, count):
        if level_of(number) == level:
            low = low_bit(number)
            sums[number ^ low] = sums[number ^ low].astype(F32) + exchange(
                sums[number].astype(BF16), low, "fsdp"
            ).astype(F32)
    return sums


def sum_all(value):
    for axis in ("ctx", "fsdp"):
        bit = 1
        while bit < lax.axis_size(axis):
            value = value + exchange(value, bit, axis)
            bit *= 2
    return value


def whole(array):
    return pl.BlockSpec(array.shape, lambda *ids: (0,) * len(array.shape))


def pick_columns(picks):
    rows = picks[0][0].shape[0]
    widths = [width for _, _, width in picks]
    if any(width % 128 for width in widths):
        return jnp.concatenate(
            [
                lax.dynamic_slice_in_dim(array, index * width, width, axis=1)
                for array, index, width in picks
            ],
            axis=1,
        )

    def kernel(index_ref, *refs):
        start = 0
        for ref, width in zip(refs, widths):
            refs[-1][:, start : start + width] = ref[...]
            start += width

    def spec(number, width):
        return pl.BlockSpec((rows, width), lambda step, index_ref: (0, index_ref[number]))

    total = sum(widths)
    return pl.pallas_call(
        kernel,
        out_shape=jax.ShapeDtypeStruct((rows, total), picks[0][0].dtype),
        grid_spec=pltpu.PrefetchScalarGridSpec(
            num_scalar_prefetch=1,
            grid=(1,),
            in_specs=[spec(number, width) for number, width in enumerate(widths)],
            out_specs=pl.BlockSpec((rows, total), lambda step, index_ref: (0, 0)),
        ),
        cost_estimate=pl.CostEstimate(
            flops=0, bytes_accessed=4 * rows * total, transcendentals=0
        ),
        name="pick_columns",
    )(jnp.stack([index for _, index, _ in picks]).astype(jnp.int32), *[p[0] for p in picks])


def place_columns(blocks, widths, indices):
    count = len(blocks)
    rows = blocks[0].shape[0]
    starts = [sum(widths[:number]) for number in range(len(widths))]
    if any(width % 128 for width in widths):
        placed = []
        for start, width in zip(starts, widths):
            result = jnp.zeros((rows, count * width), F32)
            for number in range(count):
                result = lax.dynamic_update_slice_in_dim(
                    result,
                    blocks[number][:, start : start + width].astype(F32),
                    indices[number] * width,
                    axis=1,
                )
            placed.append(result)
        return placed

    def kernel(index_ref, *refs):
        for number in range(count):

            @pl.when(pl.program_id(0) == number)
            def _():
                for out_ref, start, width in zip(refs[count:], starts, widths):
                    out_ref[...] = refs[number][:, start : start + width].astype(F32)

    return pl.pallas_call(
        kernel,
        out_shape=[jax.ShapeDtypeStruct((rows, count * width), F32) for width in widths],
        grid_spec=pltpu.PrefetchScalarGridSpec(
            num_scalar_prefetch=1,
            grid=(count,),
            in_specs=[whole(block) for block in blocks],
            out_specs=[
                pl.BlockSpec((rows, width), lambda step, index_ref: (0, index_ref[step]))
                for width in widths
            ],
        ),
        cost_estimate=pl.CostEstimate(
            flops=0, bytes_accessed=6 * count * rows * sum(widths), transcendentals=0
        ),
        name="place_columns",
    )(jnp.stack(indices).astype(jnp.int32), *blocks)


def mlp_kernel(x_even, x_odd, c_even, c_odd, w_ref, right_ref, act_ref, even_ref, odd_ref):
    hidden = act_ref.shape[1]
    rows = x_even.shape[0]
    for x_ref, c_ref, part_ref, start in (
        (x_even, c_even, even_ref, 0),
        (x_odd, c_odd, odd_ref, rows),
    ):
        both = jnp.dot(x_ref[...], w_ref[:, : 2 * hidden], preferred_element_type=F32)
        grad = jnp.dot(c_ref[...], w_ref[:, 2 * hidden :], preferred_element_type=F32)
        gate = both[:, :hidden]
        upper = both[:, hidden:]
        sigma = jax.nn.sigmoid(gate)
        gate_sigma = gate * sigma
        act_ref[start : start + rows, :] = (gate_sigma * upper).astype(BF16)
        right = jnp.concatenate(
            [
                (grad * upper * sigma * (1.0 + gate * (1.0 - sigma))).astype(BF16),
                (grad * gate_sigma).astype(BF16),
            ],
            axis=1,
        )
        right_ref[start : start + rows, :] = right
        part_ref[...] = lax.dot_general(
            right,
            w_ref[:, : 2 * hidden],
            (((1,), (1,)), ((), ())),
            preferred_element_type=F32,
        ).astype(BF16)


def mlp_both(x_even, x_odd, c_even, c_odd, weights, count):
    rows = x_even.shape[0] * 2 // count
    width = x_even.shape[1]
    hidden = weights.shape[1] // 3
    total = count * rows
    block = pl.BlockSpec((rows, width), lambda step: (step, 0))
    return pl.pallas_call(
        mlp_kernel,
        out_shape=[
            jax.ShapeDtypeStruct((total, 2 * hidden), BF16),
            jax.ShapeDtypeStruct((total, hidden), BF16),
            jax.ShapeDtypeStruct(x_even.shape, BF16),
            jax.ShapeDtypeStruct(x_even.shape, BF16),
        ],
        grid=(count // 2,),
        in_specs=[block, block, block, block, whole(weights)],
        out_specs=[
            pl.BlockSpec((2 * rows, 2 * hidden), lambda step: (step, 0)),
            pl.BlockSpec((2 * rows, hidden), lambda step: (step, 0)),
            block,
            block,
        ],
        cost_estimate=pl.CostEstimate(
            flops=10 * total * width * hidden,
            bytes_accessed=8 * total * width,
            transcendentals=total * hidden,
        ),
        name="mlp_both",
    )(x_even, x_odd, c_even, c_odd, weights)


def on_device(
    hidden_in,
    pair_table,
    attn_gain,
    query_proj,
    key_proj,
    value_proj,
    query_gain,
    key_gain,
    output_proj,
    mlp_gain,
    gate_proj,
    up_proj,
    down_proj,
    cotangent,
):
    fsdp_count = lax.axis_size("fsdp")
    fsdp_index = lax.axis_index("fsdp")
    ctx_count = lax.axis_size("ctx")
    ctx_index = lax.axis_index("ctx")
    row_count, width = hidden_in.shape[1:]
    block_len = row_count // 2
    total_rows = ctx_count * row_count
    shard_rows = width // fsdp_count
    head_width = query_gain.shape[0]
    half_head = head_width // 2
    query_total = query_proj.shape[1] // head_width
    kvhead_total = key_proj.shape[1] // head_width
    query_count = query_total // ctx_count
    kv_count = max(1, kvhead_total // ctx_count)
    kv_share = max(1, ctx_count // kvhead_total)
    group_size = query_count // kv_count
    score_scale = 1.0 / math.sqrt(head_width)
    query_width = query_proj.shape[1] // ctx_count
    kv_width = kv_count * head_width
    kv_own = key_proj.shape[1] // ctx_count
    hidden_width = gate_proj.shape[1] // ctx_count

    def block_order(values):
        return jnp.concatenate(
            [
                lax.dynamic_slice_in_dim(
                    values, (fsdp_index ^ number) * shard_rows, shard_rows, axis=values.ndim - 1
                )
                for number in range(fsdp_count)
            ],
            axis=-1,
        )

    def columns(weights, start, size):
        return lax.dynamic_slice_in_dim(weights, start, size, axis=1)

    kv_index = ctx_index // kv_share
    attn_shard = pick_columns(
        [
            (query_proj, ctx_index, query_width),
            (key_proj, kv_index, kv_width),
            (value_proj, kv_index, kv_width),
        ]
    )
    inputs = block_order(hidden_in[0])
    cot_low = block_order(cotangent[0])
    attn_gain_rel = block_order(attn_gain)
    mlp_gain_rel = block_order(mlp_gain)
    input_even, input_odd = gather_ctx(inputs)
    fsdp_levels = (fsdp_count - 1).bit_length()

    def joined(blocks):
        return jnp.concatenate([blocks[number] for number in range(fsdp_count)], axis=0)

    attn_blocks = gather_fsdp_step({0: attn_shard}, fsdp_count, 1)
    output_shard = pick_columns([(output_proj, ctx_index, query_width)])
    mlp_shard = pick_columns(
        [(weights, ctx_index, hidden_width) for weights in (gate_proj, up_proj, down_proj)]
    )
    last = max(attn_blocks)
    output_shard, attn_blocks[last] = tie(output_shard, attn_blocks[last])
    for level in range(2, fsdp_levels + 1):
        attn_blocks = gather_fsdp_step(attn_blocks, fsdp_count, level)
    output_w = joined(
        {
            number: exchange(output_shard, number, "fsdp") if number else output_shard
            for number in range(fsdp_count)
        }
    )
    attn_w = joined(attn_blocks)
    mlp_shard, attn_w = tie(mlp_shard, attn_w)
    mlp_blocks = gather_fsdp_step({0: mlp_shard}, fsdp_count, 1)

    owner_ids = ctx_index ^ jnp.arange(ctx_count, dtype=jnp.int32)
    picked = owner_ids[:, None] == jnp.arange(ctx_count, dtype=jnp.int32)[None, :]
    block_ids = jnp.sum(jnp.where(picked[:, :, None], pair_table[None], 0), axis=1)
    positions = (
        block_ids[:, :, None] * block_len + jnp.arange(block_len, dtype=jnp.int32)
    ).reshape(total_rows)
    frequency = ROPE_BASE ** (-(jnp.arange(half_head, dtype=F32) * 2.0 / head_width))
    angles = positions.astype(F32)[:, None] * frequency[None, :]
    cosine = jnp.cos(angles)[:, None, :]
    sine_part = jnp.sin(angles)[:, None, :]

    def head_prep(raw_heads, gain_vec):
        return rotate(rms_norm(raw_heads, gain_vec), cosine, sine_part)

    cot_low, input_odd = tie(cot_low, input_odd)
    cot_blocks = gather_step({0: cot_low}, ctx_count, 1)
    input_wide = interleave(input_even, input_odd, ctx_count).astype(F32)
    attn_in = rms_norm(input_wide, attn_gain_rel).astype(BF16)
    attn_raw = times(attn_in, attn_w)
    for level in range(2, gather_levels(ctx_count) + 1):
        last = max(cot_blocks)
        attn_raw, cot_blocks[last] = tie(attn_raw, cot_blocks[last])
        cot_blocks = gather_step(cot_blocks, ctx_count, level)
    query_raw = attn_raw[:, :query_width].reshape(total_rows, query_count, head_width)
    key_raw = attn_raw[:, query_width : query_width + kv_width].reshape(
        total_rows, kv_count, head_width
    )
    value_heads = (
        attn_raw[:, query_width + kv_width :].astype(BF16).reshape(total_rows, kv_count, head_width)
    )
    query_heads = head_prep(query_raw, query_gain).astype(BF16)
    key_heads = head_prep(key_raw, key_gain).astype(BF16)
    grouped_query = query_heads.reshape(total_rows, kv_count, group_size, head_width)
    allowed = (positions[None, :] <= positions[:, None])[None, None]
    scores = (
        jnp.einsum("qhgd,khd->hgqk", grouped_query, key_heads, preferred_element_type=F32)
        * score_scale
    )
    scores = jnp.where(allowed, scores, MASKED)
    row_max = jnp.max(scores, axis=-1, keepdims=True)
    row_sum = jnp.sum(jnp.exp(scores - row_max), axis=-1, keepdims=True)
    log_total = row_max + jnp.log(row_sum)
    probs = jnp.exp(scores - log_total)
    probs_low = probs.astype(BF16)
    attn_mix = (
        jnp.einsum("hgqk,khd->qhgd", probs_low, value_heads, preferred_element_type=F32)
        .reshape(total_rows, query_width)
        .astype(BF16)
    )

    def split_shards(values):
        return {
            number: values[number * shard_rows : (number + 1) * shard_rows]
            for number in range(fsdp_count)
        }

    last = max(cot_blocks)
    attn_mix, cot_blocks[last] = tie(attn_mix, cot_blocks[last])
    mix_part = times_transposed(attn_mix, output_w).astype(BF16)
    resid_sum = scatter_ctx(*split_pairs(mix_part, ctx_count))
    cot_even, cot_odd = gather_last(cot_blocks, ctx_count)
    resid = inputs.astype(F32) + resid_sum
    mlp_in = rms_norm(resid, mlp_gain_rel).astype(BF16)
    last = max(mlp_blocks)
    mlp_in, mlp_blocks[last] = tie(mlp_in, mlp_blocks[last])
    for level in range(2, fsdp_levels + 1):
        mlp_blocks = gather_fsdp_step(mlp_blocks, fsdp_count, level)
    mlp_w = joined(mlp_blocks)
    down_w = mlp_w[:, 2 * hidden_width :]
    mlp_even, mlp_odd = gather_ctx(mlp_in)
    mlp_right, hidden_act, part_even, part_odd = mlp_both(
        mlp_even, mlp_odd, cot_even, cot_odd, mlp_w, ctx_count
    )
    mlp_in_grad = scatter_ctx(part_even, part_odd)
    cot_all = interleave(cot_even, cot_odd, ctx_count)
    mlp_sums = split_shards(
        jnp.concatenate(
            [
                transposed_times(interleave(mlp_even, mlp_odd, ctx_count), mlp_right),
                transposed_times(cot_all, hidden_act),
            ],
            axis=1,
        ).astype(BF16)
    )
    resid_part, mlp_gain_grad = jax.vjp(rms_norm, resid, mlp_gain_rel)[1](mlp_in_grad)
    resid_grad = cot_low.astype(F32) + resid_part
    resid_low = resid_grad.astype(BF16)
    for level in range(fsdp_levels, 1, -1):
        mlp_sums = scatter_fsdp_step(mlp_sums, fsdp_count, level)
    resid_even, resid_odd = gather_ctx(resid_low)
    if fsdp_levels > 1:
        resid_odd, mlp_sums[2] = tie(resid_odd, mlp_sums[2])
    mlp_moved = {
        number: exchange(mlp_sums[number].astype(BF16), number, "fsdp")
        for number in range(1, fsdp_count)
        if level_of(number) == 1
    }
    resid_all = interleave(resid_even, resid_odd, ctx_count)
    mix_grad = times(resid_all, output_w).astype(BF16)
    block_part = times_transposed(hidden_act, down_w)
    output_grads = transposed_times(resid_all, attn_mix).astype(BF16)

    dmix_heads = mix_grad.reshape(total_rows, kv_count, group_size, head_width)
    delta = jnp.einsum(
        "qhgd,qhgd->hgq",
        dmix_heads,
        attn_mix.reshape(total_rows, kv_count, group_size, head_width),
        preferred_element_type=F32,
    )
    value_grad = jnp.einsum("hgqk,qhgd->khd", probs_low, dmix_heads, preferred_element_type=F32)
    prob_grad = jnp.einsum("qhgd,khd->hgqk", dmix_heads, value_heads, preferred_element_type=F32)
    score_grad = (probs * (prob_grad - delta[..., None]) * score_scale).astype(BF16)
    query_grad = jnp.einsum("hgqk,khd->qhgd", score_grad, key_heads, preferred_element_type=F32)
    key_grad = jnp.einsum("hgqk,qhgd->khd", score_grad, grouped_query, preferred_element_type=F32)
    bit = 1
    while bit < kv_share:
        both = jnp.concatenate([key_grad, value_grad], axis=1)
        moved = exchange(both, bit, "ctx").reshape((ctx_count, row_count) + both.shape[1:])
        moved = jnp.concatenate([moved[number ^ bit] for number in range(ctx_count)], axis=0)
        key_grad = key_grad + moved[:, :kv_count]
        value_grad = value_grad + moved[:, kv_count:]
        bit *= 2
    query_raw_grad, query_gain_grad = jax.vjp(head_prep, query_raw, query_gain)[1](
        query_grad.reshape(total_rows, query_count, head_width)
    )
    key_raw_grad, key_gain_grad = jax.vjp(head_prep, key_raw, key_gain)[1](key_grad)
    query_low = query_raw_grad.reshape(total_rows, -1).astype(BF16)
    key_low = key_raw_grad.reshape(total_rows, -1).astype(BF16)
    value_low = value_grad.reshape(total_rows, -1).astype(BF16)
    attn_own_w = attn_w
    if kv_share > 1:
        own_start = (ctx_index % kv_share) * kv_own
        key_low = columns(key_low, own_start, kv_own)
        value_low = columns(value_low, own_start, kv_own)
        attn_own_w = jnp.concatenate(
            [
                attn_w[:, :query_width],
                columns(attn_w, query_width + own_start, kv_own),
                columns(attn_w, query_width + kv_width + own_start, kv_own),
            ],
            axis=1,
        )
        key_gain_grad = jnp.where(ctx_index % kv_share == 0, key_gain_grad, 0.0)
    attn_right = jnp.concatenate([query_low, key_low, value_low], axis=1)
    attn_sums = split_shards(
        jnp.concatenate(
            [transposed_times(attn_in, attn_right).astype(BF16), output_grads], axis=1
        )
    )
    for level in range(fsdp_levels, 0, -1):
        attn_sums = scatter_fsdp_step(attn_sums, fsdp_count, level)
    attn_grads = attn_sums[0].astype(BF16)
    attn_in_part = times_transposed(attn_right, attn_own_w)
    both_sums = scatter_ctx(
        *split_pairs(
            jnp.concatenate([attn_in_part.astype(BF16), block_part.astype(BF16)], axis=1),
            ctx_count,
        )
    )
    attn_in_grad = both_sums[:, :width]
    block_out = (resid + both_sums[:, width:]).astype(BF16)
    mlp_total = mlp_sums[0].astype(F32)
    for moved in mlp_moved.values():
        mlp_total = mlp_total + moved.astype(F32)
    mlp_grads = mlp_total.astype(BF16)
    own_wide = inputs.astype(F32)
    input_part = jax.vjp(lambda values: rms_norm(values, attn_gain_rel), own_wide)[1](
        attn_in_grad
    )[0]
    input_grad = resid_grad + input_part
    attn_gain_grad = jnp.sum(
        attn_in_part
        * (
            input_wide
            * lax.rsqrt(jnp.mean(input_wide * input_wide, axis=-1, keepdims=True) + NORM_EPS)
        ),
        axis=0,
    )
    gains = sum_all(
        jnp.concatenate(
            [
                block_order(attn_gain_grad),
                block_order(mlp_gain_grad),
                query_gain_grad,
                key_gain_grad,
            ]
        )
    )

    def placed(own, widths):
        even, odd = gather_ctx(own)
        blocks = []
        for number in range(ctx_count):
            start = number // 2 * shard_rows
            blocks.append((odd if number % 2 else even)[start : start + shard_rows])
        return place_columns(
            blocks, widths, [ctx_index ^ number for number in range(ctx_count)]
        )

    mlp_outs = placed(mlp_grads, (hidden_width,) * 3)
    attn_outs = placed(attn_grads, (query_width, kv_own, kv_own, query_width))
    return (
        block_order(block_out)[None],
        block_order(input_grad)[None],
        gains[:width],
        attn_outs[0],
        attn_outs[1],
        attn_outs[2],
        gains[2 * width : 2 * width + head_width],
        gains[2 * width + head_width :],
        attn_outs[3],
        gains[width : 2 * width],
        mlp_outs[0],
        mlp_outs[1],
        mlp_outs[2],
    )


def solution(mesh):
    in_specs = (
        P("fsdp", "ctx", None),
        P(),
        P(),
        P("fsdp", None),
        P("fsdp", None),
        P("fsdp", None),
        P(),
        P(),
        P("fsdp", None),
        P(),
        P("fsdp", None),
        P("fsdp", None),
        P("fsdp", None),
        P("fsdp", "ctx", None),
    )
    out_specs = (
        P("fsdp", "ctx", None),
        P("fsdp", "ctx", None),
        P(),
        P("fsdp", None),
        P("fsdp", None),
        P("fsdp", None),
        P(),
        P(),
        P("fsdp", None),
        P(),
        P("fsdp", None),
        P("fsdp", None),
        P("fsdp", None),
    )
    return jax.shard_map(
        on_device, mesh=mesh, in_specs=in_specs, out_specs=out_specs, check_vma=False
    )
```

```python
import math

import jax
import jax.numpy as jnp
from jax import lax
from jax.experimental import pallas as pl
from jax.experimental.pallas import tpu as pltpu
from jax.sharding import PartitionSpec as P


NORM_EPS = 1e-06
ROPE_BASE = 1000000.0
MASKED = -1e30
F32 = jnp.float32
BF16 = jnp.bfloat16


def rms_norm(values, gain_vec):
    return (
        values * lax.rsqrt(jnp.mean(values * values, axis=-1, keepdims=True) + NORM_EPS) * gain_vec
    )


def times_transposed(lhs_mat, rhs_mat):
    return lax.dot_general(
        lhs_mat, rhs_mat, (((1,), (1,)), ((), ())), preferred_element_type=F32
    )


def transposed_times(lhs_mat, rhs_mat):
    return lax.dot_general(
        lhs_mat, rhs_mat, (((0,), (0,)), ((), ())), preferred_element_type=F32
    )


def exchange(value, bit, axis):
    count = lax.axis_size(axis)
    return lax.ppermute(value, axis, [(index, index ^ bit) for index in range(count)])


def low_bit(number):
    return number & -number


def top_bit(number):
    return 1 << (number.bit_length() - 1)


def level_of(number):
    return bin(number).count("1")


def even_numbers(count, level):
    return [number for number in range(0, count, 2) if level_of(number) == level]


def gather_levels(count):
    return (count // 2).bit_length() - 1


def gather_step(blocks, count, level):
    half = blocks[0].shape[0] // 2
    blocks = dict(blocks)
    for number in even_numbers(count, level):
        low, top = low_bit(number), top_bit(number)
        if low == top:
            blocks[number] = exchange(blocks[0], low, "ctx")
        else:
            blocks[number] = jnp.concatenate(
                [
                    exchange(blocks[number ^ top][:half], top, "ctx"),
                    exchange(blocks[number ^ low][half:], low, "ctx"),
                ],
                axis=0,
            )
    return blocks


def gather_last(blocks, count):
    even = jnp.concatenate([blocks[number] for number in range(0, count, 2)], axis=0)
    return even, exchange(even, 1, "ctx")


def gather_ctx(own):
    count = lax.axis_size("ctx")
    blocks = {0: own}
    for level in range(1, gather_levels(count) + 1):
        blocks = gather_step(blocks, count, level)
    return gather_last(blocks, count)


def interleave(even, odd, count):
    rows = even.shape[0] * 2 // count
    both = jnp.stack(
        [even.reshape(count // 2, rows, -1), odd.reshape(count // 2, rows, -1)], axis=1
    )
    return both.reshape(count * rows, -1)


def scatter_ctx(even, odd):
    count = lax.axis_size("ctx")
    rows = even.shape[0] * 2 // count
    half = rows // 2
    moved = exchange(odd, 1, "ctx")

    def piece(number, start, stop):
        base = number // 2 * rows
        return even[base + start : base + stop].astype(F32) + moved[
            base + start : base + stop
        ].astype(F32)

    halves = {
        number: [piece(number, 0, half), piece(number, half, rows)]
        for number in range(0, count, 2)
    }
    for level in range(gather_levels(count), 1, -1):
        for number in even_numbers(count, level):
            low, top = low_bit(number), top_bit(number)
            first, second = (part.astype(BF16) for part in halves[number])
            halves[number ^ top][0] += exchange(first, top, "ctx").astype(F32)
            halves[number ^ low][1] += exchange(second, low, "ctx").astype(F32)
    total = jnp.concatenate(halves[0], axis=0)
    for number in even_numbers(count, 1):
        sent = jnp.concatenate(halves[number], axis=0).astype(BF16)
        total = total + exchange(sent, number, "ctx").astype(F32)
    return total


def gather_fsdp_step(blocks, count, level):
    blocks = dict(blocks)
    for number in range(1, count):
        if level_of(number) == level:
            low = low_bit(number)
            blocks[number] = exchange(blocks[number ^ low], low, "fsdp")
    return blocks


def scatter_fsdp_step(sums, count, level):
    sums = dict(sums)
    for number in range(1, count):
        if level_of(number) == level:
            low = low_bit(number)
            sums[number ^ low] = sums[number ^ low].astype(F32) + exchange(
                sums[number].astype(BF16), low, "fsdp"
            ).astype(F32)
    return sums


def sum_all(value):
    for axis in ("ctx", "fsdp"):
        bit = 1
        while bit < lax.axis_size(axis):
            value = value + exchange(value, bit, axis)
            bit *= 2
    return value


def whole(array):
    return pl.BlockSpec(array.shape, lambda *ids: (0,) * len(array.shape))


def pick_columns(picks):
    rows = picks[0][0].shape[0]
    widths = [width for _, _, width in picks]
    if any(width % 128 for width in widths):
        return jnp.concatenate(
            [
                lax.dynamic_slice_in_dim(array, index * width, width, axis=1)
                for array, index, width in picks
            ],
            axis=1,
        )

    def kernel(index_ref, *refs):
        start = 0
        for ref, width in zip(refs, widths):
            refs[-1][:, start : start + width] = ref[...]
            start += width

    def spec(number, width):
        return pl.BlockSpec((rows, width), lambda step, index_ref: (0, index_ref[number]))

    total = sum(widths)
    return pl.pallas_call(
        kernel,
        out_shape=jax.ShapeDtypeStruct((rows, total), picks[0][0].dtype),
        grid_spec=pltpu.PrefetchScalarGridSpec(
            num_scalar_prefetch=1,
            grid=(1,),
            in_specs=[spec(number, width) for number, width in enumerate(widths)],
            out_specs=pl.BlockSpec((rows, total), lambda step, index_ref: (0, 0)),
        ),
        cost_estimate=pl.CostEstimate(
            flops=0, bytes_accessed=4 * rows * total, transcendentals=0
        ),
        name="pick_columns",
    )(jnp.stack([index for _, index, _ in picks]).astype(jnp.int32), *[p[0] for p in picks])


def place_columns(even, odd, widths, ctx_index):
    count = lax.axis_size("ctx")
    rows = even.shape[0] * 2 // count
    starts = [sum(widths[:number]) for number in range(len(widths))]
    if any(width % 128 for width in widths):
        placed = []
        for start, width in zip(starts, widths):
            result = jnp.zeros((rows, count * width), F32)
            for number in range(count):
                base = number // 2 * rows
                result = lax.dynamic_update_slice_in_dim(
                    result,
                    (odd if number % 2 else even)[
                        base : base + rows, start : start + width
                    ].astype(F32),
                    (ctx_index ^ number) * width,
                    axis=1,
                )
            placed.append(result)
        return placed

    def kernel(index_ref, even_ref, odd_ref, *out_refs):
        for parity in range(2):

            @pl.when(index_ref[0] == parity)
            def _():
                sides = (odd_ref, even_ref) if parity else (even_ref, odd_ref)
                for out_ref, start, width in zip(out_refs, starts, widths):
                    for side, ref in enumerate(sides):
                        out_ref[:, side * width : (side + 1) * width] = ref[
                            :, start : start + width
                        ].astype(F32)

    block = pl.BlockSpec((rows, sum(widths)), lambda step, index_ref: (step, 0))
    index = [ctx_index % 2] + [(ctx_index ^ number) // 2 for number in range(0, count, 2)]
    return pl.pallas_call(
        kernel,
        out_shape=[jax.ShapeDtypeStruct((rows, count * width), F32) for width in widths],
        grid_spec=pltpu.PrefetchScalarGridSpec(
            num_scalar_prefetch=1,
            grid=(count // 2,),
            in_specs=[block, block],
            out_specs=[
                pl.BlockSpec((rows, 2 * width), lambda step, index_ref: (0, index_ref[step + 1]))
                for width in widths
            ],
        ),
        cost_estimate=pl.CostEstimate(
            flops=0, bytes_accessed=6 * count * rows * sum(widths), transcendentals=0
        ),
        name="place_columns",
    )(jnp.stack(index).astype(jnp.int32), even, odd)


def own_kernel(index_ref, hidden_ref, cot_ref, gains_ref, both_ref, order_ref):
    width = hidden_ref.shape[1]
    count = index_ref.shape[0]
    size = width // count
    for number in range(count):
        source = pl.ds(pl.multiple_of(index_ref[number] * size, size), size)
        target = slice(number * size, (number + 1) * size)
        both_ref[:, target] = hidden_ref[:, source]
        both_ref[:, width + target.start : width + target.stop] = cot_ref[:, source]
        order_ref[:, target] = gains_ref[:, source]


def own_blocks(hidden, cot, gains, indices):
    rows, width = hidden.shape
    return pl.pallas_call(
        own_kernel,
        out_shape=[
            jax.ShapeDtypeStruct((rows, 2 * width), BF16),
            jax.ShapeDtypeStruct(gains.shape, F32),
        ],
        in_specs=[pl.BlockSpec(memory_space=pltpu.SMEM)]
        + [pl.BlockSpec(memory_space=pltpu.VMEM)] * 3,
        out_specs=[pl.BlockSpec(memory_space=pltpu.VMEM)] * 2,
        cost_estimate=pl.CostEstimate(
            flops=0, bytes_accessed=8 * rows * width, transcendentals=0
        ),
        name="own_blocks",
    )(indices, hidden, cot, gains)


def mlp_kernel(x_even, x_odd, c_even, c_odd, w_ref, right_ref, act_ref, even_ref, odd_ref):
    hidden = act_ref.shape[1]
    rows = x_even.shape[0]
    for x_ref, c_ref, part_ref, start in (
        (x_even, c_even, even_ref, 0),
        (x_odd, c_odd, odd_ref, rows),
    ):
        both = jnp.dot(x_ref[...], w_ref[:, : 2 * hidden], preferred_element_type=F32)
        grad = jnp.dot(c_ref[...], w_ref[:, 2 * hidden :], preferred_element_type=F32)
        gate = both[:, :hidden]
        upper = both[:, hidden:]
        sigma = jax.nn.sigmoid(gate)
        gate_sigma = gate * sigma
        act_ref[start : start + rows, :] = (gate_sigma * upper).astype(BF16)
        right = jnp.concatenate(
            [
                (grad * upper * sigma * (1.0 + gate * (1.0 - sigma))).astype(BF16),
                (grad * gate_sigma).astype(BF16),
            ],
            axis=1,
        )
        right_ref[start : start + rows, :] = right
        part_ref[...] = lax.dot_general(
            right,
            w_ref[:, : 2 * hidden],
            (((1,), (1,)), ((), ())),
            preferred_element_type=F32,
        ).astype(BF16)


def mlp_both(x_even, x_odd, c_even, c_odd, weights, count):
    rows = x_even.shape[0] * 2 // count
    width = x_even.shape[1]
    hidden = weights.shape[1] // 3
    total = count * rows
    block = pl.BlockSpec((rows, width), lambda step: (step, 0))
    side = pl.BlockSpec((rows, width), lambda step: (step, 1))
    return pl.pallas_call(
        mlp_kernel,
        out_shape=[
            jax.ShapeDtypeStruct((total, 2 * hidden), BF16),
            jax.ShapeDtypeStruct((total, hidden), BF16),
            jax.ShapeDtypeStruct(x_even.shape, BF16),
            jax.ShapeDtypeStruct(x_even.shape, BF16),
        ],
        grid=(count // 2,),
        in_specs=[block, block, side, side, whole(weights)],
        out_specs=[
            pl.BlockSpec((2 * rows, 2 * hidden), lambda step: (step, 0)),
            pl.BlockSpec((2 * rows, hidden), lambda step: (step, 0)),
            block,
            block,
        ],
        cost_estimate=pl.CostEstimate(
            flops=10 * total * width * hidden,
            bytes_accessed=8 * total * width,
            transcendentals=total * hidden,
        ),
        name="mlp_both",
    )(x_even, x_odd, c_even, c_odd, weights)


def rotated(values, cosine, sine_part):
    return values * cosine + pltpu.roll(values, values.shape[1] // 2, 1) * sine_part


def head_scale(raw):
    return lax.rsqrt(jnp.mean(raw * raw, axis=-1, keepdims=True) + NORM_EPS)


def head_back(grad, raw, gain_row, cosine, sine_part):
    turned = grad * cosine + pltpu.roll(grad * sine_part, grad.shape[1] // 2, 1)
    scale = head_scale(raw)
    scaled = turned * gain_row
    mean_part = jnp.mean(scaled * raw, axis=-1, keepdims=True)
    return scale * scaled - raw * (scale * scale * scale * mean_part), turned * raw * scale


def project_kernel(
    x_even, x_odd, gain_ref, w_ref, qgain_ref, kgain_ref, cos_ref, sin_ref,
    in_ref, raw_ref, q_ref, k_ref, v_ref,
):
    head = qgain_ref.shape[1]
    q_width = q_ref.shape[1]
    kv_width = k_ref.shape[1]
    rows = x_even.shape[0]
    for x_ref, start in ((x_even, 0), (x_odd, rows)):
        x = x_ref[...].astype(F32)
        normed = rms_norm(x, gain_ref[...]).astype(BF16)
        in_ref[start : start + rows, :] = normed
        raw = jnp.dot(normed, w_ref[:, : q_width + 2 * kv_width], preferred_element_type=F32)
        raw_ref[start : start + rows, :] = raw[:, : q_width + kv_width]
        cosine = cos_ref[start : start + rows, :]
        sine_part = sin_ref[start : start + rows, :]
        for column in range(0, q_width, head):
            part = raw[:, column : column + head]
            q_ref[start : start + rows, column : column + head] = rotated(
                part * head_scale(part) * qgain_ref[...], cosine, sine_part
            ).astype(BF16)
        for column in range(0, kv_width, head):
            part = raw[:, q_width + column : q_width + column + head]
            k_ref[start : start + rows, column : column + head] = rotated(
                part * head_scale(part) * kgain_ref[...], cosine, sine_part
            ).astype(BF16)
        v_ref[start : start + rows, :] = raw[:, q_width + kv_width :].astype(BF16)


def project(x_even, x_odd, gain, weights, q_gain, k_gain, cosine, sine_part, q_width, kv_width):
    width = gain.shape[1]
    head = q_gain.shape[1]
    total = cosine.shape[0]
    rows = total // (2 * lax.axis_size("ctx") // 2)
    block = pl.BlockSpec((rows, width), lambda step: (step, 0))

    def wide(columns):
        return pl.BlockSpec((2 * rows, columns), lambda step: (step, 0))

    return pl.pallas_call(
        project_kernel,
        out_shape=[
            jax.ShapeDtypeStruct((total, width), BF16),
            jax.ShapeDtypeStruct((total, q_width + kv_width), F32),
            jax.ShapeDtypeStruct((total, q_width), BF16),
            jax.ShapeDtypeStruct((total, kv_width), BF16),
            jax.ShapeDtypeStruct((total, kv_width), BF16),
        ],
        grid=(total // (2 * rows),),
        in_specs=[
            block, block, whole(gain), whole(weights), whole(q_gain), whole(k_gain),
            wide(head), wide(head),
        ],
        out_specs=[
            wide(width), wide(q_width + kv_width), wide(q_width), wide(kv_width), wide(kv_width),
        ],
        cost_estimate=pl.CostEstimate(
            flops=2 * total * width * (q_width + 2 * kv_width),
            bytes_accessed=8 * total * width,
            transcendentals=total,
        ),
        name="project",
    )(x_even, x_odd, gain, weights, q_gain, k_gain, cosine, sine_part)


def nt(lhs, rhs):
    return lax.dot_general(lhs, rhs, (((1,), (1,)), ((), ())), preferred_element_type=F32)


def attend_kernel(
    q_ref, k_ref, v_ref, row_ref, col_ref, w_ref, mix_ref, lse_ref, even_ref, odd_ref, vt_ref
):
    kv_width = k_ref.shape[1]
    q_width = q_ref.shape[1]
    head = q_width // lse_ref.shape[0]
    group = q_width // kv_width
    scale = 1.0 / math.sqrt(head)

    @pl.when(pl.program_id(0) == 0)
    def _():
        vt_ref[...] = v_ref[...].astype(F32).T.astype(BF16)

    allowed = col_ref[...] <= row_ref[...]
    for number in range(q_width // head):
        kv = number // group * head
        column = number * head
        scores = jnp.where(
            allowed, nt(k_ref[:, kv : kv + head], q_ref[:, column : column + head]) * scale, MASKED
        )
        top = jnp.max(scores, axis=0, keepdims=True)
        raised = jnp.exp(scores - top)
        total = jnp.sum(raised, axis=0, keepdims=True)
        lse_ref[number : number + 1, :] = top + jnp.log(total)
        probs = (raised * (1.0 / total)).astype(BF16)
        mixed = jnp.dot(vt_ref[kv : kv + head, :], probs, preferred_element_type=F32)
        mix_ref[:, column : column + head] = mixed.T.astype(BF16)
    rows = even_ref.shape[0]
    out = nt(mix_ref[...], w_ref[...]).astype(BF16)
    even_ref[...] = out[:rows]
    odd_ref[...] = out[rows:]


def attend(q, k, v, pos_row, pos_col, out_w, head):
    total, q_width = q.shape
    kv_width = k.shape[1]
    width = out_w.shape[0]
    steps = lax.axis_size("ctx") // 2
    rows = total // (2 * steps)
    heads = q_width // head

    def wide(columns):
        return pl.BlockSpec((2 * rows, columns), lambda step: (step, 0))

    half = pl.BlockSpec((rows, width), lambda step: (step, 0))
    return pl.pallas_call(
        attend_kernel,
        out_shape=[
            jax.ShapeDtypeStruct((total, q_width), BF16),
            jax.ShapeDtypeStruct((heads, total), F32),
            jax.ShapeDtypeStruct((total // 2, width), BF16),
            jax.ShapeDtypeStruct((total // 2, width), BF16),
        ],
        grid=(steps,),
        in_specs=[
            wide(q_width), whole(k), whole(v),
            pl.BlockSpec((1, 2 * rows), lambda step: (0, step)),
            whole(pos_col), whole(out_w),
        ],
        out_specs=[
            wide(q_width), pl.BlockSpec((heads, 2 * rows), lambda step: (0, step)), half, half,
        ],
        scratch_shapes=[pltpu.VMEM((kv_width, total), BF16)],
        cost_estimate=pl.CostEstimate(
            flops=4 * total * total * q_width,
            bytes_accessed=8 * total * width,
            transcendentals=total * total * heads,
        ),
        name="attend",
    )(q, k, v, pos_row, pos_col, out_w)


def attend_back_kernel(
    q_ref, k_ref, v_ref, row_ref, col_ref, w_ref, mix_ref, lse_ref, g_even, g_odd,
    raw_ref, qgain_ref, cos_ref, sin_ref,
    low_ref, dk_ref, dv_ref, dgain_ref, kt_ref, dmix_ref,
):
    head = qgain_ref.shape[1]
    kv_width = k_ref.shape[1]
    q_width = q_ref.shape[1]
    group = q_width // kv_width
    scale = 1.0 / math.sqrt(head)
    rows = g_even.shape[0]

    @pl.when(pl.program_id(0) == 0)
    def _():
        kt_ref[...] = k_ref[...].astype(F32).T.astype(BF16)
        dk_ref[...] = jnp.zeros_like(dk_ref)
        dv_ref[...] = jnp.zeros_like(dv_ref)
        dgain_ref[...] = jnp.zeros_like(dgain_ref)

    dmix_ref[:rows, :] = jnp.dot(g_even[...], w_ref[...], preferred_element_type=F32).astype(BF16)
    dmix_ref[rows:, :] = jnp.dot(g_odd[...], w_ref[...], preferred_element_type=F32).astype(BF16)
    allowed = col_ref[...] <= row_ref[...]
    for number in range(q_width // head):
        kv = number // group * head
        column = number * head
        q = q_ref[:, column : column + head]
        dmix = dmix_ref[:, column : column + head]
        mix = mix_ref[:, column : column + head]
        delta = jnp.sum((dmix.astype(F32) * mix.astype(F32)).T, axis=0, keepdims=True)
        scores = nt(k_ref[:, kv : kv + head], q) * scale
        probs = jnp.exp(jnp.where(allowed, scores - lse_ref[number : number + 1, :], MASKED))
        dv_ref[:, kv : kv + head] += jnp.dot(
            probs.astype(BF16), dmix, preferred_element_type=F32
        )
        prob_grad = nt(v_ref[:, kv : kv + head], dmix)
        score_grad = (probs * (prob_grad - delta) * scale).astype(BF16)
        dk_ref[:, kv : kv + head] += jnp.dot(score_grad, q, preferred_element_type=F32)
        dq = jnp.dot(kt_ref[kv : kv + head, :], score_grad, preferred_element_type=F32).T
        raw_grad, gain_part = head_back(
            dq, raw_ref[:, column : column + head], qgain_ref[...], cos_ref[...], sin_ref[...]
        )
        low_ref[:, column : column + head] = raw_grad.astype(BF16)
        dgain_ref[...] += jnp.sum(gain_part, axis=0, keepdims=True)


def attend_back(q, k, v, pos_row, pos_col, out_w, mix, lse, g_even, g_odd, raw, q_gain, cosine, sine_part):
    total, q_width = q.shape
    kv_width = k.shape[1]
    width = out_w.shape[0]
    steps = lax.axis_size("ctx") // 2
    rows = total // (2 * steps)
    heads = lse.shape[0]
    head = q_gain.shape[1]

    def wide(columns):
        return pl.BlockSpec((2 * rows, columns), lambda step: (step, 0))

    def fixed(shape):
        return pl.BlockSpec(shape, lambda step: (0, 0))

    half = pl.BlockSpec((rows, width), lambda step: (step, 0))
    return pl.pallas_call(
        attend_back_kernel,
        out_shape=[
            jax.ShapeDtypeStruct((total, q_width), BF16),
            jax.ShapeDtypeStruct((total, kv_width), F32),
            jax.ShapeDtypeStruct((total, kv_width), F32),
            jax.ShapeDtypeStruct((1, head), F32),
        ],
        grid=(steps,),
        in_specs=[
            wide(q_width), whole(k), whole(v),
            pl.BlockSpec((1, 2 * rows), lambda step: (0, step)),
            whole(pos_col), whole(out_w), wide(q_width),
            pl.BlockSpec((heads, 2 * rows), lambda step: (0, step)),
            half, half, wide(q_width), whole(q_gain), wide(head), wide(head),
        ],
        out_specs=[
            wide(q_width), fixed((total, kv_width)), fixed((total, kv_width)), fixed((1, head)),
        ],
        scratch_shapes=[
            pltpu.VMEM((kv_width, total), BF16),
            pltpu.VMEM((2 * rows, q_width), BF16),
        ],
        cost_estimate=pl.CostEstimate(
            flops=10 * total * total * q_width,
            bytes_accessed=8 * total * width,
            transcendentals=total * total * heads,
        ),
        name="attend_back",
    )(q, k, v, pos_row, pos_col, out_w, mix, lse, g_even, g_odd, raw, q_gain, cosine, sine_part)


def project_back_kernel(
    low_ref, dk_ref, dv_ref, raw_ref, kgain_ref, cos_ref, sin_ref, x_even, x_odd, w_ref, blk_ref,
    right_ref, even_ref, odd_ref, again_ref, dgain_ref,
):
    head = kgain_ref.shape[1]
    kv_width = dk_ref.shape[1]
    q_width = low_ref.shape[1]
    rows, width = x_even.shape

    @pl.when(pl.program_id(0) == 0)
    def _():
        again_ref[...] = jnp.zeros_like(again_ref)
        dgain_ref[...] = jnp.zeros_like(dgain_ref)

    right_ref[:, :q_width] = low_ref[...]
    for column in range(0, kv_width, head):
        raw_grad, gain_part = head_back(
            dk_ref[:, column : column + head],
            raw_ref[:, q_width + column : q_width + column + head],
            kgain_ref[...],
            cos_ref[...],
            sin_ref[...],
        )
        right_ref[:, q_width + column : q_width + column + head] = raw_grad.astype(BF16)
        dgain_ref[...] += jnp.sum(gain_part, axis=0, keepdims=True)
    right_ref[:, q_width + kv_width :] = dv_ref[...].astype(BF16)
    for x_ref, part_ref, start in ((x_even, even_ref, 0), (x_odd, odd_ref, rows)):
        part = nt(right_ref[start : start + rows, :], w_ref[...])
        x = x_ref[...].astype(F32)
        again_ref[...] += jnp.sum(part * (x * head_scale(x)), axis=0, keepdims=True)
        part_ref[:, :width] = part.astype(BF16)
        part_ref[:, width:] = blk_ref[start : start + rows, :]


def project_back(low, dk, dv, raw, k_gain, cosine, sine_part, x_even, x_odd, weights, block_part):
    total, q_width = low.shape
    kv_width = dk.shape[1]
    width = weights.shape[0]
    steps = lax.axis_size("ctx") // 2
    rows = total // (2 * steps)
    head = k_gain.shape[1]

    def wide(columns):
        return pl.BlockSpec((2 * rows, columns), lambda step: (step, 0))

    def fixed(shape):
        return pl.BlockSpec(shape, lambda step: (0, 0))

    half = pl.BlockSpec((rows, width), lambda step: (step, 0))
    both = pl.BlockSpec((rows, 2 * width), lambda step: (step, 0))
    return pl.pallas_call(
        project_back_kernel,
        out_shape=[
            jax.ShapeDtypeStruct((total, q_width + 2 * kv_width), BF16),
            jax.ShapeDtypeStruct((total // 2, 2 * width), BF16),
            jax.ShapeDtypeStruct((total // 2, 2 * width), BF16),
            jax.ShapeDtypeStruct((1, width), F32),
            jax.ShapeDtypeStruct((1, head), F32),
        ],
        grid=(steps,),
        in_specs=[
            wide(q_width), wide(kv_width), wide(kv_width), wide(q_width + kv_width),
            whole(k_gain), wide(head), wide(head), half, half, whole(weights), wide(width),
        ],
        out_specs=[
            wide(q_width + 2 * kv_width), both, both, fixed((1, width)), fixed((1, head)),
        ],
        cost_estimate=pl.CostEstimate(
            flops=2 * total * width * (q_width + 2 * kv_width),
            bytes_accessed=12 * total * width,
            transcendentals=total,
        ),
        name="project_back",
    )(low, dk, dv, raw, k_gain, cosine, sine_part, x_even, x_odd, weights, block_part)


def on_device_all(
    hidden_in,
    pair_table,
    attn_gain,
    query_proj,
    key_proj,
    value_proj,
    query_gain,
    key_gain,
    output_proj,
    mlp_gain,
    gate_proj,
    up_proj,
    down_proj,
    cotangent,
):
    fsdp_count = lax.axis_size("fsdp")
    fsdp_index = lax.axis_index("fsdp")
    ctx_count = lax.axis_size("ctx")
    ctx_index = lax.axis_index("ctx")
    row_count, width = hidden_in.shape[1:]
    block_len = row_count // 2
    total_rows = ctx_count * row_count
    shard_rows = width // fsdp_count
    head_width = query_gain.shape[0]
    half_head = head_width // 2
    kvhead_total = key_proj.shape[1] // head_width
    kv_count = max(1, kvhead_total // ctx_count)
    kv_share = max(1, ctx_count // kvhead_total)
    query_width = query_proj.shape[1] // ctx_count
    kv_width = kv_count * head_width
    kv_own = key_proj.shape[1] // ctx_count
    hidden_width = gate_proj.shape[1] // ctx_count

    fsdp_order = fsdp_index ^ jnp.arange(fsdp_count, dtype=jnp.int32)

    def block_order(values):
        return jnp.concatenate(
            [
                lax.dynamic_slice_in_dim(
                    values, (fsdp_index ^ number) * shard_rows, shard_rows, axis=values.ndim - 1
                )
                for number in range(fsdp_count)
            ],
            axis=-1,
        )

    def columns(weights, start, size):
        return lax.dynamic_slice_in_dim(weights, start, size, axis=1)

    kv_index = ctx_index // kv_share
    both_own, gains_rel = own_blocks(
        hidden_in[0], cotangent[0], jnp.stack([attn_gain, mlp_gain]), fsdp_order
    )
    inputs = both_own[:, :width]
    cot_low = both_own[:, width:]
    attn_gain_rel = gains_rel[0]
    mlp_gain_rel = gains_rel[1]
    fsdp_levels = (fsdp_count - 1).bit_length()
    attn_width = query_width + 2 * kv_width

    def joined(blocks):
        return jnp.concatenate([blocks[number] for number in range(fsdp_count)], axis=0)

    both_even, both_odd = gather_ctx(both_own)
    first_shard = pick_columns(
        [
            (query_proj, ctx_index, query_width),
            (key_proj, kv_index, kv_width),
            (value_proj, kv_index, kv_width),
            (output_proj, ctx_index, query_width),
        ]
    )
    first_blocks = {0: first_shard}
    for level in range(1, fsdp_levels + 1):
        first_blocks = gather_fsdp_step(first_blocks, fsdp_count, level)
    first_w = joined(first_blocks)
    attn_w = first_w[:, :attn_width]
    output_w = first_w[:, attn_width:]
    mlp_shard = pick_columns(
        [(weights, ctx_index, hidden_width) for weights in (gate_proj, up_proj, down_proj)]
    )
    mlp_blocks = gather_fsdp_step({0: mlp_shard}, fsdp_count, 1)

    owner_ids = ctx_index ^ jnp.arange(ctx_count, dtype=jnp.int32)
    picked = owner_ids[:, None] == jnp.arange(ctx_count, dtype=jnp.int32)[None, :]
    block_ids = jnp.sum(jnp.where(picked[:, :, None], pair_table[None], 0), axis=1)
    positions = (
        block_ids[:, :, None] * block_len + jnp.arange(block_len, dtype=jnp.int32)
    ).reshape(total_rows)
    pos_row = positions.reshape(1, total_rows)
    pos_col = positions.reshape(total_rows, 1)
    lanes = jnp.arange(head_width, dtype=jnp.int32)
    frequency = ROPE_BASE ** (-((lanes % half_head).astype(F32) * 2.0 / head_width))
    angles = positions.astype(F32)[:, None] * frequency[None, :]
    cosine = jnp.cos(angles)
    sine_part = jnp.sin(angles) * jnp.where(lanes < half_head, -1.0, 1.0)[None, :]

    query_row = query_gain.reshape(1, head_width)
    key_row = key_gain.reshape(1, head_width)
    attn_in, attn_raw, query_heads, key_heads, value_heads = project(
        both_even, both_odd, attn_gain_rel.reshape(1, width), first_w, query_row, key_row,
        cosine, sine_part, query_width, kv_width,
    )
    attn_mix, log_total, mix_even, mix_odd = attend(
        query_heads, key_heads, value_heads, pos_row, pos_col, output_w, head_width
    )

    def split_shards(values):
        return {
            number: values[number * shard_rows : (number + 1) * shard_rows]
            for number in range(fsdp_count)
        }

    resid_sum = scatter_ctx(mix_even, mix_odd)
    cot_even = both_even[:, width:]
    cot_odd = both_odd[:, width:]
    resid = inputs.astype(F32) + resid_sum
    mlp_in = rms_norm(resid, mlp_gain_rel).astype(BF16)
    for level in range(2, fsdp_levels + 1):
        mlp_blocks = gather_fsdp_step(mlp_blocks, fsdp_count, level)
    mlp_w = joined(mlp_blocks)
    down_w = mlp_w[:, 2 * hidden_width :]
    mlp_even, mlp_odd = gather_ctx(mlp_in)
    mlp_right, hidden_act, part_even, part_odd = mlp_both(
        mlp_even, mlp_odd, both_even, both_odd, mlp_w, ctx_count
    )
    mlp_in_grad = scatter_ctx(part_even, part_odd)
    cot_all = interleave(cot_even, cot_odd, ctx_count)
    mlp_sums = split_shards(
        jnp.concatenate(
            [
                transposed_times(interleave(mlp_even, mlp_odd, ctx_count), mlp_right),
                transposed_times(cot_all, hidden_act),
            ],
            axis=1,
        ).astype(BF16)
    )
    resid_part, mlp_gain_grad = jax.vjp(rms_norm, resid, mlp_gain_rel)[1](mlp_in_grad)
    resid_grad = cot_low.astype(F32) + resid_part
    resid_low = resid_grad.astype(BF16)
    for level in range(fsdp_levels, 1, -1):
        mlp_sums = scatter_fsdp_step(mlp_sums, fsdp_count, level)
    resid_even, resid_odd = gather_ctx(resid_low)
    mlp_moved = {
        number: exchange(mlp_sums[number].astype(BF16), number, "fsdp")
        for number in range(1, fsdp_count)
        if level_of(number) == 1
    }
    resid_all = interleave(resid_even, resid_odd, ctx_count)
    block_part = times_transposed(hidden_act, down_w).astype(BF16)
    output_grads = transposed_times(resid_all, attn_mix).astype(BF16)

    query_low, key_grad, value_grad, query_gain_grad = attend_back(
        query_heads, key_heads, value_heads, pos_row, pos_col, output_w, attn_mix, log_total,
        resid_even, resid_odd, attn_raw, query_row, cosine, sine_part,
    )
    bit = 1
    while bit < kv_share:
        moved = exchange(jnp.concatenate([key_grad, value_grad], axis=1), bit, "ctx")
        moved = moved.reshape(ctx_count, row_count, 2 * kv_width)
        moved = jnp.concatenate([moved[number ^ bit] for number in range(ctx_count)], axis=0)
        key_grad = key_grad + moved[:, :kv_width]
        value_grad = value_grad + moved[:, kv_width:]
        bit *= 2
    attn_own_w = attn_w
    own_start = (ctx_index % kv_share) * kv_own
    if kv_share > 1:
        place = jnp.arange(attn_width) - query_width
        owned = (place < 0) | (
            (place % kv_width >= own_start) & (place % kv_width < own_start + kv_own)
        )
        attn_own_w = jnp.where(owned[None, :], attn_w, 0).astype(BF16)
    attn_right, tail_even, tail_odd, attn_gain_grad, key_gain_grad = project_back(
        query_low, key_grad, value_grad, attn_raw, key_row, cosine, sine_part,
        both_even, both_odd, attn_own_w, block_part,
    )
    attn_gain_grad = attn_gain_grad[0]
    query_gain_grad = query_gain_grad[0]
    key_gain_grad = key_gain_grad[0]
    if kv_share > 1:
        attn_right = jnp.concatenate(
            [
                attn_right[:, :query_width],
                columns(attn_right, query_width + own_start, kv_own),
                columns(attn_right, query_width + kv_width + own_start, kv_own),
            ],
            axis=1,
        )
        key_gain_grad = jnp.where(ctx_index % kv_share == 0, key_gain_grad, 0.0)
    attn_sums = split_shards(
        jnp.concatenate(
            [transposed_times(attn_in, attn_right).astype(BF16), output_grads], axis=1
        )
    )
    for level in range(fsdp_levels, 0, -1):
        attn_sums = scatter_fsdp_step(attn_sums, fsdp_count, level)
    attn_grads = attn_sums[0].astype(BF16)
    both_sums = scatter_ctx(tail_even, tail_odd)
    attn_in_grad = both_sums[:, :width]
    block_out = (resid + both_sums[:, width:]).astype(BF16)
    mlp_total = mlp_sums[0].astype(F32)
    for moved in mlp_moved.values():
        mlp_total = mlp_total + moved.astype(F32)
    mlp_grads = mlp_total.astype(BF16)
    own_wide = inputs.astype(F32)
    input_part = jax.vjp(lambda values: rms_norm(values, attn_gain_rel), own_wide)[1](
        attn_in_grad
    )[0]
    input_grad = resid_grad + input_part
    gains = sum_all(
        jnp.concatenate(
            [
                block_order(attn_gain_grad),
                block_order(mlp_gain_grad),
                query_gain_grad,
                key_gain_grad,
            ]
        )
    )

    def placed(own, widths):
        even, odd = gather_ctx(own)
        return place_columns(even, odd, widths, ctx_index)

    mlp_outs = placed(mlp_grads, (hidden_width,) * 3)
    attn_outs = placed(attn_grads, (query_width, kv_own, kv_own, query_width))
    return (
        block_order(block_out)[None],
        block_order(input_grad)[None],
        gains[:width],
        attn_outs[0],
        attn_outs[1],
        attn_outs[2],
        gains[2 * width : 2 * width + head_width],
        gains[2 * width + head_width :],
        attn_outs[3],
        gains[width : 2 * width],
        mlp_outs[0],
        mlp_outs[1],
        mlp_outs[2],
    )


def solution(mesh):
    in_specs = (
        P("fsdp", "ctx", None),
        P(),
        P(),
        P("fsdp", None),
        P("fsdp", None),
        P("fsdp", None),
        P(),
        P(),
        P("fsdp", None),
        P(),
        P("fsdp", None),
        P("fsdp", None),
        P("fsdp", None),
        P("fsdp", "ctx", None),
    )
    out_specs = (
        P("fsdp", "ctx", None),
        P("fsdp", "ctx", None),
        P(),
        P("fsdp", None),
        P("fsdp", None),
        P("fsdp", None),
        P(),
        P(),
        P("fsdp", None),
        P(),
        P("fsdp", None),
        P("fsdp", None),
        P("fsdp", None),
    )
    return jax.shard_map(
        on_device_all, mesh=mesh, in_specs=in_specs, out_specs=out_specs, check_vma=False
    )
```

```python
import functools
import math

import jax
import jax.numpy as jnp
from jax import lax
from jax.experimental import pallas as pl
from jax.experimental.pallas import tpu as pltpu
from jax.sharding import PartitionSpec as P


NORM_EPS = 1e-06
ROPE_BASE = 1000000.0
MASKED = -1e30
F32 = jnp.float32
BF16 = jnp.bfloat16


def rms_norm(values, gain_vec):
    return (
        values * lax.rsqrt(jnp.mean(values * values, axis=-1, keepdims=True) + NORM_EPS) * gain_vec
    )


def times_transposed(lhs_mat, rhs_mat):
    return lax.dot_general(
        lhs_mat, rhs_mat, (((1,), (1,)), ((), ())), preferred_element_type=F32
    )


def transposed_times(lhs_mat, rhs_mat):
    return lax.dot_general(
        lhs_mat, rhs_mat, (((0,), (0,)), ((), ())), preferred_element_type=F32
    )


def tie(*values):
    return lax.optimization_barrier(values)


def exchange(value, bit, axis):
    count = lax.axis_size(axis)
    return lax.ppermute(value, axis, [(index, index ^ bit) for index in range(count)])


def low_bit(number):
    return number & -number


def top_bit(number):
    return 1 << (number.bit_length() - 1)


def level_of(number):
    return bin(number).count("1")


def even_numbers(count, level):
    return [number for number in range(0, count, 2) if level_of(number) == level]


def gather_levels(count):
    return (count // 2).bit_length() - 1


def gather_ctx(own):
    count = lax.axis_size("ctx")
    rows = own.shape[0]
    half = rows // 2
    parts = {0: [own]}
    for level in range(1, gather_levels(count) + 1):
        for number in even_numbers(count, level):
            low, top = low_bit(number), top_bit(number)
            if level == 1:
                parts[number] = [exchange(own, low, "ctx")]
            else:
                parts[number] = [
                    exchange(rows_of(parts[number ^ top], 0, half), top, "ctx"),
                    exchange(rows_of(parts[number ^ low], half, rows), low, "ctx"),
                ]
    pieces = []
    for number in range(0, count, 2):
        start = number // 2 * rows
        for part in parts[number]:
            pieces.append((0, start, part))
            other = exchange(part, 1, "ctx")
            pieces.append((1, start, other))
            start += part.shape[0]
    return pieces


def rows_of(parts, start, stop):
    if len(parts) > 1:
        return parts[0 if start == 0 else 1]
    return parts[0][start:stop]


def fetch_pieces(step, refs, plan, buffers, sems, block_rows, columns=None):
    copies = []
    for number, (ref, (odd, start, rows)) in enumerate(zip(refs, plan)):
        source = ref if columns is None else ref.at[:, columns]
        copies.append(
            (
                start // block_rows,
                pltpu.make_async_copy(
                    source, buffers[odd].at[pl.ds(start, rows), :], sems.at[number]
                ),
            )
        )

    @pl.when(step == 0)
    def _():
        for _, copy in copies:
            copy.start()

    for block in range(buffers[0].shape[0] // block_rows):

        @pl.when(step == block)
        def _():
            for owner, copy in copies:
                if owner == block:
                    copy.wait()


def piece_plan(pieces):
    return [(odd, start, array.shape[0]) for odd, start, array in pieces]


def piece_arrays(pieces):
    return [array for _, _, array in pieces]


def piece_scratch(pieces, rows, width):
    return [
        pltpu.VMEM((rows, width), BF16),
        pltpu.VMEM((rows, width), BF16),
        pltpu.SemaphoreType.DMA((len(pieces),)),
    ]


def in_place(pieces):
    return [pl.BlockSpec(memory_space=pl.ANY)] * len(pieces)


def first_sums_kernel(even_ref, odd_ref, first_ref, second_ref):
    half = first_ref.shape[0]
    total = (even_ref[...].astype(F32) + odd_ref[...].astype(F32)).astype(BF16)
    first_ref[...] = total[:half]
    second_ref[...] = total[half:]


def next_sums_kernel(even_two, odd_two, even_four, odd_four, first, second, two_ref, four_ref):
    half = first.shape[0]
    two = even_two[...].astype(F32) + odd_two[...].astype(F32)
    two_ref[:half, :] = (two[:half] + first[...].astype(F32)).astype(BF16)
    two_ref[half:, :] = two[half:].astype(BF16)
    four = even_four[...].astype(F32) + odd_four[...].astype(F32)
    four_ref[:half, :] = four[:half].astype(BF16)
    four_ref[half:, :] = (four[half:] + second[...].astype(F32)).astype(BF16)


def scatter_eight(even, odd):
    moved = exchange(odd, 1, "ctx")
    rows = even.shape[0] // 4
    half = rows // 2
    width = even.shape[1]

    def block(number):
        return pl.BlockSpec((rows, width), lambda step: (number, 0))

    part = pl.BlockSpec((half, width), lambda step: (0, 0))
    cost = pl.CostEstimate(flops=0, bytes_accessed=8 * rows * width, transcendentals=0)
    first, second = pl.pallas_call(
        first_sums_kernel,
        out_shape=[jax.ShapeDtypeStruct((half, width), BF16)] * 2,
        grid=(1,),
        in_specs=[block(3), block(3)],
        out_specs=[part, part],
        cost_estimate=cost,
        name="first_sums",
    )(even, moved)
    first = exchange(first, 4, "ctx")
    second = exchange(second, 2, "ctx")
    two, four = pl.pallas_call(
        next_sums_kernel,
        out_shape=[jax.ShapeDtypeStruct((rows, width), BF16)] * 2,
        grid=(1,),
        in_specs=[block(1), block(1), block(2), block(2), part, part],
        out_specs=[block(0), block(0)],
        cost_estimate=cost,
        name="next_sums",
    )(even, moved, even, moved, first, second)
    two = exchange(two, 2, "ctx")
    four = exchange(four, 4, "ctx")
    return (
        (even[:rows].astype(F32) + moved[:rows].astype(F32))
        + two.astype(F32)
        + four.astype(F32)
    )


def scatter_ctx(even, odd):
    count = lax.axis_size("ctx")
    if count == 8:
        return scatter_eight(even, odd)
    rows = even.shape[0] * 2 // count
    half = rows // 2
    moved = exchange(odd, 1, "ctx")

    def piece(number, start, stop):
        base = number // 2 * rows
        return even[base + start : base + stop].astype(F32) + moved[
            base + start : base + stop
        ].astype(F32)

    halves = {
        number: [piece(number, 0, half), piece(number, half, rows)]
        for number in range(0, count, 2)
    }
    for level in range(gather_levels(count), 1, -1):
        for number in even_numbers(count, level):
            low, top = low_bit(number), top_bit(number)
            first, second = tie(*(part.astype(BF16) for part in halves[number]))
            halves[number ^ top][0] += exchange(first, top, "ctx").astype(F32)
            halves[number ^ low][1] += exchange(second, low, "ctx").astype(F32)
    total = jnp.concatenate(halves[0], axis=0)
    for number in even_numbers(count, 1):
        sent = jnp.concatenate(halves[number], axis=0).astype(BF16)
        total = total + exchange(sent, number, "ctx").astype(F32)
    return total


def gather_fsdp_step(blocks, count, level):
    blocks = dict(blocks)
    for number in range(1, count):
        if level_of(number) == level:
            low = low_bit(number)
            blocks[number] = exchange(blocks[number ^ low], low, "fsdp")
    return blocks


def scatter_fsdp_step(sums, count, level):
    sums = dict(sums)
    for number in range(1, count):
        if level_of(number) == level:
            low = low_bit(number)
            sums[number ^ low] = sums[number ^ low].astype(F32) + exchange(
                sums[number].astype(BF16), low, "fsdp"
            ).astype(F32)
    return sums


def sum_all(value):
    for axis in ("ctx", "fsdp"):
        bit = 1
        while bit < lax.axis_size(axis):
            value = value + exchange(value, bit, axis)
            bit *= 2
    return value


def whole(array):
    return pl.BlockSpec(array.shape, lambda *ids: (0,) * len(array.shape))


def pick_columns(picks):
    rows = picks[0][0].shape[0]
    widths = [width for _, _, width in picks]
    if any(width % 128 for width in widths):
        return jnp.concatenate(
            [
                lax.dynamic_slice_in_dim(array, index * width, width, axis=1)
                for array, index, width in picks
            ],
            axis=1,
        )

    def kernel(index_ref, *refs):
        start = 0
        for ref, width in zip(refs, widths):
            refs[-1][:, start : start + width] = ref[...]
            start += width

    def spec(number, width):
        return pl.BlockSpec((rows, width), lambda step, index_ref: (0, index_ref[number]))

    total = sum(widths)
    return pl.pallas_call(
        kernel,
        out_shape=jax.ShapeDtypeStruct((rows, total), picks[0][0].dtype),
        grid_spec=pltpu.PrefetchScalarGridSpec(
            num_scalar_prefetch=1,
            grid=(1,),
            in_specs=[spec(number, width) for number, width in enumerate(widths)],
            out_specs=pl.BlockSpec((rows, total), lambda step, index_ref: (0, 0)),
        ),
        cost_estimate=pl.CostEstimate(
            flops=0, bytes_accessed=4 * rows * total, transcendentals=0
        ),
        name="pick_columns",
    )(jnp.stack([index for _, index, _ in picks]).astype(jnp.int32), *[p[0] for p in picks])


def place_columns(pieces, widths, ctx_index):
    count = lax.axis_size("ctx")
    rows = pieces[0][2].shape[0]
    starts = [sum(widths[:number]) for number in range(len(widths))]
    if any(width % 128 for width in widths):
        placed = []
        for start, width in zip(starts, widths):
            result = jnp.zeros((rows, count * width), F32)
            for odd, row, array in pieces:
                result = lax.dynamic_update_slice(
                    result,
                    array[:, start : start + width].astype(F32),
                    (row % rows, (ctx_index ^ (row // rows * 2 + odd)) * width),
                )
            placed.append(result)
        return placed
    plan = piece_plan(pieces)

    def kernel(index_ref, *refs):
        step = pl.program_id(0)
        out_refs = refs[len(plan) : len(plan) + len(widths)]
        buffers, sems = refs[-3:-1], refs[-1]
        fetch_pieces(step, refs[: len(plan)], plan, buffers, sems, rows)
        here = pl.ds(pl.multiple_of(step * rows, rows), rows)
        for parity in range(2):

            @pl.when(index_ref[0] == parity)
            def _():
                sides = (buffers[1], buffers[0]) if parity else buffers
                for out_ref, start, width in zip(out_refs, starts, widths):
                    for side, ref in enumerate(sides):
                        out_ref[:, side * width : (side + 1) * width] = ref[
                            here, start : start + width
                        ].astype(F32)

    index = [ctx_index % 2] + [(ctx_index ^ number) // 2 for number in range(0, count, 2)]
    return pl.pallas_call(
        kernel,
        out_shape=[jax.ShapeDtypeStruct((rows, count * width), F32) for width in widths],
        grid_spec=pltpu.PrefetchScalarGridSpec(
            num_scalar_prefetch=1,
            grid=(count // 2,),
            in_specs=in_place(pieces),
            out_specs=[
                pl.BlockSpec((rows, 2 * width), lambda step, index_ref: (0, index_ref[step + 1]))
                for width in widths
            ],
            scratch_shapes=piece_scratch(pieces, rows * count // 2, sum(widths)),
        ),
        cost_estimate=pl.CostEstimate(
            flops=0, bytes_accessed=6 * count * rows * sum(widths), transcendentals=0
        ),
        name="place_columns",
    )(jnp.stack(index).astype(jnp.int32), *piece_arrays(pieces))


def own_kernel(index_ref, hidden_ref, cot_ref, both_ref):
    width = hidden_ref.shape[1]
    count = index_ref.shape[0]
    size = width // count
    for number in range(count):
        source = pl.ds(pl.multiple_of(index_ref[number] * size, size), size)
        target = slice(number * size, (number + 1) * size)
        both_ref[:, target] = hidden_ref[:, source]
        both_ref[:, width + target.start : width + target.stop] = cot_ref[:, source]


def own_blocks(hidden, cot, indices):
    rows, width = hidden.shape
    return pl.pallas_call(
        own_kernel,
        out_shape=jax.ShapeDtypeStruct((rows, 2 * width), BF16),
        in_specs=[pl.BlockSpec(memory_space=pltpu.SMEM)]
        + [pl.BlockSpec(memory_space=pltpu.VMEM)] * 2,
        out_specs=pl.BlockSpec(memory_space=pltpu.VMEM),
        cost_estimate=pl.CostEstimate(
            flops=0, bytes_accessed=8 * rows * width, transcendentals=0
        ),
        name="own_blocks",
    )(indices, hidden, cot)


def here_rows(buffers, step, rows):
    here = pl.ds(pl.multiple_of(step * rows, rows), rows)
    return jnp.concatenate([buffers[0][here, :], buffers[1][here, :]], axis=0)


def mlp_kernel(plan, chunks, *refs):
    pieces, refs = refs[: len(plan)], refs[len(plan) :]
    c_ref, w_refs, refs = refs[0], refs[1 : 1 + chunks], refs[1 + chunks :]
    right_ref, act_ref, even_ref, odd_ref, x_all = refs[:5]
    buffers, sems = refs[5:7], refs[7]
    step = pl.program_id(0)
    hidden = act_ref.shape[1]
    rows = even_ref.shape[0]
    size = even_ref.shape[1] // chunks
    fetch_pieces(step, pieces, plan, buffers, sems, rows)
    x = here_rows(buffers, step, rows)
    x_all[...] = x
    c = c_ref[...]
    both = jnp.zeros((2 * rows, 2 * hidden), F32)
    grad = jnp.zeros((2 * rows, hidden), F32)
    for number, w_ref in enumerate(w_refs):
        side = slice(number * size, (number + 1) * size)
        both += jnp.dot(x[:, side], w_ref[:, : 2 * hidden], preferred_element_type=F32)
        grad += jnp.dot(c[:, side], w_ref[:, 2 * hidden :], preferred_element_type=F32)
    gate = both[:, :hidden]
    upper = both[:, hidden:]
    sigma = jax.nn.sigmoid(gate)
    gate_sigma = gate * sigma
    act_ref[...] = (gate_sigma * upper).astype(BF16)
    right_ref[:, :hidden] = (grad * upper * sigma * (1.0 + gate * (1.0 - sigma))).astype(BF16)
    right_ref[:, hidden:] = (grad * gate_sigma).astype(BF16)
    right = right_ref[...]
    for number, w_ref in enumerate(w_refs):
        part = nt(right, w_ref[:, : 2 * hidden]).astype(BF16)
        even_ref[:, number * size : (number + 1) * size] = part[:rows]
        odd_ref[:, number * size : (number + 1) * size] = part[rows:]


def mlp_both(pieces, both_all, weights, count):
    total, width = both_all.shape
    width //= 2
    rows = total // count
    hidden = weights[0].shape[1] // 3
    block = pl.BlockSpec((rows, width), lambda step: (step, 0))

    def wide(columns):
        return pl.BlockSpec((2 * rows, columns), lambda step: (step, 0))

    return pl.pallas_call(
        functools.partial(mlp_kernel, piece_plan(pieces), len(weights)),
        out_shape=[
            jax.ShapeDtypeStruct((total, 2 * hidden), BF16),
            jax.ShapeDtypeStruct((total, hidden), BF16),
            jax.ShapeDtypeStruct((total // 2, width), BF16),
            jax.ShapeDtypeStruct((total // 2, width), BF16),
            jax.ShapeDtypeStruct((total, width), BF16),
        ],
        grid=(count // 2,),
        in_specs=in_place(pieces)
        + [pl.BlockSpec((2 * rows, width), lambda step: (step, 1))]
        + [whole(part) for part in weights],
        out_specs=[wide(2 * hidden), wide(hidden), block, block, wide(width)],
        scratch_shapes=piece_scratch(pieces, total // 2, width),
        cost_estimate=pl.CostEstimate(
            flops=10 * total * width * hidden,
            bytes_accessed=12 * total * width,
            transcendentals=total * hidden,
        ),
        name="mlp_both",
    )(*piece_arrays(pieces), both_all, *weights)


def grads_kernel(left_one, right_one, left_two, right_two, *out_refs):
    split = right_one.shape[1]
    for number, out_ref in enumerate(out_refs):

        @pl.when(pl.program_id(0) == number)
        def _():
            out_ref[:, :split] = transposed_times(left_one[...], right_one[...]).astype(BF16)
            out_ref[:, split:] = transposed_times(left_two[...], right_two[...]).astype(BF16)


def weight_grads(left_one, right_one, left_two, right_two, skipped=0):
    chunks = lax.axis_size("fsdp")
    total, width = left_one.shape
    size = width // chunks
    columns = right_one.shape[1] + right_two.shape[1]
    block = pl.BlockSpec((total, size), lambda step: (0, step))
    return pl.pallas_call(
        grads_kernel,
        out_shape=[jax.ShapeDtypeStruct((size, columns), BF16)] * chunks,
        grid=(chunks,),
        in_specs=[
            block,
            whole(right_one),
            pl.BlockSpec((total, size), lambda step: (0, skipped + step)),
            whole(right_two),
        ],
        out_specs=[pl.BlockSpec((size, columns), lambda step: (0, 0))] * chunks,
        cost_estimate=pl.CostEstimate(
            flops=2 * total * width * columns,
            bytes_accessed=4 * total * (width + columns),
            transcendentals=0,
        ),
        name="weight_grads",
    )(left_one, right_one, left_two, right_two)


def rotated(values, cosine, sine_part):
    return values * cosine + pltpu.roll(values, values.shape[1] // 2, 1) * sine_part


def head_scale(raw):
    return lax.rsqrt(jnp.mean(raw * raw, axis=-1, keepdims=True) + NORM_EPS)


def head_back(grad, raw, gain_row, cosine, sine_part):
    turned = grad * cosine + pltpu.roll(grad * sine_part, grad.shape[1] // 2, 1)
    scale = head_scale(raw)
    scaled = turned * gain_row
    mean_part = jnp.mean(scaled * raw, axis=-1, keepdims=True)
    return scale * scaled - raw * (scale * scale * scale * mean_part), turned * raw * scale


def project_kernel(plan, chunks, *refs):
    pieces, refs = refs[: len(plan)], refs[len(plan) :]
    w_refs, refs = refs[:chunks], refs[chunks:]
    gain_ref, qgain_ref, kgain_ref, cos_ref, sin_ref = refs[:5]
    in_ref, raw_ref, q_ref, k_ref, v_ref, both_ref = refs[5:11]
    buffers, sems = refs[11:13], refs[13]
    step = pl.program_id(0)
    head = qgain_ref.shape[1]
    q_width = q_ref.shape[1]
    kv_width = k_ref.shape[1]
    width = in_ref.shape[1]
    size = width // chunks
    rows = in_ref.shape[0] // 2
    fetch_pieces(step, pieces, plan, buffers, sems, rows)
    both = here_rows(buffers, step, rows)
    both_ref[...] = both
    normed = rms_norm(both[:, :width].astype(F32), gain_ref[...]).astype(BF16)
    in_ref[...] = normed
    raw = jnp.zeros((2 * rows, q_width + 2 * kv_width), F32)
    for number, w_ref in enumerate(w_refs):
        raw += jnp.dot(
            normed[:, number * size : (number + 1) * size],
            w_ref[...],
            preferred_element_type=F32,
        )
    raw_ref[...] = raw[:, : q_width + kv_width]
    cosine = cos_ref[...]
    sine_part = sin_ref[...]
    for column in range(0, q_width, head):
        part = raw[:, column : column + head]
        q_ref[:, column : column + head] = rotated(
            part * head_scale(part) * qgain_ref[...], cosine, sine_part
        ).astype(BF16)
    for column in range(0, kv_width, head):
        part = raw[:, q_width + column : q_width + column + head]
        k_ref[:, column : column + head] = rotated(
            part * head_scale(part) * kgain_ref[...], cosine, sine_part
        ).astype(BF16)
    v_ref[...] = raw[:, q_width + kv_width :].astype(BF16)


def project(pieces, weights, gain, q_gain, k_gain, cosine, sine_part, q_width, kv_width):
    width = gain.shape[1]
    head = q_gain.shape[1]
    total = cosine.shape[0]
    steps = lax.axis_size("ctx") // 2
    rows = total // (2 * steps)

    def wide(columns):
        return pl.BlockSpec((2 * rows, columns), lambda step: (step, 0))

    first_columns = pl.BlockSpec(
        (weights[0].shape[0], q_width + 2 * kv_width), lambda step: (0, 0)
    )
    return pl.pallas_call(
        functools.partial(project_kernel, piece_plan(pieces), len(weights)),
        out_shape=[
            jax.ShapeDtypeStruct((total, width), BF16),
            jax.ShapeDtypeStruct((total, q_width + kv_width), F32),
            jax.ShapeDtypeStruct((total, q_width), BF16),
            jax.ShapeDtypeStruct((total, kv_width), BF16),
            jax.ShapeDtypeStruct((total, kv_width), BF16),
            jax.ShapeDtypeStruct((total, 2 * width), BF16),
        ],
        grid=(steps,),
        in_specs=in_place(pieces)
        + [first_columns] * len(weights)
        + [whole(gain), whole(q_gain), whole(k_gain), wide(head), wide(head)],
        out_specs=[
            wide(width), wide(q_width + kv_width), wide(q_width), wide(kv_width), wide(kv_width),
            wide(2 * width),
        ],
        scratch_shapes=piece_scratch(pieces, total // 2, 2 * width),
        cost_estimate=pl.CostEstimate(
            flops=2 * total * width * (q_width + 2 * kv_width),
            bytes_accessed=12 * total * width,
            transcendentals=total,
        ),
        name="project",
    )(*piece_arrays(pieces), *weights, gain, q_gain, k_gain, cosine, sine_part)


def nt(lhs, rhs):
    return lax.dot_general(lhs, rhs, (((1,), (1,)), ((), ())), preferred_element_type=F32)


def attend_kernel(chunks, q_ref, k_ref, v_ref, row_ref, col_ref, *refs):
    w_refs, refs = refs[:chunks], refs[chunks:]
    mix_ref, lse_ref, even_ref, odd_ref, vt_ref = refs
    kv_width = k_ref.shape[1]
    q_width = q_ref.shape[1]
    head = q_width // lse_ref.shape[0]
    group = q_width // kv_width
    scale = 1.0 / math.sqrt(head)

    @pl.when(pl.program_id(0) == 0)
    def _():
        vt_ref[...] = v_ref[...].astype(F32).T.astype(BF16)

    allowed = col_ref[...] <= row_ref[...]
    for number in range(q_width // head):
        kv = number // group * head
        column = number * head
        scores = jnp.where(
            allowed, nt(k_ref[:, kv : kv + head], q_ref[:, column : column + head]) * scale, MASKED
        )
        top = jnp.max(scores, axis=0, keepdims=True)
        raised = jnp.exp(scores - top)
        total = jnp.sum(raised, axis=0, keepdims=True)
        lse_ref[number : number + 1, :] = top + jnp.log(total)
        probs = (raised * (1.0 / total)).astype(BF16)
        mixed = jnp.dot(vt_ref[kv : kv + head, :], probs, preferred_element_type=F32)
        mix_ref[:, column : column + head] = mixed.T.astype(BF16)
    rows = even_ref.shape[0]
    size = even_ref.shape[1] // chunks
    mix = mix_ref[...]
    for number, w_ref in enumerate(w_refs):
        out = nt(mix, w_ref[...]).astype(BF16)
        even_ref[:, number * size : (number + 1) * size] = out[:rows]
        odd_ref[:, number * size : (number + 1) * size] = out[rows:]


def attend(q, k, v, pos_row, pos_col, weights, head):
    total, q_width = q.shape
    kv_width = k.shape[1]
    width = weights[0].shape[0] * len(weights)
    steps = lax.axis_size("ctx") // 2
    rows = total // (2 * steps)
    heads = q_width // head
    last_columns = pl.BlockSpec(
        (weights[0].shape[0], q_width), lambda step: (0, weights[0].shape[1] // q_width - 1)
    )

    def wide(columns):
        return pl.BlockSpec((2 * rows, columns), lambda step: (step, 0))

    half = pl.BlockSpec((rows, width), lambda step: (step, 0))
    return pl.pallas_call(
        functools.partial(attend_kernel, len(weights)),
        out_shape=[
            jax.ShapeDtypeStruct((total, q_width), BF16),
            jax.ShapeDtypeStruct((heads, total), F32),
            jax.ShapeDtypeStruct((total // 2, width), BF16),
            jax.ShapeDtypeStruct((total // 2, width), BF16),
        ],
        grid=(steps,),
        in_specs=[
            wide(q_width), whole(k), whole(v),
            pl.BlockSpec((1, 2 * rows), lambda step: (0, step)),
            whole(pos_col),
        ]
        + [last_columns] * len(weights),
        out_specs=[
            wide(q_width), pl.BlockSpec((heads, 2 * rows), lambda step: (0, step)), half, half,
        ],
        scratch_shapes=[pltpu.VMEM((kv_width, total), BF16)],
        cost_estimate=pl.CostEstimate(
            flops=4 * total * total * q_width,
            bytes_accessed=8 * total * width,
            transcendentals=total * total * heads,
        ),
        name="attend",
    )(q, k, v, pos_row, pos_col, *weights)


def attend_back_kernel(plan, chunks, *refs):
    pieces, refs = refs[: len(plan)], refs[len(plan) :]
    w_refs, refs = refs[:chunks], refs[chunks:]
    q_ref, k_ref, v_ref, row_ref, col_ref, mix_ref, lse_ref = refs[:7]
    raw_ref, qgain_ref, cos_ref, sin_ref = refs[7:11]
    low_ref, dk_ref, dv_ref, dgain_ref, all_ref = refs[11:16]
    buffers, sems, kt_ref = refs[16:18], refs[18], refs[19]
    step = pl.program_id(0)
    head = qgain_ref.shape[1]
    kv_width = k_ref.shape[1]
    q_width = q_ref.shape[1]
    group = q_width // kv_width
    scale = 1.0 / math.sqrt(head)
    rows = q_ref.shape[0] // 2
    size = all_ref.shape[1] // chunks

    @pl.when(pl.program_id(0) == 0)
    def _():
        kt_ref[...] = k_ref[...].astype(F32).T.astype(BF16)
        dk_ref[...] = jnp.zeros_like(dk_ref)
        dv_ref[...] = jnp.zeros_like(dv_ref)
        dgain_ref[...] = jnp.zeros_like(dgain_ref)

    fetch_pieces(step, pieces, plan, buffers, sems, rows)
    grad = here_rows(buffers, step, rows)
    all_ref[...] = grad
    dmix_all = jnp.zeros((2 * rows, q_width), F32)
    for number, w_ref in enumerate(w_refs):
        dmix_all += jnp.dot(
            grad[:, number * size : (number + 1) * size],
            w_ref[...],
            preferred_element_type=F32,
        )
    dmix_all = dmix_all.astype(BF16)
    allowed = col_ref[...] <= row_ref[...]
    for number in range(q_width // head):
        kv = number // group * head
        column = number * head
        q = q_ref[:, column : column + head]
        dmix = dmix_all[:, column : column + head]
        mix = mix_ref[:, column : column + head]
        delta = jnp.sum((dmix.astype(F32) * mix.astype(F32)).T, axis=0, keepdims=True)
        scores = nt(k_ref[:, kv : kv + head], q) * scale
        probs = jnp.exp(jnp.where(allowed, scores - lse_ref[number : number + 1, :], MASKED))
        dv_ref[:, kv : kv + head] += jnp.dot(
            probs.astype(BF16), dmix, preferred_element_type=F32
        )
        prob_grad = nt(v_ref[:, kv : kv + head], dmix)
        score_grad = (probs * (prob_grad - delta) * scale).astype(BF16)
        dk_ref[:, kv : kv + head] += jnp.dot(score_grad, q, preferred_element_type=F32)
        dq = jnp.dot(kt_ref[kv : kv + head, :], score_grad, preferred_element_type=F32).T
        raw_grad, gain_part = head_back(
            dq, raw_ref[:, column : column + head], qgain_ref[...], cos_ref[...], sin_ref[...]
        )
        low_ref[:, column : column + head] = raw_grad.astype(BF16)
        dgain_ref[...] += jnp.sum(gain_part, axis=0, keepdims=True)


def attend_back(pieces, weights, q, k, v, pos_row, pos_col, mix, lse, raw, q_gain, cosine, sine_part):
    total, q_width = q.shape
    kv_width = k.shape[1]
    width = weights[0].shape[0] * len(weights)
    steps = lax.axis_size("ctx") // 2
    rows = total // (2 * steps)
    heads = lse.shape[0]
    last_columns = pl.BlockSpec(
        (weights[0].shape[0], q_width), lambda step: (0, weights[0].shape[1] // q_width - 1)
    )
    head = q_gain.shape[1]

    def wide(columns):
        return pl.BlockSpec((2 * rows, columns), lambda step: (step, 0))

    def fixed(shape):
        return pl.BlockSpec(shape, lambda step: (0, 0))

    return pl.pallas_call(
        functools.partial(attend_back_kernel, piece_plan(pieces), len(weights)),
        out_shape=[
            jax.ShapeDtypeStruct((total, q_width), BF16),
            jax.ShapeDtypeStruct((total, kv_width), F32),
            jax.ShapeDtypeStruct((total, kv_width), F32),
            jax.ShapeDtypeStruct((1, head), F32),
            jax.ShapeDtypeStruct((total, width), BF16),
        ],
        grid=(steps,),
        in_specs=in_place(pieces)
        + [last_columns] * len(weights)
        + [
            wide(q_width), whole(k), whole(v),
            pl.BlockSpec((1, 2 * rows), lambda step: (0, step)),
            whole(pos_col), wide(q_width),
            pl.BlockSpec((heads, 2 * rows), lambda step: (0, step)),
            wide(q_width), whole(q_gain), wide(head), wide(head),
        ],
        out_specs=[
            wide(q_width), fixed((total, kv_width)), fixed((total, kv_width)), fixed((1, head)),
            wide(width),
        ],
        scratch_shapes=piece_scratch(pieces, total // 2, width)
        + [pltpu.VMEM((kv_width, total), BF16)],
        cost_estimate=pl.CostEstimate(
            flops=10 * total * total * q_width,
            bytes_accessed=8 * total * width,
            transcendentals=total * total * heads,
        ),
        name="attend_back",
    )(
        *piece_arrays(pieces), *weights,
        q, k, v, pos_row, pos_col, mix, lse, raw, q_gain, cosine, sine_part,
    )


def project_back_kernel(
    chunks, low_ref, dk_ref, dv_ref, raw_ref, kgain_ref, cos_ref, sin_ref, x_ref, blk_ref, *refs
):
    w_refs, refs = refs[:chunks], refs[chunks:]
    right_ref, even_ref, odd_ref, again_ref, dgain_ref = refs
    head = kgain_ref.shape[1]
    kv_width = dk_ref.shape[1]
    q_width = low_ref.shape[1]
    rows = even_ref.shape[0]
    width = x_ref.shape[1]
    size = width // chunks

    @pl.when(pl.program_id(0) == 0)
    def _():
        again_ref[...] = jnp.zeros_like(again_ref)
        dgain_ref[...] = jnp.zeros_like(dgain_ref)

    right_ref[:, :q_width] = low_ref[...]
    for column in range(0, kv_width, head):
        raw_grad, gain_part = head_back(
            dk_ref[:, column : column + head],
            raw_ref[:, q_width + column : q_width + column + head],
            kgain_ref[...],
            cos_ref[...],
            sin_ref[...],
        )
        right_ref[:, q_width + column : q_width + column + head] = raw_grad.astype(BF16)
        dgain_ref[...] += jnp.sum(gain_part, axis=0, keepdims=True)
    right_ref[:, q_width + kv_width :] = dv_ref[...].astype(BF16)
    right = right_ref[...]
    x = x_ref[...].astype(F32)
    normed = x * head_scale(x)
    for number, w_ref in enumerate(w_refs):
        side = slice(number * size, (number + 1) * size)
        part = nt(right, w_ref[...])
        again_ref[:, side] += jnp.sum(part * normed[:, side], axis=0, keepdims=True)
        part = part.astype(BF16)
        even_ref[:, side] = part[:rows]
        odd_ref[:, side] = part[rows:]
    even_ref[:, width:] = blk_ref[:rows, :]
    odd_ref[:, width:] = blk_ref[rows:, :]


def project_back(low, dk, dv, raw, k_gain, cosine, sine_part, both_all, weights, block_part):
    total, q_width = low.shape
    kv_width = dk.shape[1]
    width = both_all.shape[1] // 2
    steps = lax.axis_size("ctx") // 2
    rows = total // (2 * steps)
    head = k_gain.shape[1]

    def wide(columns):
        return pl.BlockSpec((2 * rows, columns), lambda step: (step, 0))

    def fixed(shape):
        return pl.BlockSpec(shape, lambda step: (0, 0))

    first_columns = pl.BlockSpec(
        (weights[0].shape[0], q_width + 2 * kv_width), lambda step: (0, 0)
    )
    both = pl.BlockSpec((rows, 2 * width), lambda step: (step, 0))
    return pl.pallas_call(
        functools.partial(project_back_kernel, len(weights)),
        out_shape=[
            jax.ShapeDtypeStruct((total, q_width + 2 * kv_width), BF16),
            jax.ShapeDtypeStruct((total // 2, 2 * width), BF16),
            jax.ShapeDtypeStruct((total // 2, 2 * width), BF16),
            jax.ShapeDtypeStruct((1, width), F32),
            jax.ShapeDtypeStruct((1, head), F32),
        ],
        grid=(steps,),
        in_specs=[
            wide(q_width), wide(kv_width), wide(kv_width), wide(q_width + kv_width),
            whole(k_gain), wide(head), wide(head), wide(width), wide(width),
        ]
        + [first_columns] * len(weights),
        out_specs=[
            wide(q_width + 2 * kv_width), both, both, fixed((1, width)), fixed((1, head)),
        ],
        cost_estimate=pl.CostEstimate(
            flops=2 * total * width * (q_width + 2 * kv_width),
            bytes_accessed=12 * total * width,
            transcendentals=total,
        ),
        name="project_back",
    )(low, dk, dv, raw, k_gain, cosine, sine_part, both_all, block_part, *weights)


def on_device_all(
    hidden_in,
    pair_table,
    attn_gain,
    query_proj,
    key_proj,
    value_proj,
    query_gain,
    key_gain,
    output_proj,
    mlp_gain,
    gate_proj,
    up_proj,
    down_proj,
    cotangent,
):
    fsdp_count = lax.axis_size("fsdp")
    fsdp_index = lax.axis_index("fsdp")
    ctx_count = lax.axis_size("ctx")
    ctx_index = lax.axis_index("ctx")
    row_count, width = hidden_in.shape[1:]
    block_len = row_count // 2
    total_rows = ctx_count * row_count
    shard_rows = width // fsdp_count
    head_width = query_gain.shape[0]
    half_head = head_width // 2
    kvhead_total = key_proj.shape[1] // head_width
    kv_count = max(1, kvhead_total // ctx_count)
    kv_share = max(1, ctx_count // kvhead_total)
    query_width = query_proj.shape[1] // ctx_count
    kv_width = kv_count * head_width
    kv_own = key_proj.shape[1] // ctx_count
    hidden_width = gate_proj.shape[1] // ctx_count

    fsdp_order = fsdp_index ^ jnp.arange(fsdp_count, dtype=jnp.int32)

    def block_order(values):
        return jnp.concatenate(
            [
                lax.dynamic_slice_in_dim(
                    values, (fsdp_index ^ number) * shard_rows, shard_rows, axis=values.ndim - 1
                )
                for number in range(fsdp_count)
            ],
            axis=-1,
        )

    def columns(weights, start, size):
        return lax.dynamic_slice_in_dim(weights, start, size, axis=1)

    kv_index = ctx_index // kv_share
    both_own = own_blocks(hidden_in[0], cotangent[0], fsdp_order)
    inputs = both_own[:, :width]
    cot_low = both_own[:, width:]
    gains_rel = block_order(jnp.stack([attn_gain, mlp_gain]))
    attn_gain_rel = gains_rel[0]
    mlp_gain_rel = gains_rel[1]
    fsdp_levels = (fsdp_count - 1).bit_length()
    attn_width = query_width + 2 * kv_width

    both_pieces = gather_ctx(both_own)
    first_shard = pick_columns(
        [
            (query_proj, ctx_index, query_width),
            (key_proj, kv_index, kv_width),
            (value_proj, kv_index, kv_width),
            (output_proj, ctx_index, query_width),
        ]
    )
    first_blocks = {0: first_shard}
    for level in range(1, fsdp_levels + 1):
        first_blocks = gather_fsdp_step(first_blocks, fsdp_count, level)
    first_parts = [first_blocks[number] for number in range(fsdp_count)]
    mlp_shard = pick_columns(
        [(weights, ctx_index, hidden_width) for weights in (gate_proj, up_proj, down_proj)]
    )
    mlp_blocks = gather_fsdp_step({0: mlp_shard}, fsdp_count, 1)

    owner_ids = ctx_index ^ jnp.arange(ctx_count, dtype=jnp.int32)
    picked = owner_ids[:, None] == jnp.arange(ctx_count, dtype=jnp.int32)[None, :]
    block_ids = jnp.sum(jnp.where(picked[:, :, None], pair_table[None], 0), axis=1)
    positions = (
        block_ids[:, :, None] * block_len + jnp.arange(block_len, dtype=jnp.int32)
    ).reshape(total_rows)
    pos_row = positions.reshape(1, total_rows)
    pos_col = positions.reshape(total_rows, 1)
    lanes = jnp.arange(head_width, dtype=jnp.int32)
    frequency = ROPE_BASE ** (-((lanes % half_head).astype(F32) * 2.0 / head_width))
    angles = positions.astype(F32)[:, None] * frequency[None, :]
    cosine = jnp.cos(angles)
    sine_part = jnp.sin(angles) * jnp.where(lanes < half_head, -1.0, 1.0)[None, :]

    query_row = query_gain.reshape(1, head_width)
    key_row = key_gain.reshape(1, head_width)
    attn_in, attn_raw, query_heads, key_heads, value_heads, both_all = project(
        both_pieces, first_parts, attn_gain_rel.reshape(1, width), query_row, key_row,
        cosine, sine_part, query_width, kv_width,
    )
    attn_mix, log_total, mix_even, mix_odd = attend(
        query_heads, key_heads, value_heads, pos_row, pos_col, first_parts, head_width
    )

    resid_sum = scatter_ctx(mix_even, mix_odd)
    resid = inputs.astype(F32) + resid_sum
    mlp_in = rms_norm(resid, mlp_gain_rel).astype(BF16)
    for level in range(2, fsdp_levels + 1):
        mlp_blocks = gather_fsdp_step(mlp_blocks, fsdp_count, level)
    mlp_parts = [mlp_blocks[number] for number in range(fsdp_count)]
    mlp_pieces = gather_ctx(mlp_in)
    mlp_right, hidden_act, part_even, part_odd, mlp_all = mlp_both(
        mlp_pieces, both_all, mlp_parts, ctx_count
    )
    mlp_in_grad = scatter_ctx(part_even, part_odd)
    mlp_sums = dict(enumerate(weight_grads(mlp_all, mlp_right, both_all, hidden_act, fsdp_count)))
    down_w = jnp.concatenate([part[:, 2 * hidden_width :] for part in mlp_parts], axis=0)
    block_part = times_transposed(hidden_act, down_w).astype(BF16)
    resid_part, mlp_gain_grad = jax.vjp(rms_norm, resid, mlp_gain_rel)[1](mlp_in_grad)
    resid_grad = cot_low.astype(F32) + resid_part
    resid_low = resid_grad.astype(BF16)
    for level in range(fsdp_levels, 1, -1):
        mlp_sums = scatter_fsdp_step(mlp_sums, fsdp_count, level)
    resid_pieces = gather_ctx(resid_low)
    mlp_moved = {
        number: exchange(mlp_sums[number].astype(BF16), number, "fsdp")
        for number in range(1, fsdp_count)
        if level_of(number) == 1
    }
    query_low, key_grad, value_grad, query_gain_grad, resid_all = attend_back(
        resid_pieces, first_parts, query_heads, key_heads, value_heads, pos_row, pos_col,
        attn_mix, log_total, attn_raw, query_row, cosine, sine_part,
    )
    bit = 1
    while bit < kv_share:
        moved = exchange(jnp.concatenate([key_grad, value_grad], axis=1), bit, "ctx")
        moved = moved.reshape(ctx_count, row_count, 2 * kv_width)
        moved = jnp.concatenate([moved[number ^ bit] for number in range(ctx_count)], axis=0)
        key_grad = key_grad + moved[:, :kv_width]
        value_grad = value_grad + moved[:, kv_width:]
        bit *= 2
    own_parts = first_parts
    own_start = (ctx_index % kv_share) * kv_own
    if kv_share > 1:
        place = jnp.arange(attn_width) - query_width
        owned = (place < 0) | (
            (place % kv_width >= own_start) & (place % kv_width < own_start + kv_own)
        )
        own_parts = [
            jnp.where(owned[None, :], part[:, :attn_width], 0).astype(BF16)
            for part in first_parts
        ]
    attn_right, tail_even, tail_odd, attn_gain_grad, key_gain_grad = project_back(
        query_low, key_grad, value_grad, attn_raw, key_row, cosine, sine_part,
        both_all, own_parts, block_part,
    )
    attn_gain_grad = attn_gain_grad[0]
    query_gain_grad = query_gain_grad[0]
    key_gain_grad = key_gain_grad[0]
    if kv_share > 1:
        attn_right = jnp.concatenate(
            [
                attn_right[:, :query_width],
                columns(attn_right, query_width + own_start, kv_own),
                columns(attn_right, query_width + kv_width + own_start, kv_own),
            ],
            axis=1,
        )
        key_gain_grad = jnp.where(ctx_index % kv_share == 0, key_gain_grad, 0.0)
    attn_sums = dict(enumerate(weight_grads(attn_in, attn_right, resid_all, attn_mix)))
    for level in range(fsdp_levels, 0, -1):
        attn_sums = scatter_fsdp_step(attn_sums, fsdp_count, level)
    attn_grads = attn_sums[0].astype(BF16)
    both_sums = scatter_ctx(tail_even, tail_odd)
    attn_in_grad = both_sums[:, :width]
    block_out = (resid + both_sums[:, width:]).astype(BF16)
    mlp_total = mlp_sums[0].astype(F32)
    for moved in mlp_moved.values():
        mlp_total = mlp_total + moved.astype(F32)
    mlp_grads = mlp_total.astype(BF16)
    own_wide = inputs.astype(F32)
    input_part = jax.vjp(lambda values: rms_norm(values, attn_gain_rel), own_wide)[1](
        attn_in_grad
    )[0]
    input_grad = resid_grad + input_part
    gains = sum_all(
        jnp.concatenate(
            [
                block_order(attn_gain_grad),
                block_order(mlp_gain_grad),
                query_gain_grad,
                key_gain_grad,
            ]
        )
    )

    outs = (
        block_order(block_out)[None],
        block_order(input_grad)[None],
        gains[:width],
        gains[2 * width : 2 * width + head_width],
        gains[2 * width + head_width :],
        gains[width : 2 * width],
    )
    mlp_pieces = gather_ctx(mlp_grads)
    mlp_outs = place_columns(mlp_pieces, (hidden_width,) * 3, ctx_index)
    attn_pieces = gather_ctx(attn_grads)
    last_piece, *outs = tie(attn_pieces[-1][2], *outs)
    attn_pieces[-1] = attn_pieces[-1][:2] + (last_piece,)
    attn_outs = place_columns(attn_pieces, (query_width, kv_own, kv_own, query_width), ctx_index)
    return (
        outs[0],
        outs[1],
        outs[2],
        attn_outs[0],
        attn_outs[1],
        attn_outs[2],
        outs[3],
        outs[4],
        attn_outs[3],
        outs[5],
        mlp_outs[0],
        mlp_outs[1],
        mlp_outs[2],
    )


def solution(mesh):
    in_specs = (
        P("fsdp", "ctx", None),
        P(),
        P(),
        P("fsdp", None),
        P("fsdp", None),
        P("fsdp", None),
        P(),
        P(),
        P("fsdp", None),
        P(),
        P("fsdp", None),
        P("fsdp", None),
        P("fsdp", None),
        P("fsdp", "ctx", None),
    )
    out_specs = (
        P("fsdp", "ctx", None),
        P("fsdp", "ctx", None),
        P(),
        P("fsdp", None),
        P("fsdp", None),
        P("fsdp", None),
        P(),
        P(),
        P("fsdp", None),
        P(),
        P("fsdp", None),
        P("fsdp", None),
        P("fsdp", None),
    )
    return jax.shard_map(
        on_device_all, mesh=mesh, in_specs=in_specs, out_specs=out_specs, check_vma=False
    )
```

```python
import functools
import math

import jax
import jax.numpy as jnp
from jax import lax
from jax.experimental import pallas as pl
from jax.experimental.pallas import tpu as pltpu
from jax.sharding import PartitionSpec as P


NORM_EPS = 1e-06
ROPE_BASE = 1000000.0
MASKED = -1e30
F32 = jnp.float32
BF16 = jnp.bfloat16


def rms_norm(values, gain_vec):
    return (
        values * lax.rsqrt(jnp.mean(values * values, axis=-1, keepdims=True) + NORM_EPS) * gain_vec
    )


def transposed_times(lhs_mat, rhs_mat):
    return lax.dot_general(
        lhs_mat, rhs_mat, (((0,), (0,)), ((), ())), preferred_element_type=F32
    )


def tie(*values):
    return lax.optimization_barrier(values)


def exchange(value, bit, axis):
    count = lax.axis_size(axis)
    return lax.ppermute(value, axis, [(index, index ^ bit) for index in range(count)])


def low_bit(number):
    return number & -number


def top_bit(number):
    return 1 << (number.bit_length() - 1)


def level_of(number):
    return bin(number).count("1")


def even_numbers(count, level):
    return [number for number in range(0, count, 2) if level_of(number) == level]


def gather_levels(count):
    return (count // 2).bit_length() - 1


def gather_ctx(own):
    count = lax.axis_size("ctx")
    rows = own.shape[0]
    half = rows // 2
    parts = {0: [own]}
    for level in range(1, gather_levels(count) + 1):
        for number in even_numbers(count, level):
            low, top = low_bit(number), top_bit(number)
            if level == 1:
                parts[number] = [exchange(own, low, "ctx")]
            else:
                parts[number] = [
                    exchange(rows_of(parts[number ^ top], 0, half), top, "ctx"),
                    exchange(rows_of(parts[number ^ low], half, rows), low, "ctx"),
                ]
    pieces = []
    for number in range(0, count, 2):
        start = number // 2 * rows
        for part in parts[number]:
            pieces.append((0, start, part))
            other = exchange(part, 1, "ctx")
            pieces.append((1, start, other))
            start += part.shape[0]
    return pieces


def rows_of(parts, start, stop):
    if len(parts) > 1:
        return parts[0 if start == 0 else 1]
    return parts[0][start:stop]


def fetch_pieces(step, refs, plan, buffers, sems, block_rows, columns=None):
    copies = []
    for number, (ref, (odd, start, rows)) in enumerate(zip(refs, plan)):
        source = ref if columns is None else ref.at[:, columns]
        copies.append(
            (
                start // block_rows,
                pltpu.make_async_copy(
                    source, buffers[odd].at[pl.ds(start, rows), :], sems.at[number]
                ),
            )
        )

    @pl.when(step == 0)
    def _():
        for _, copy in copies:
            copy.start()

    for block in range(buffers[0].shape[0] // block_rows):

        @pl.when(step == block)
        def _():
            for owner, copy in copies:
                if owner == block:
                    copy.wait()


def piece_plan(pieces):
    return [(odd, start, array.shape[0]) for odd, start, array in pieces]


def piece_arrays(pieces):
    return [array for _, _, array in pieces]


def piece_scratch(pieces, rows, width):
    return [
        pltpu.VMEM((rows, width), BF16),
        pltpu.VMEM((rows, width), BF16),
        pltpu.SemaphoreType.DMA((len(pieces),)),
    ]


def in_place(pieces):
    return [pl.BlockSpec(memory_space=pl.ANY)] * len(pieces)


def first_sums_kernel(even_ref, odd_ref, first_ref, second_ref):
    half = first_ref.shape[0]
    total = (even_ref[...].astype(F32) + odd_ref[...].astype(F32)).astype(BF16)
    first_ref[...] = total[:half]
    second_ref[...] = total[half:]


def next_sums_kernel(even_two, odd_two, even_four, odd_four, first, second, two_ref, four_ref):
    half = first.shape[0]
    two = even_two[...].astype(F32) + odd_two[...].astype(F32)
    two_ref[:half, :] = (two[:half] + first[...].astype(F32)).astype(BF16)
    two_ref[half:, :] = two[half:].astype(BF16)
    four = even_four[...].astype(F32) + odd_four[...].astype(F32)
    four_ref[:half, :] = four[:half].astype(BF16)
    four_ref[half:, :] = (four[half:] + second[...].astype(F32)).astype(BF16)


def scatter_eight(even, odd):
    moved = exchange(odd, 1, "ctx")
    rows = even.shape[0] // 4
    half = rows // 2
    width = even.shape[1]

    def block(number):
        return pl.BlockSpec((rows, width), lambda step: (number, 0))

    part = pl.BlockSpec((half, width), lambda step: (0, 0))
    cost = pl.CostEstimate(flops=0, bytes_accessed=8 * rows * width, transcendentals=0)
    first, second = pl.pallas_call(
        first_sums_kernel,
        out_shape=[jax.ShapeDtypeStruct((half, width), BF16)] * 2,
        grid=(1,),
        in_specs=[block(3), block(3)],
        out_specs=[part, part],
        cost_estimate=cost,
        name="first_sums",
    )(even, moved)
    first = exchange(first, 4, "ctx")
    second = exchange(second, 2, "ctx")
    two, four = pl.pallas_call(
        next_sums_kernel,
        out_shape=[jax.ShapeDtypeStruct((rows, width), BF16)] * 2,
        grid=(1,),
        in_specs=[block(1), block(1), block(2), block(2), part, part],
        out_specs=[block(0), block(0)],
        cost_estimate=cost,
        name="next_sums",
    )(even, moved, even, moved, first, second)
    two = exchange(two, 2, "ctx")
    four = exchange(four, 4, "ctx")
    return (
        (even[:rows].astype(F32) + moved[:rows].astype(F32))
        + two.astype(F32)
        + four.astype(F32)
    )


def scatter_ctx(even, odd):
    count = lax.axis_size("ctx")
    if count == 8:
        return scatter_eight(even, odd)
    rows = even.shape[0] * 2 // count
    half = rows // 2
    moved = exchange(odd, 1, "ctx")

    def piece(number, start, stop):
        base = number // 2 * rows
        return even[base + start : base + stop].astype(F32) + moved[
            base + start : base + stop
        ].astype(F32)

    halves = {
        number: [piece(number, 0, half), piece(number, half, rows)]
        for number in range(0, count, 2)
    }
    for level in range(gather_levels(count), 1, -1):
        for number in even_numbers(count, level):
            low, top = low_bit(number), top_bit(number)
            first, second = tie(*(part.astype(BF16) for part in halves[number]))
            halves[number ^ top][0] += exchange(first, top, "ctx").astype(F32)
            halves[number ^ low][1] += exchange(second, low, "ctx").astype(F32)
    total = jnp.concatenate(halves[0], axis=0)
    for number in even_numbers(count, 1):
        sent = jnp.concatenate(halves[number], axis=0).astype(BF16)
        total = total + exchange(sent, number, "ctx").astype(F32)
    return total


def gather_fsdp_step(blocks, count, level):
    blocks = dict(blocks)
    for number in range(1, count):
        if level_of(number) == level:
            low = low_bit(number)
            blocks[number] = exchange(blocks[number ^ low], low, "fsdp")
    return blocks


def scatter_fsdp_step(sums, count, level):
    sums = dict(sums)
    for number in range(1, count):
        if level_of(number) == level:
            low = low_bit(number)
            sums[number ^ low] = sums[number ^ low].astype(F32) + exchange(
                sums[number].astype(BF16), low, "fsdp"
            ).astype(F32)
    return sums


def sum_all(value):
    for axis in ("ctx", "fsdp"):
        bit = 1
        while bit < lax.axis_size(axis):
            value = value + exchange(value, bit, axis)
            bit *= 2
    return value


def whole(array):
    return pl.BlockSpec(array.shape, lambda *ids: (0,) * len(array.shape))


def pick_columns(picks):
    rows = picks[0][0].shape[0]
    widths = [width for _, _, width in picks]
    if any(width % 128 for width in widths):
        return jnp.concatenate(
            [
                lax.dynamic_slice_in_dim(array, index * width, width, axis=1)
                for array, index, width in picks
            ],
            axis=1,
        )

    def kernel(index_ref, *refs):
        start = 0
        for ref, width in zip(refs, widths):
            refs[-1][:, start : start + width] = ref[...]
            start += width

    def spec(number, width):
        return pl.BlockSpec((rows, width), lambda step, index_ref: (0, index_ref[number]))

    total = sum(widths)
    return pl.pallas_call(
        kernel,
        out_shape=jax.ShapeDtypeStruct((rows, total), picks[0][0].dtype),
        grid_spec=pltpu.PrefetchScalarGridSpec(
            num_scalar_prefetch=1,
            grid=(1,),
            in_specs=[spec(number, width) for number, width in enumerate(widths)],
            out_specs=pl.BlockSpec((rows, total), lambda step, index_ref: (0, 0)),
        ),
        cost_estimate=pl.CostEstimate(
            flops=0, bytes_accessed=4 * rows * total, transcendentals=0
        ),
        name="pick_columns",
    )(jnp.stack([index for _, index, _ in picks]).astype(jnp.int32), *[p[0] for p in picks])


def place_columns(pieces, widths, ctx_index):
    count = lax.axis_size("ctx")
    rows = pieces[0][2].shape[0]
    starts = [sum(widths[:number]) for number in range(len(widths))]
    if any(width % 128 for width in widths):
        placed = []
        for start, width in zip(starts, widths):
            result = jnp.zeros((rows, count * width), F32)
            for odd, row, array in pieces:
                result = lax.dynamic_update_slice(
                    result,
                    array[:, start : start + width].astype(F32),
                    (row % rows, (ctx_index ^ (row // rows * 2 + odd)) * width),
                )
            placed.append(result)
        return placed
    plan = piece_plan(pieces)

    def kernel(index_ref, *refs):
        step = pl.program_id(0)
        out_refs = refs[len(plan) : len(plan) + len(widths)]
        buffers, sems = refs[-3:-1], refs[-1]
        fetch_pieces(step, refs[: len(plan)], plan, buffers, sems, rows)
        here = pl.ds(pl.multiple_of(step * rows, rows), rows)
        for parity in range(2):

            @pl.when(index_ref[0] == parity)
            def _():
                sides = (buffers[1], buffers[0]) if parity else buffers
                for out_ref, start, width in zip(out_refs, starts, widths):
                    for side, ref in enumerate(sides):
                        out_ref[:, side * width : (side + 1) * width] = ref[
                            here, start : start + width
                        ].astype(F32)

    index = [ctx_index % 2] + [(ctx_index ^ number) // 2 for number in range(0, count, 2)]
    return pl.pallas_call(
        kernel,
        out_shape=[jax.ShapeDtypeStruct((rows, count * width), F32) for width in widths],
        grid_spec=pltpu.PrefetchScalarGridSpec(
            num_scalar_prefetch=1,
            grid=(count // 2,),
            in_specs=in_place(pieces),
            out_specs=[
                pl.BlockSpec((rows, 2 * width), lambda step, index_ref: (0, index_ref[step + 1]))
                for width in widths
            ],
            scratch_shapes=piece_scratch(pieces, rows * count // 2, sum(widths)),
        ),
        cost_estimate=pl.CostEstimate(
            flops=0, bytes_accessed=6 * count * rows * sum(widths), transcendentals=0
        ),
        name="place_columns",
    )(jnp.stack(index).astype(jnp.int32), *piece_arrays(pieces))


def own_kernel(index_ref, hidden_ref, cot_ref, both_ref):
    width = hidden_ref.shape[1]
    count = index_ref.shape[0]
    size = width // count
    for number in range(count):
        source = pl.ds(pl.multiple_of(index_ref[number] * size, size), size)
        target = slice(number * size, (number + 1) * size)
        both_ref[:, target] = hidden_ref[:, source]
        both_ref[:, width + target.start : width + target.stop] = cot_ref[:, source]


def gains_kernel(index_ref, attn_ref, mlp_ref, query_ref, key_ref, out_ref):
    width = attn_ref.shape[1]
    head = query_ref.shape[1]
    count = index_ref.shape[0]
    size = width // count
    for start, ref in ((0, attn_ref), (width, mlp_ref)):
        for number in range(count):
            source = pl.ds(pl.multiple_of(index_ref[number] * size, size), size)
            out_ref[:, start + number * size : start + (number + 1) * size] = ref[:, source]
    out_ref[:, 2 * width : 2 * width + head] = query_ref[...]
    out_ref[:, 2 * width + head :] = key_ref[...]


def join_gains(attn, mlp, query, key, indices):
    columns = 2 * attn.shape[1] + 2 * query.shape[1]
    return pl.pallas_call(
        gains_kernel,
        out_shape=jax.ShapeDtypeStruct((1, columns), F32),
        in_specs=[pl.BlockSpec(memory_space=pltpu.SMEM)]
        + [pl.BlockSpec(memory_space=pltpu.VMEM)] * 4,
        out_specs=pl.BlockSpec(memory_space=pltpu.VMEM),
        cost_estimate=pl.CostEstimate(flops=0, bytes_accessed=8 * columns, transcendentals=0),
        name="join_gains",
    )(indices, attn, mlp, query, key)


def own_blocks(hidden, cot, indices):
    rows, width = hidden.shape
    return pl.pallas_call(
        own_kernel,
        out_shape=jax.ShapeDtypeStruct((rows, 2 * width), BF16),
        in_specs=[pl.BlockSpec(memory_space=pltpu.SMEM)]
        + [pl.BlockSpec(memory_space=pltpu.VMEM)] * 2,
        out_specs=pl.BlockSpec(memory_space=pltpu.VMEM),
        cost_estimate=pl.CostEstimate(
            flops=0, bytes_accessed=8 * rows * width, transcendentals=0
        ),
        name="own_blocks",
    )(indices, hidden, cot)


def here_rows(buffers, step, rows):
    here = pl.ds(pl.multiple_of(step * rows, rows), rows)
    return jnp.concatenate([buffers[0][here, :], buffers[1][here, :]], axis=0)


def mlp_kernel(plan, chunks, *refs):
    pieces, refs = refs[: len(plan)], refs[len(plan) :]
    c_ref, w_refs, refs = refs[0], refs[1 : 1 + chunks], refs[1 + chunks :]
    right_ref, act_ref, even_ref, odd_ref, x_all = refs[:5]
    buffers, sems = refs[5:7], refs[7]
    step = pl.program_id(0)
    hidden = act_ref.shape[1]
    rows = even_ref.shape[0]
    size = even_ref.shape[1] // chunks
    fetch_pieces(step, pieces, plan, buffers, sems, rows)
    x = here_rows(buffers, step, rows)
    x_all[...] = x
    c = c_ref[...]
    both = jnp.zeros((2 * rows, 2 * hidden), F32)
    grad = jnp.zeros((2 * rows, hidden), F32)
    for number, w_ref in enumerate(w_refs):
        side = slice(number * size, (number + 1) * size)
        both += jnp.dot(x[:, side], w_ref[:, : 2 * hidden], preferred_element_type=F32)
        grad += jnp.dot(c[:, side], w_ref[:, 2 * hidden :], preferred_element_type=F32)
    gate = both[:, :hidden]
    upper = both[:, hidden:]
    sigma = jax.nn.sigmoid(gate)
    gate_sigma = gate * sigma
    act_ref[...] = (gate_sigma * upper).astype(BF16)
    right_ref[:, :hidden] = (grad * upper * sigma * (1.0 + gate * (1.0 - sigma))).astype(BF16)
    right_ref[:, hidden:] = (grad * gate_sigma).astype(BF16)
    right = right_ref[...]
    for number, w_ref in enumerate(w_refs):
        part = nt(right, w_ref[:, : 2 * hidden]).astype(BF16)
        even_ref[:, number * size : (number + 1) * size] = part[:rows]
        odd_ref[:, number * size : (number + 1) * size] = part[rows:]


def mlp_both(pieces, both_all, weights, count):
    total, width = both_all.shape
    width //= 2
    rows = total // count
    hidden = weights[0].shape[1] // 3
    block = pl.BlockSpec((rows, width), lambda step: (step, 0))

    def wide(columns):
        return pl.BlockSpec((2 * rows, columns), lambda step: (step, 0))

    return pl.pallas_call(
        functools.partial(mlp_kernel, piece_plan(pieces), len(weights)),
        out_shape=[
            jax.ShapeDtypeStruct((total, 2 * hidden), BF16),
            jax.ShapeDtypeStruct((total, hidden), BF16),
            jax.ShapeDtypeStruct((total // 2, width), BF16),
            jax.ShapeDtypeStruct((total // 2, width), BF16),
            jax.ShapeDtypeStruct((total, width), BF16),
        ],
        grid=(count // 2,),
        in_specs=in_place(pieces)
        + [pl.BlockSpec((2 * rows, width), lambda step: (step, 1))]
        + [whole(part) for part in weights],
        out_specs=[wide(2 * hidden), wide(hidden), block, block, wide(width)],
        scratch_shapes=piece_scratch(pieces, total // 2, width),
        cost_estimate=pl.CostEstimate(
            flops=10 * total * width * hidden,
            bytes_accessed=12 * total * width,
            transcendentals=total * hidden,
        ),
        name="mlp_both",
    )(*piece_arrays(pieces), both_all, *weights)


def grads_kernel(left_one, right_one, left_two, right_two, *out_refs):
    split = right_one.shape[1]
    for number, out_ref in enumerate(out_refs):

        @pl.when(pl.program_id(0) == number)
        def _():
            out_ref[:, :split] = transposed_times(left_one[...], right_one[...]).astype(BF16)
            out_ref[:, split:] = transposed_times(left_two[...], right_two[...]).astype(BF16)


def weight_grads(numbers, left_one, right_one, left_two, right_two, skipped=0):
    first, chunks = numbers[0], len(numbers)
    total, width = left_one.shape
    size = width // lax.axis_size("fsdp")
    columns = right_one.shape[1] + right_two.shape[1]
    block = pl.BlockSpec((total, size), lambda step: (0, first + step))
    return pl.pallas_call(
        grads_kernel,
        out_shape=[jax.ShapeDtypeStruct((size, columns), BF16)] * chunks,
        grid=(chunks,),
        in_specs=[
            block,
            whole(right_one),
            pl.BlockSpec((total, size), lambda step: (0, skipped + first + step)),
            whole(right_two),
        ],
        out_specs=[pl.BlockSpec((size, columns), lambda step: (0, 0))] * chunks,
        cost_estimate=pl.CostEstimate(
            flops=2 * total * size * chunks * columns,
            bytes_accessed=4 * total * (size * chunks + columns),
            transcendentals=0,
        ),
        name="weight_grads",
    )(left_one, right_one, left_two, right_two)


def rotated(values, cosine, sine_part):
    return values * cosine + pltpu.roll(values, values.shape[1] // 2, 1) * sine_part


def head_scale(raw):
    return lax.rsqrt(jnp.mean(raw * raw, axis=-1, keepdims=True) + NORM_EPS)


def head_back(grad, raw, gain_row, cosine, sine_part):
    turned = grad * cosine + pltpu.roll(grad * sine_part, grad.shape[1] // 2, 1)
    scale = head_scale(raw)
    scaled = turned * gain_row
    mean_part = jnp.mean(scaled * raw, axis=-1, keepdims=True)
    return scale * scaled - raw * (scale * scale * scale * mean_part), turned * raw * scale


def project_kernel(plan, chunks, *refs):
    pieces, refs = refs[: len(plan)], refs[len(plan) :]
    w_refs, refs = refs[:chunks], refs[chunks:]
    gain_ref, qgain_ref, kgain_ref, cos_ref, sin_ref = refs[:5]
    in_ref, raw_ref, q_ref, k_ref, v_ref, both_ref = refs[5:11]
    buffers, sems = refs[11:13], refs[13]
    step = pl.program_id(0)
    head = qgain_ref.shape[1]
    q_width = q_ref.shape[1]
    kv_width = k_ref.shape[1]
    width = in_ref.shape[1]
    size = width // chunks
    rows = in_ref.shape[0] // 2
    fetch_pieces(step, pieces, plan, buffers, sems, rows)
    both = here_rows(buffers, step, rows)
    both_ref[...] = both
    normed = rms_norm(both[:, :width].astype(F32), gain_ref[...]).astype(BF16)
    in_ref[...] = normed
    raw = jnp.zeros((2 * rows, q_width + 2 * kv_width), F32)
    for number, w_ref in enumerate(w_refs):
        raw += jnp.dot(
            normed[:, number * size : (number + 1) * size],
            w_ref[...],
            preferred_element_type=F32,
        )
    raw_ref[...] = raw[:, : q_width + kv_width]
    cosine = cos_ref[...]
    sine_part = sin_ref[...]
    for column in range(0, q_width, head):
        part = raw[:, column : column + head]
        q_ref[:, column : column + head] = rotated(
            part * head_scale(part) * qgain_ref[...], cosine, sine_part
        ).astype(BF16)
    for column in range(0, kv_width, head):
        part = raw[:, q_width + column : q_width + column + head]
        k_ref[:, column : column + head] = rotated(
            part * head_scale(part) * kgain_ref[...], cosine, sine_part
        ).astype(BF16)
    v_ref[...] = raw[:, q_width + kv_width :].astype(BF16)


def project(pieces, weights, gain, q_gain, k_gain, cosine, sine_part, q_width, kv_width):
    width = gain.shape[1]
    head = q_gain.shape[1]
    total = cosine.shape[0]
    steps = lax.axis_size("ctx") // 2
    rows = total // (2 * steps)

    def wide(columns):
        return pl.BlockSpec((2 * rows, columns), lambda step: (step, 0))

    first_columns = pl.BlockSpec(
        (weights[0].shape[0], q_width + 2 * kv_width), lambda step: (0, 0)
    )
    return pl.pallas_call(
        functools.partial(project_kernel, piece_plan(pieces), len(weights)),
        out_shape=[
            jax.ShapeDtypeStruct((total, width), BF16),
            jax.ShapeDtypeStruct((total, q_width + kv_width), F32),
            jax.ShapeDtypeStruct((total, q_width), BF16),
            jax.ShapeDtypeStruct((total, kv_width), BF16),
            jax.ShapeDtypeStruct((total, kv_width), BF16),
            jax.ShapeDtypeStruct((total, 2 * width), BF16),
        ],
        grid=(steps,),
        in_specs=in_place(pieces)
        + [first_columns] * len(weights)
        + [whole(gain), whole(q_gain), whole(k_gain), wide(head), wide(head)],
        out_specs=[
            wide(width), wide(q_width + kv_width), wide(q_width), wide(kv_width), wide(kv_width),
            wide(2 * width),
        ],
        scratch_shapes=piece_scratch(pieces, total // 2, 2 * width),
        cost_estimate=pl.CostEstimate(
            flops=2 * total * width * (q_width + 2 * kv_width),
            bytes_accessed=12 * total * width,
            transcendentals=total,
        ),
        name="project",
    )(*piece_arrays(pieces), *weights, gain, q_gain, k_gain, cosine, sine_part)


def nt(lhs, rhs):
    return lax.dot_general(lhs, rhs, (((1,), (1,)), ((), ())), preferred_element_type=F32)


def attend_kernel(chunks, q_ref, k_ref, v_ref, row_ref, col_ref, *refs):
    w_refs, refs = refs[:chunks], refs[chunks:]
    mix_ref, lse_ref, even_ref, odd_ref, vt_ref = refs
    kv_width = k_ref.shape[1]
    q_width = q_ref.shape[1]
    head = q_width // lse_ref.shape[0]
    group = q_width // kv_width
    scale = 1.0 / math.sqrt(head)

    @pl.when(pl.program_id(0) == 0)
    def _():
        vt_ref[...] = v_ref[...].astype(F32).T.astype(BF16)

    allowed = col_ref[...] <= row_ref[...]
    for number in range(q_width // head):
        kv = number // group * head
        column = number * head
        scores = jnp.where(
            allowed, nt(k_ref[:, kv : kv + head], q_ref[:, column : column + head]) * scale, MASKED
        )
        top = jnp.max(scores, axis=0, keepdims=True)
        raised = jnp.exp(scores - top)
        total = jnp.sum(raised, axis=0, keepdims=True)
        lse_ref[number : number + 1, :] = top + jnp.log(total)
        probs = (raised * (1.0 / total)).astype(BF16)
        mixed = jnp.dot(vt_ref[kv : kv + head, :], probs, preferred_element_type=F32)
        mix_ref[:, column : column + head] = mixed.T.astype(BF16)
    rows = even_ref.shape[0]
    size = even_ref.shape[1] // chunks
    mix = mix_ref[...]
    for number, w_ref in enumerate(w_refs):
        out = nt(mix, w_ref[...]).astype(BF16)
        even_ref[:, number * size : (number + 1) * size] = out[:rows]
        odd_ref[:, number * size : (number + 1) * size] = out[rows:]


def attend(q, k, v, pos_row, pos_col, weights, head):
    total, q_width = q.shape
    kv_width = k.shape[1]
    width = weights[0].shape[0] * len(weights)
    steps = lax.axis_size("ctx") // 2
    rows = total // (2 * steps)
    heads = q_width // head
    last_columns = pl.BlockSpec(
        (weights[0].shape[0], q_width), lambda step: (0, weights[0].shape[1] // q_width - 1)
    )

    def wide(columns):
        return pl.BlockSpec((2 * rows, columns), lambda step: (step, 0))

    half = pl.BlockSpec((rows, width), lambda step: (step, 0))
    return pl.pallas_call(
        functools.partial(attend_kernel, len(weights)),
        out_shape=[
            jax.ShapeDtypeStruct((total, q_width), BF16),
            jax.ShapeDtypeStruct((heads, total), F32),
            jax.ShapeDtypeStruct((total // 2, width), BF16),
            jax.ShapeDtypeStruct((total // 2, width), BF16),
        ],
        grid=(steps,),
        in_specs=[
            wide(q_width), whole(k), whole(v),
            pl.BlockSpec((1, 2 * rows), lambda step: (0, step)),
            whole(pos_col),
        ]
        + [last_columns] * len(weights),
        out_specs=[
            wide(q_width), pl.BlockSpec((heads, 2 * rows), lambda step: (0, step)), half, half,
        ],
        scratch_shapes=[pltpu.VMEM((kv_width, total), BF16)],
        cost_estimate=pl.CostEstimate(
            flops=4 * total * total * q_width,
            bytes_accessed=8 * total * width,
            transcendentals=total * total * heads,
        ),
        name="attend",
    )(q, k, v, pos_row, pos_col, *weights)


def attend_back_kernel(plan, chunks, *refs):
    pieces, refs = refs[: len(plan)], refs[len(plan) :]
    w_refs, refs = refs[:chunks], refs[chunks:]
    q_ref, k_ref, v_ref, row_ref, col_ref, mix_ref, lse_ref = refs[:7]
    raw_ref, qgain_ref, cos_ref, sin_ref = refs[7:11]
    low_ref, dk_ref, dv_ref, dgain_ref, all_ref = refs[11:16]
    buffers, sems, kt_ref = refs[16:18], refs[18], refs[19]
    step = pl.program_id(0)
    head = qgain_ref.shape[1]
    kv_width = k_ref.shape[1]
    q_width = q_ref.shape[1]
    group = q_width // kv_width
    scale = 1.0 / math.sqrt(head)
    rows = q_ref.shape[0] // 2
    size = all_ref.shape[1] // chunks

    @pl.when(pl.program_id(0) == 0)
    def _():
        kt_ref[...] = k_ref[...].astype(F32).T.astype(BF16)
        dk_ref[...] = jnp.zeros_like(dk_ref)
        dv_ref[...] = jnp.zeros_like(dv_ref)
        dgain_ref[...] = jnp.zeros_like(dgain_ref)

    fetch_pieces(step, pieces, plan, buffers, sems, rows)
    grad = here_rows(buffers, step, rows)
    all_ref[...] = grad
    dmix_all = jnp.zeros((2 * rows, q_width), F32)
    for number, w_ref in enumerate(w_refs):
        dmix_all += jnp.dot(
            grad[:, number * size : (number + 1) * size],
            w_ref[...],
            preferred_element_type=F32,
        )
    dmix_all = dmix_all.astype(BF16)
    allowed = col_ref[...] <= row_ref[...]
    for number in range(q_width // head):
        kv = number // group * head
        column = number * head
        q = q_ref[:, column : column + head]
        dmix = dmix_all[:, column : column + head]
        mix = mix_ref[:, column : column + head]
        delta = jnp.sum((dmix.astype(F32) * mix.astype(F32)).T, axis=0, keepdims=True)
        scores = nt(k_ref[:, kv : kv + head], q) * scale
        probs = jnp.exp(jnp.where(allowed, scores - lse_ref[number : number + 1, :], MASKED))
        dv_ref[:, kv : kv + head] += jnp.dot(
            probs.astype(BF16), dmix, preferred_element_type=F32
        )
        prob_grad = nt(v_ref[:, kv : kv + head], dmix)
        score_grad = (probs * (prob_grad - delta) * scale).astype(BF16)
        dk_ref[:, kv : kv + head] += jnp.dot(score_grad, q, preferred_element_type=F32)
        dq = jnp.dot(kt_ref[kv : kv + head, :], score_grad, preferred_element_type=F32).T
        raw_grad, gain_part = head_back(
            dq, raw_ref[:, column : column + head], qgain_ref[...], cos_ref[...], sin_ref[...]
        )
        low_ref[:, column : column + head] = raw_grad.astype(BF16)
        dgain_ref[...] += jnp.sum(gain_part, axis=0, keepdims=True)


def attend_back(pieces, weights, q, k, v, pos_row, pos_col, mix, lse, raw, q_gain, cosine, sine_part):
    total, q_width = q.shape
    kv_width = k.shape[1]
    width = weights[0].shape[0] * len(weights)
    steps = lax.axis_size("ctx") // 2
    rows = total // (2 * steps)
    heads = lse.shape[0]
    last_columns = pl.BlockSpec(
        (weights[0].shape[0], q_width), lambda step: (0, weights[0].shape[1] // q_width - 1)
    )
    head = q_gain.shape[1]

    def wide(columns):
        return pl.BlockSpec((2 * rows, columns), lambda step: (step, 0))

    def fixed(shape):
        return pl.BlockSpec(shape, lambda step: (0, 0))

    return pl.pallas_call(
        functools.partial(attend_back_kernel, piece_plan(pieces), len(weights)),
        out_shape=[
            jax.ShapeDtypeStruct((total, q_width), BF16),
            jax.ShapeDtypeStruct((total, kv_width), F32),
            jax.ShapeDtypeStruct((total, kv_width), F32),
            jax.ShapeDtypeStruct((1, head), F32),
            jax.ShapeDtypeStruct((total, width), BF16),
        ],
        grid=(steps,),
        in_specs=in_place(pieces)
        + [last_columns] * len(weights)
        + [
            wide(q_width), whole(k), whole(v),
            pl.BlockSpec((1, 2 * rows), lambda step: (0, step)),
            whole(pos_col), wide(q_width),
            pl.BlockSpec((heads, 2 * rows), lambda step: (0, step)),
            wide(q_width), whole(q_gain), wide(head), wide(head),
        ],
        out_specs=[
            wide(q_width), fixed((total, kv_width)), fixed((total, kv_width)), fixed((1, head)),
            wide(width),
        ],
        scratch_shapes=piece_scratch(pieces, total // 2, width)
        + [pltpu.VMEM((kv_width, total), BF16)],
        cost_estimate=pl.CostEstimate(
            flops=10 * total * total * q_width,
            bytes_accessed=8 * total * width,
            transcendentals=total * total * heads,
        ),
        name="attend_back",
    )(
        *piece_arrays(pieces), *weights,
        q, k, v, pos_row, pos_col, mix, lse, raw, q_gain, cosine, sine_part,
    )


def project_back_kernel(
    chunks, low_ref, dk_ref, dv_ref, raw_ref, kgain_ref, cos_ref, sin_ref, x_ref, act_ref, *refs
):
    w_refs, d_refs, refs = refs[:chunks], refs[chunks : 2 * chunks], refs[2 * chunks :]
    right_ref, even_ref, odd_ref, again_ref, dgain_ref = refs
    head = kgain_ref.shape[1]
    kv_width = dk_ref.shape[1]
    q_width = low_ref.shape[1]
    rows = even_ref.shape[0]
    width = x_ref.shape[1]
    size = width // chunks

    @pl.when(pl.program_id(0) == 0)
    def _():
        again_ref[...] = jnp.zeros_like(again_ref)
        dgain_ref[...] = jnp.zeros_like(dgain_ref)

    right_ref[:, :q_width] = low_ref[...]
    for column in range(0, kv_width, head):
        raw_grad, gain_part = head_back(
            dk_ref[:, column : column + head],
            raw_ref[:, q_width + column : q_width + column + head],
            kgain_ref[...],
            cos_ref[...],
            sin_ref[...],
        )
        right_ref[:, q_width + column : q_width + column + head] = raw_grad.astype(BF16)
        dgain_ref[...] += jnp.sum(gain_part, axis=0, keepdims=True)
    right_ref[:, q_width + kv_width :] = dv_ref[...].astype(BF16)
    right = right_ref[...]
    x = x_ref[...].astype(F32)
    normed = x * head_scale(x)
    for number, w_ref in enumerate(w_refs):
        side = slice(number * size, (number + 1) * size)
        part = nt(right, w_ref[...])
        again_ref[:, side] += jnp.sum(part * normed[:, side], axis=0, keepdims=True)
        part = part.astype(BF16)
        even_ref[:, side] = part[:rows]
        odd_ref[:, side] = part[rows:]
    act = act_ref[...]
    for number, d_ref in enumerate(d_refs):
        side = slice(width + number * size, width + (number + 1) * size)
        part = nt(act, d_ref[:, d_ref.shape[1] - act.shape[1] :]).astype(BF16)
        even_ref[:, side] = part[:rows]
        odd_ref[:, side] = part[rows:]


def project_back(low, dk, dv, raw, k_gain, cosine, sine_part, both_all, weights, act, mlp_parts):
    total, q_width = low.shape
    kv_width = dk.shape[1]
    width = both_all.shape[1] // 2
    steps = lax.axis_size("ctx") // 2
    rows = total // (2 * steps)
    head = k_gain.shape[1]

    def wide(columns):
        return pl.BlockSpec((2 * rows, columns), lambda step: (step, 0))

    def fixed(shape):
        return pl.BlockSpec(shape, lambda step: (0, 0))

    first_columns = pl.BlockSpec(
        (weights[0].shape[0], q_width + 2 * kv_width), lambda step: (0, 0)
    )
    hidden = act.shape[1]
    if hidden % 128:
        down_columns = whole(mlp_parts[0])
    else:
        down_columns = pl.BlockSpec((mlp_parts[0].shape[0], hidden), lambda step: (0, 2))
    both = pl.BlockSpec((rows, 2 * width), lambda step: (step, 0))
    return pl.pallas_call(
        functools.partial(project_back_kernel, len(weights)),
        out_shape=[
            jax.ShapeDtypeStruct((total, q_width + 2 * kv_width), BF16),
            jax.ShapeDtypeStruct((total // 2, 2 * width), BF16),
            jax.ShapeDtypeStruct((total // 2, 2 * width), BF16),
            jax.ShapeDtypeStruct((1, width), F32),
            jax.ShapeDtypeStruct((1, head), F32),
        ],
        grid=(steps,),
        in_specs=[
            wide(q_width), wide(kv_width), wide(kv_width), wide(q_width + kv_width),
            whole(k_gain), wide(head), wide(head), wide(width), wide(hidden),
        ]
        + [first_columns] * len(weights)
        + [down_columns] * len(weights),
        out_specs=[
            wide(q_width + 2 * kv_width), both, both, fixed((1, width)), fixed((1, head)),
        ],
        cost_estimate=pl.CostEstimate(
            flops=2 * total * width * (q_width + 2 * kv_width),
            bytes_accessed=12 * total * width,
            transcendentals=total,
        ),
        name="project_back",
    )(low, dk, dv, raw, k_gain, cosine, sine_part, both_all, act, *weights, *mlp_parts)


def on_device_all(
    hidden_in,
    pair_table,
    attn_gain,
    query_proj,
    key_proj,
    value_proj,
    query_gain,
    key_gain,
    output_proj,
    mlp_gain,
    gate_proj,
    up_proj,
    down_proj,
    cotangent,
):
    fsdp_count = lax.axis_size("fsdp")
    fsdp_index = lax.axis_index("fsdp")
    ctx_count = lax.axis_size("ctx")
    ctx_index = lax.axis_index("ctx")
    row_count, width = hidden_in.shape[1:]
    block_len = row_count // 2
    total_rows = ctx_count * row_count
    shard_rows = width // fsdp_count
    head_width = query_gain.shape[0]
    half_head = head_width // 2
    kvhead_total = key_proj.shape[1] // head_width
    kv_count = max(1, kvhead_total // ctx_count)
    kv_share = max(1, ctx_count // kvhead_total)
    query_width = query_proj.shape[1] // ctx_count
    kv_width = kv_count * head_width
    kv_own = key_proj.shape[1] // ctx_count
    hidden_width = gate_proj.shape[1] // ctx_count

    fsdp_order = fsdp_index ^ jnp.arange(fsdp_count, dtype=jnp.int32)

    def block_order(values):
        return jnp.concatenate(
            [
                lax.dynamic_slice_in_dim(
                    values, (fsdp_index ^ number) * shard_rows, shard_rows, axis=values.ndim - 1
                )
                for number in range(fsdp_count)
            ],
            axis=-1,
        )

    def columns(weights, start, size):
        return lax.dynamic_slice_in_dim(weights, start, size, axis=1)

    kv_index = ctx_index // kv_share
    both_own = own_blocks(hidden_in[0], cotangent[0], fsdp_order)
    inputs = both_own[:, :width]
    cot_low = both_own[:, width:]
    gains_rel = block_order(jnp.stack([attn_gain, mlp_gain]))
    attn_gain_rel = gains_rel[0]
    mlp_gain_rel = gains_rel[1]
    fsdp_levels = (fsdp_count - 1).bit_length()
    attn_width = query_width + 2 * kv_width

    both_pieces = gather_ctx(both_own)
    first_shard = pick_columns(
        [
            (query_proj, ctx_index, query_width),
            (key_proj, kv_index, kv_width),
            (value_proj, kv_index, kv_width),
            (output_proj, ctx_index, query_width),
        ]
    )
    first_blocks = {0: first_shard}
    for level in range(1, fsdp_levels + 1):
        first_blocks = gather_fsdp_step(first_blocks, fsdp_count, level)
    first_parts = [first_blocks[number] for number in range(fsdp_count)]
    mlp_shard = pick_columns(
        [(weights, ctx_index, hidden_width) for weights in (gate_proj, up_proj, down_proj)]
    )
    mlp_blocks = gather_fsdp_step({0: mlp_shard}, fsdp_count, 1)

    owner_ids = ctx_index ^ jnp.arange(ctx_count, dtype=jnp.int32)
    picked = owner_ids[:, None] == jnp.arange(ctx_count, dtype=jnp.int32)[None, :]
    block_ids = jnp.sum(jnp.where(picked[:, :, None], pair_table[None], 0), axis=1)
    positions = (
        block_ids[:, :, None] * block_len + jnp.arange(block_len, dtype=jnp.int32)
    ).reshape(total_rows)
    pos_row = positions.reshape(1, total_rows)
    pos_col = positions.reshape(total_rows, 1)
    lanes = jnp.arange(head_width, dtype=jnp.int32)
    frequency = ROPE_BASE ** (-((lanes % half_head).astype(F32) * 2.0 / head_width))
    angles = positions.astype(F32)[:, None] * frequency[None, :]
    cosine = jnp.cos(angles)
    sine_part = jnp.sin(angles) * jnp.where(lanes < half_head, -1.0, 1.0)[None, :]

    query_row = query_gain.reshape(1, head_width)
    key_row = key_gain.reshape(1, head_width)
    attn_in, attn_raw, query_heads, key_heads, value_heads, both_all = project(
        both_pieces, first_parts, attn_gain_rel.reshape(1, width), query_row, key_row,
        cosine, sine_part, query_width, kv_width,
    )
    attn_mix, log_total, mix_even, mix_odd = attend(
        query_heads, key_heads, value_heads, pos_row, pos_col, first_parts, head_width
    )

    resid_sum = scatter_ctx(mix_even, mix_odd)
    resid = inputs.astype(F32) + resid_sum
    mlp_in = rms_norm(resid, mlp_gain_rel).astype(BF16)
    for level in range(2, fsdp_levels + 1):
        mlp_blocks = gather_fsdp_step(mlp_blocks, fsdp_count, level)
    mlp_parts = [mlp_blocks[number] for number in range(fsdp_count)]
    mlp_pieces = gather_ctx(mlp_in)
    mlp_right, hidden_act, part_even, part_odd, mlp_all = mlp_both(
        mlp_pieces, both_all, mlp_parts, ctx_count
    )
    mlp_in_grad = scatter_ctx(part_even, part_odd)
    last = fsdp_count - 1

    def all_grads(*operands):
        sums = {last: weight_grads([last], *operands)[0]}
        if last:
            numbers = list(range(last))
            sums.update(zip(numbers, weight_grads(numbers, *operands)))
        return sums

    mlp_sums = all_grads(mlp_all, mlp_right, both_all, hidden_act, fsdp_count)
    resid_part, mlp_gain_grad = jax.vjp(rms_norm, resid, mlp_gain_rel)[1](mlp_in_grad)
    resid_grad = cot_low.astype(F32) + resid_part
    resid_low = resid_grad.astype(BF16)
    for level in range(fsdp_levels, 1, -1):
        mlp_sums = scatter_fsdp_step(mlp_sums, fsdp_count, level)
    resid_pieces = gather_ctx(resid_low)
    mlp_moved = {
        number: exchange(mlp_sums[number].astype(BF16), number, "fsdp")
        for number in range(1, fsdp_count)
        if level_of(number) == 1
    }
    query_low, key_grad, value_grad, query_gain_grad, resid_all = attend_back(
        resid_pieces, first_parts, query_heads, key_heads, value_heads, pos_row, pos_col,
        attn_mix, log_total, attn_raw, query_row, cosine, sine_part,
    )
    bit = 1
    while bit < kv_share:
        moved = exchange(jnp.concatenate([key_grad, value_grad], axis=1), bit, "ctx")
        moved = moved.reshape(ctx_count, row_count, 2 * kv_width)
        moved = jnp.concatenate([moved[number ^ bit] for number in range(ctx_count)], axis=0)
        key_grad = key_grad + moved[:, :kv_width]
        value_grad = value_grad + moved[:, kv_width:]
        bit *= 2
    own_parts = first_parts
    own_start = (ctx_index % kv_share) * kv_own
    if kv_share > 1:
        place = jnp.arange(attn_width) - query_width
        owned = (place < 0) | (
            (place % kv_width >= own_start) & (place % kv_width < own_start + kv_own)
        )
        own_parts = [
            jnp.where(owned[None, :], part[:, :attn_width], 0).astype(BF16)
            for part in first_parts
        ]
    attn_right, tail_even, tail_odd, attn_gain_grad, key_gain_grad = project_back(
        query_low, key_grad, value_grad, attn_raw, key_row, cosine, sine_part,
        both_all, own_parts, hidden_act, mlp_parts,
    )
    if kv_share > 1:
        attn_right = jnp.concatenate(
            [
                attn_right[:, :query_width],
                columns(attn_right, query_width + own_start, kv_own),
                columns(attn_right, query_width + kv_width + own_start, kv_own),
            ],
            axis=1,
        )
        key_gain_grad = jnp.where(ctx_index % kv_share == 0, key_gain_grad, 0.0)
    attn_sums = all_grads(attn_in, attn_right, resid_all, attn_mix)
    for level in range(fsdp_levels, 0, -1):
        attn_sums = scatter_fsdp_step(attn_sums, fsdp_count, level)
    attn_grads = attn_sums[0].astype(BF16)
    both_sums = scatter_ctx(tail_even, tail_odd)
    attn_in_grad = both_sums[:, :width]
    block_out = (resid + both_sums[:, width:]).astype(BF16)
    mlp_total = mlp_sums[0].astype(F32)
    for moved in mlp_moved.values():
        mlp_total = mlp_total + moved.astype(F32)
    mlp_grads = mlp_total.astype(BF16)
    own_wide = inputs.astype(F32)
    input_part = jax.vjp(lambda values: rms_norm(values, attn_gain_rel), own_wide)[1](
        attn_in_grad
    )[0]
    input_grad = resid_grad + input_part
    gains = join_gains(
        attn_gain_grad, mlp_gain_grad.reshape(1, width), query_gain_grad, key_gain_grad,
        fsdp_order,
    )
    gains = sum_all(gains)[0]
    outs = (
        block_order(block_out)[None],
        block_order(input_grad)[None],
        gains[:width],
        gains[2 * width : 2 * width + head_width],
        gains[2 * width + head_width :],
        gains[width : 2 * width],
    )
    mlp_pieces = gather_ctx(mlp_grads)
    mlp_outs = place_columns(mlp_pieces, (hidden_width,) * 3, ctx_index)
    attn_pieces = gather_ctx(attn_grads)
    last_piece, *outs = tie(attn_pieces[-1][2], *outs)
    attn_pieces[-1] = attn_pieces[-1][:2] + (last_piece,)
    attn_outs = place_columns(attn_pieces, (query_width, kv_own, kv_own, query_width), ctx_index)
    return (
        outs[0],
        outs[1],
        outs[2],
        attn_outs[0],
        attn_outs[1],
        attn_outs[2],
        outs[3],
        outs[4],
        attn_outs[3],
        outs[5],
        mlp_outs[0],
        mlp_outs[1],
        mlp_outs[2],
    )


def solution(mesh):
    in_specs = (
        P("fsdp", "ctx", None),
        P(),
        P(),
        P("fsdp", None),
        P("fsdp", None),
        P("fsdp", None),
        P(),
        P(),
        P("fsdp", None),
        P(),
        P("fsdp", None),
        P("fsdp", None),
        P("fsdp", None),
        P("fsdp", "ctx", None),
    )
    out_specs = (
        P("fsdp", "ctx", None),
        P("fsdp", "ctx", None),
        P(),
        P("fsdp", None),
        P("fsdp", None),
        P("fsdp", None),
        P(),
        P(),
        P("fsdp", None),
        P(),
        P("fsdp", None),
        P("fsdp", None),
        P("fsdp", None),
    )
    return jax.shard_map(
        on_device_all, mesh=mesh, in_specs=in_specs, out_specs=out_specs, check_vma=False
    )
```

```python
import functools
import math

import jax
import jax.numpy as jnp
from jax import lax
from jax.experimental import pallas as pl
from jax.experimental.pallas import tpu as pltpu
from jax.sharding import PartitionSpec as P


NORM_EPS = 1e-06
ROPE_BASE = 1000000.0
MASKED = -1e30
F32 = jnp.float32
BF16 = jnp.bfloat16
CTX = "ctx"
FSDP = "fsdp"


def rms_norm(values, gain_vec):
    return (
        values * lax.rsqrt(jnp.mean(values * values, axis=-1, keepdims=True) + NORM_EPS) * gain_vec
    )


def transposed_times(lhs_mat, rhs_mat):
    return lax.dot_general(
        lhs_mat, rhs_mat, (((0,), (0,)), ((), ())), preferred_element_type=F32
    )


def tie(*values):
    return lax.optimization_barrier(values)


def exchange(value, bit, axis):
    count = lax.axis_size(axis)
    return lax.ppermute(value, axis, [(index, index ^ bit) for index in range(count)])


def low_bit(number):
    return number & -number


def top_bit(number):
    return 1 << (number.bit_length() - 1)


def level_of(number):
    return bin(number).count("1")


def even_numbers(count, level):
    return [number for number in range(0, count, 2) if level_of(number) == level]


def gather_levels(count):
    return (count // 2).bit_length() - 1


def gather_ctx(own):
    count = lax.axis_size(CTX)
    rows = own.shape[0]
    half = rows // 2
    parts = {0: [own]}
    for level in range(1, gather_levels(count) + 1):
        for number in even_numbers(count, level):
            low, top = low_bit(number), top_bit(number)
            if level == 1:
                parts[number] = [exchange(own, low, CTX)]
            else:
                parts[number] = [
                    exchange(rows_of(parts[number ^ top], 0, half), top, CTX),
                    exchange(rows_of(parts[number ^ low], half, rows), low, CTX),
                ]
    pieces = []
    for number in range(0, count, 2):
        start = number // 2 * rows
        for part in parts[number]:
            pieces.append((0, start, part))
            other = exchange(part, 1, CTX)
            pieces.append((1, start, other))
            start += part.shape[0]
    return pieces


def rows_of(parts, start, stop):
    if len(parts) > 1:
        return parts[0 if start == 0 else 1]
    return parts[0][start:stop]


def fetch_pieces(step, refs, plan, buffers, sems, block_rows, columns=None):
    copies = []
    for number, (ref, (odd, start, rows)) in enumerate(zip(refs, plan)):
        source = ref if columns is None else ref.at[:, columns]
        copies.append(
            (
                start // block_rows,
                pltpu.make_async_copy(
                    source, buffers[odd].at[pl.ds(start, rows), :], sems.at[number]
                ),
            )
        )

    @pl.when(step == 0)
    def _():
        for _, copy in copies:
            copy.start()

    for block in range(buffers[0].shape[0] // block_rows):

        @pl.when(step == block)
        def _():
            for owner, copy in copies:
                if owner == block:
                    copy.wait()


def piece_plan(pieces):
    return [(odd, start, array.shape[0]) for odd, start, array in pieces]


def piece_arrays(pieces):
    return [array for _, _, array in pieces]


def piece_scratch(pieces, rows, width):
    return [
        pltpu.VMEM((rows, width), BF16),
        pltpu.VMEM((rows, width), BF16),
        pltpu.SemaphoreType.DMA((len(pieces),)),
    ]


def in_place(pieces):
    return [pl.BlockSpec(memory_space=pl.ANY)] * len(pieces)


def first_sums_kernel(even_ref, odd_ref, first_ref, second_ref):
    half = first_ref.shape[0]
    total = (even_ref[...].astype(F32) + odd_ref[...].astype(F32)).astype(BF16)
    first_ref[...] = total[:half]
    second_ref[...] = total[half:]


def next_sums_kernel(even_two, odd_two, even_four, odd_four, first, second, two_ref, four_ref):
    half = first.shape[0]
    two = even_two[...].astype(F32) + odd_two[...].astype(F32)
    two_ref[:half, :] = (two[:half] + first[...].astype(F32)).astype(BF16)
    two_ref[half:, :] = two[half:].astype(BF16)
    four = even_four[...].astype(F32) + odd_four[...].astype(F32)
    four_ref[:half, :] = four[:half].astype(BF16)
    four_ref[half:, :] = (four[half:] + second[...].astype(F32)).astype(BF16)


def scatter_eight(even, odd):
    moved = exchange(odd, 1, CTX)
    rows = even.shape[0] // 4
    half = rows // 2
    width = even.shape[1]

    def block(number):
        return pl.BlockSpec((rows, width), lambda step: (number, 0))

    part = pl.BlockSpec((half, width), lambda step: (0, 0))
    cost = pl.CostEstimate(flops=0, bytes_accessed=8 * rows * width, transcendentals=0)
    first, second = pl.pallas_call(
        first_sums_kernel,
        out_shape=[jax.ShapeDtypeStruct((half, width), BF16)] * 2,
        grid=(1,),
        in_specs=[block(3), block(3)],
        out_specs=[part, part],
        cost_estimate=cost,
    )(even, moved)
    first = exchange(first, 4, CTX)
    second = exchange(second, 2, CTX)
    two, four = pl.pallas_call(
        next_sums_kernel,
        out_shape=[jax.ShapeDtypeStruct((rows, width), BF16)] * 2,
        grid=(1,),
        in_specs=[block(1), block(1), block(2), block(2), part, part],
        out_specs=[block(0), block(0)],
        cost_estimate=cost,
    )(even, moved, even, moved, first, second)
    two = exchange(two, 2, CTX)
    four = exchange(four, 4, CTX)
    return (
        (even[:rows].astype(F32) + moved[:rows].astype(F32))
        + two.astype(F32)
        + four.astype(F32)
    )


def scatter_ctx(even, odd, local_kernels=False):
    count = lax.axis_size(CTX)
    if local_kernels and count == 8:
        return scatter_eight(even, odd)
    rows = even.shape[0] * 2 // count
    half = rows // 2
    moved = exchange(odd, 1, CTX)

    def piece(number, start, stop):
        base = number // 2 * rows
        return even[base + start : base + stop].astype(F32) + moved[
            base + start : base + stop
        ].astype(F32)

    halves = {
        number: [piece(number, 0, half), piece(number, half, rows)]
        for number in range(0, count, 2)
    }
    for level in range(gather_levels(count), 1, -1):
        for number in even_numbers(count, level):
            low, top = low_bit(number), top_bit(number)
            first, second = tie(*(part.astype(BF16) for part in halves[number]))
            halves[number ^ top][0] += exchange(first, top, CTX).astype(F32)
            halves[number ^ low][1] += exchange(second, low, CTX).astype(F32)
    total = jnp.concatenate(halves[0], axis=0)
    for number in even_numbers(count, 1):
        sent = jnp.concatenate(halves[number], axis=0).astype(BF16)
        total = total + exchange(sent, number, CTX).astype(F32)
    return total


def gather_fsdp_step(blocks, count, level):
    blocks = dict(blocks)
    for number in range(1, count):
        if level_of(number) == level:
            low = low_bit(number)
            blocks[number] = exchange(blocks[number ^ low], low, FSDP)
    return blocks


def scatter_fsdp_step(sums, count, level):
    sums = dict(sums)
    for number in range(1, count):
        if level_of(number) == level:
            low = low_bit(number)
            sums[number ^ low] = sums[number ^ low].astype(F32) + exchange(
                sums[number].astype(BF16), low, FSDP
            ).astype(F32)
    return sums


def sum_all(value):
    for axis in (CTX, FSDP):
        bit = 1
        while bit < lax.axis_size(axis):
            value = value + exchange(value, bit, axis)
            bit *= 2
    return value


def whole(array):
    return pl.BlockSpec(array.shape, lambda *ids: (0,) * len(array.shape))


def pick_columns(picks):
    rows = picks[0][0].shape[0]
    widths = [width for _, _, width in picks]
    if any(width % 128 for width in widths):
        return jnp.concatenate(
            [
                lax.dynamic_slice_in_dim(array, index * width, width, axis=1)
                for array, index, width in picks
            ],
            axis=1,
        )

    def kernel(index_ref, *refs):
        start = 0
        for ref, width in zip(refs, widths):
            refs[-1][:, start : start + width] = ref[...]
            start += width

    def spec(number, width):
        return pl.BlockSpec((rows, width), lambda step, index_ref: (0, index_ref[number]))

    total = sum(widths)
    return pl.pallas_call(
        kernel,
        out_shape=jax.ShapeDtypeStruct((rows, total), picks[0][0].dtype),
        grid_spec=pltpu.PrefetchScalarGridSpec(
            num_scalar_prefetch=1,
            grid=(1,),
            in_specs=[spec(number, width) for number, width in enumerate(widths)],
            out_specs=pl.BlockSpec((rows, total), lambda step, index_ref: (0, 0)),
        ),
        cost_estimate=pl.CostEstimate(
            flops=0, bytes_accessed=4 * rows * total, transcendentals=0
        ),
    )(jnp.stack([index for _, index, _ in picks]).astype(jnp.int32), *[p[0] for p in picks])


def place_columns(pieces, widths, ctx_index):
    count = lax.axis_size(CTX)
    rows = pieces[0][2].shape[0]
    starts = [sum(widths[:number]) for number in range(len(widths))]
    if any(width % 128 for width in widths):
        placed = []
        for start, width in zip(starts, widths):
            result = jnp.zeros((rows, count * width), F32)
            for odd, row, array in pieces:
                result = lax.dynamic_update_slice(
                    result,
                    array[:, start : start + width].astype(F32),
                    (row % rows, (ctx_index ^ (row // rows * 2 + odd)) * width),
                )
            placed.append(result)
        return placed
    plan = piece_plan(pieces)

    def kernel(index_ref, *refs):
        step = pl.program_id(0)
        out_refs = refs[len(plan) : len(plan) + len(widths)]
        buffers, sems = refs[-3:-1], refs[-1]
        fetch_pieces(step, refs[: len(plan)], plan, buffers, sems, rows)
        here = pl.ds(pl.multiple_of(step * rows, rows), rows)
        for parity in range(2):

            @pl.when(index_ref[0] == parity)
            def _():
                sides = (buffers[1], buffers[0]) if parity else buffers
                for out_ref, start, width in zip(out_refs, starts, widths):
                    for side, ref in enumerate(sides):
                        out_ref[:, side * width : (side + 1) * width] = ref[
                            here, start : start + width
                        ].astype(F32)

    index = [ctx_index % 2] + [(ctx_index ^ number) // 2 for number in range(0, count, 2)]
    return pl.pallas_call(
        kernel,
        out_shape=[jax.ShapeDtypeStruct((rows, count * width), F32) for width in widths],
        grid_spec=pltpu.PrefetchScalarGridSpec(
            num_scalar_prefetch=1,
            grid=(count // 2,),
            in_specs=in_place(pieces),
            out_specs=[
                pl.BlockSpec((rows, 2 * width), lambda step, index_ref: (0, index_ref[step + 1]))
                for width in widths
            ],
            scratch_shapes=piece_scratch(pieces, rows * count // 2, sum(widths)),
        ),
        cost_estimate=pl.CostEstimate(
            flops=0, bytes_accessed=6 * count * rows * sum(widths), transcendentals=0
        ),
    )(jnp.stack(index).astype(jnp.int32), *piece_arrays(pieces))


def own_kernel(index_ref, hidden_ref, cot_ref, both_ref):
    width = hidden_ref.shape[1]
    count = index_ref.shape[0]
    size = width // count
    for number in range(count):
        source = pl.ds(pl.multiple_of(index_ref[number] * size, size), size)
        target = slice(number * size, (number + 1) * size)
        both_ref[:, target] = hidden_ref[:, source]
        both_ref[:, width + target.start : width + target.stop] = cot_ref[:, source]


def gains_kernel(index_ref, attn_ref, mlp_ref, query_ref, key_ref, out_ref):
    width = attn_ref.shape[1]
    head = query_ref.shape[1]
    count = index_ref.shape[0]
    size = width // count
    for start, ref in ((0, attn_ref), (width, mlp_ref)):
        for number in range(count):
            source = pl.ds(pl.multiple_of(index_ref[number] * size, size), size)
            out_ref[:, start + number * size : start + (number + 1) * size] = ref[:, source]
    out_ref[:, 2 * width : 2 * width + head] = query_ref[...]
    out_ref[:, 2 * width + head :] = key_ref[...]


def join_gains(attn, mlp, query, key, indices):
    columns = 2 * attn.shape[1] + 2 * query.shape[1]
    return pl.pallas_call(
        gains_kernel,
        out_shape=jax.ShapeDtypeStruct((1, columns), F32),
        in_specs=[pl.BlockSpec(memory_space=pltpu.SMEM)]
        + [pl.BlockSpec(memory_space=pltpu.VMEM)] * 4,
        out_specs=pl.BlockSpec(memory_space=pltpu.VMEM),
        cost_estimate=pl.CostEstimate(flops=0, bytes_accessed=8 * columns, transcendentals=0),
    )(indices, attn, mlp, query, key)


def own_blocks(hidden, cot, indices):
    rows, width = hidden.shape
    return pl.pallas_call(
        own_kernel,
        out_shape=jax.ShapeDtypeStruct((rows, 2 * width), BF16),
        in_specs=[pl.BlockSpec(memory_space=pltpu.SMEM)]
        + [pl.BlockSpec(memory_space=pltpu.VMEM)] * 2,
        out_specs=pl.BlockSpec(memory_space=pltpu.VMEM),
        cost_estimate=pl.CostEstimate(
            flops=0, bytes_accessed=8 * rows * width, transcendentals=0
        ),
    )(indices, hidden, cot)


def here_rows(buffers, step, rows):
    here = pl.ds(pl.multiple_of(step * rows, rows), rows)
    return jnp.concatenate([buffers[0][here, :], buffers[1][here, :]], axis=0)


def mlp_kernel(plan, chunks, *refs):
    pieces, refs = refs[: len(plan)], refs[len(plan) :]
    c_ref, w_refs, refs = refs[0], refs[1 : 1 + chunks], refs[1 + chunks :]
    right_ref, act_ref, even_ref, odd_ref, x_all = refs[:5]
    buffers, sems = refs[5:7], refs[7]
    step = pl.program_id(0)
    hidden = act_ref.shape[1]
    rows = even_ref.shape[0]
    size = even_ref.shape[1] // chunks
    fetch_pieces(step, pieces, plan, buffers, sems, rows)
    x = here_rows(buffers, step, rows)
    x_all[...] = x
    c = c_ref[...]
    both = jnp.zeros((2 * rows, 2 * hidden), F32)
    grad = jnp.zeros((2 * rows, hidden), F32)
    for number, w_ref in enumerate(w_refs):
        side = slice(number * size, (number + 1) * size)
        both += jnp.dot(x[:, side], w_ref[:, : 2 * hidden], preferred_element_type=F32)
        grad += jnp.dot(c[:, side], w_ref[:, 2 * hidden :], preferred_element_type=F32)
    gate = both[:, :hidden]
    upper = both[:, hidden:]
    sigma = jax.nn.sigmoid(gate)
    gate_sigma = gate * sigma
    act_ref[...] = (gate_sigma * upper).astype(BF16)
    right_ref[:, :hidden] = (grad * upper * sigma * (1.0 + gate * (1.0 - sigma))).astype(BF16)
    right_ref[:, hidden:] = (grad * gate_sigma).astype(BF16)
    right = right_ref[...]
    for number, w_ref in enumerate(w_refs):
        part = nt(right, w_ref[:, : 2 * hidden]).astype(BF16)
        even_ref[:, number * size : (number + 1) * size] = part[:rows]
        odd_ref[:, number * size : (number + 1) * size] = part[rows:]


def mlp_both(pieces, both_all, weights, count):
    total, width = both_all.shape
    width //= 2
    rows = total // count
    hidden = weights[0].shape[1] // 3
    block = pl.BlockSpec((rows, width), lambda step: (step, 0))

    def wide(columns):
        return pl.BlockSpec((2 * rows, columns), lambda step: (step, 0))

    return pl.pallas_call(
        functools.partial(mlp_kernel, piece_plan(pieces), len(weights)),
        out_shape=[
            jax.ShapeDtypeStruct((total, 2 * hidden), BF16),
            jax.ShapeDtypeStruct((total, hidden), BF16),
            jax.ShapeDtypeStruct((total // 2, width), BF16),
            jax.ShapeDtypeStruct((total // 2, width), BF16),
            jax.ShapeDtypeStruct((total, width), BF16),
        ],
        grid=(count // 2,),
        in_specs=in_place(pieces)
        + [pl.BlockSpec((2 * rows, width), lambda step: (step, 1))]
        + [whole(part) for part in weights],
        out_specs=[wide(2 * hidden), wide(hidden), block, block, wide(width)],
        scratch_shapes=piece_scratch(pieces, total // 2, width),
        cost_estimate=pl.CostEstimate(
            flops=10 * total * width * hidden,
            bytes_accessed=12 * total * width,
            transcendentals=total * hidden,
        ),
    )(*piece_arrays(pieces), both_all, *weights)


def grads_kernel(left_one, right_one, left_two, right_two, *out_refs):
    split = right_one.shape[1]
    for number, out_ref in enumerate(out_refs):

        @pl.when(pl.program_id(0) == number)
        def _():
            out_ref[:, :split] = transposed_times(left_one[...], right_one[...]).astype(BF16)
            out_ref[:, split:] = transposed_times(left_two[...], right_two[...]).astype(BF16)


def weight_grads(numbers, left_one, right_one, left_two, right_two, skipped=0):
    first, chunks = numbers[0], len(numbers)
    total, width = left_one.shape
    size = width // lax.axis_size(FSDP)
    columns = right_one.shape[1] + right_two.shape[1]
    block = pl.BlockSpec((total, size), lambda step: (0, first + step))
    return pl.pallas_call(
        grads_kernel,
        out_shape=[jax.ShapeDtypeStruct((size, columns), BF16)] * chunks,
        grid=(chunks,),
        in_specs=[
            block,
            whole(right_one),
            pl.BlockSpec((total, size), lambda step: (0, skipped + first + step)),
            whole(right_two),
        ],
        out_specs=[pl.BlockSpec((size, columns), lambda step: (0, 0))] * chunks,
        cost_estimate=pl.CostEstimate(
            flops=2 * total * size * chunks * columns,
            bytes_accessed=4 * total * (size * chunks + columns),
            transcendentals=0,
        ),
    )(left_one, right_one, left_two, right_two)


def rotated(values, cosine, sine_part):
    return values * cosine + pltpu.roll(values, values.shape[1] // 2, 1) * sine_part


def head_scale(raw):
    return lax.rsqrt(jnp.mean(raw * raw, axis=-1, keepdims=True) + NORM_EPS)


def head_back(grad, raw, gain_row, cosine, sine_part):
    turned = grad * cosine + pltpu.roll(grad * sine_part, grad.shape[1] // 2, 1)
    scale = head_scale(raw)
    scaled = turned * gain_row
    mean_part = jnp.mean(scaled * raw, axis=-1, keepdims=True)
    return scale * scaled - raw * (scale * scale * scale * mean_part), turned * raw * scale


def project_kernel(plan, chunks, *refs):
    pieces, refs = refs[: len(plan)], refs[len(plan) :]
    w_refs, refs = refs[:chunks], refs[chunks:]
    gain_ref, qgain_ref, kgain_ref, cos_ref, sin_ref = refs[:5]
    in_ref, raw_ref, q_ref, k_ref, v_ref, both_ref = refs[5:11]
    buffers, sems = refs[11:13], refs[13]
    step = pl.program_id(0)
    head = qgain_ref.shape[1]
    q_width = q_ref.shape[1]
    kv_width = k_ref.shape[1]
    width = in_ref.shape[1]
    size = width // chunks
    rows = in_ref.shape[0] // 2
    fetch_pieces(step, pieces, plan, buffers, sems, rows)
    both = here_rows(buffers, step, rows)
    both_ref[...] = both
    normed = rms_norm(both[:, :width].astype(F32), gain_ref[...]).astype(BF16)
    in_ref[...] = normed
    raw = jnp.zeros((2 * rows, q_width + 2 * kv_width), F32)
    for number, w_ref in enumerate(w_refs):
        raw += jnp.dot(
            normed[:, number * size : (number + 1) * size],
            w_ref[...],
            preferred_element_type=F32,
        )
    raw_ref[...] = raw[:, : q_width + kv_width]
    cosine = cos_ref[...]
    sine_part = sin_ref[...]
    for column in range(0, q_width, head):
        part = raw[:, column : column + head]
        q_ref[:, column : column + head] = rotated(
            part * head_scale(part) * qgain_ref[...], cosine, sine_part
        ).astype(BF16)
    for column in range(0, kv_width, head):
        part = raw[:, q_width + column : q_width + column + head]
        k_ref[:, column : column + head] = rotated(
            part * head_scale(part) * kgain_ref[...], cosine, sine_part
        ).astype(BF16)
    v_ref[...] = raw[:, q_width + kv_width :].astype(BF16)


def project(pieces, weights, gain, q_gain, k_gain, cosine, sine_part, q_width, kv_width):
    width = gain.shape[1]
    head = q_gain.shape[1]
    total = cosine.shape[0]
    steps = lax.axis_size(CTX) // 2
    rows = total // (2 * steps)

    def wide(columns):
        return pl.BlockSpec((2 * rows, columns), lambda step: (step, 0))

    first_columns = pl.BlockSpec(
        (weights[0].shape[0], q_width + 2 * kv_width), lambda step: (0, 0)
    )
    return pl.pallas_call(
        functools.partial(project_kernel, piece_plan(pieces), len(weights)),
        out_shape=[
            jax.ShapeDtypeStruct((total, width), BF16),
            jax.ShapeDtypeStruct((total, q_width + kv_width), F32),
            jax.ShapeDtypeStruct((total, q_width), BF16),
            jax.ShapeDtypeStruct((total, kv_width), BF16),
            jax.ShapeDtypeStruct((total, kv_width), BF16),
            jax.ShapeDtypeStruct((total, 2 * width), BF16),
        ],
        grid=(steps,),
        in_specs=in_place(pieces)
        + [first_columns] * len(weights)
        + [whole(gain), whole(q_gain), whole(k_gain), wide(head), wide(head)],
        out_specs=[
            wide(width), wide(q_width + kv_width), wide(q_width), wide(kv_width), wide(kv_width),
            wide(2 * width),
        ],
        scratch_shapes=piece_scratch(pieces, total // 2, 2 * width),
        cost_estimate=pl.CostEstimate(
            flops=2 * total * width * (q_width + 2 * kv_width),
            bytes_accessed=12 * total * width,
            transcendentals=total,
        ),
    )(*piece_arrays(pieces), *weights, gain, q_gain, k_gain, cosine, sine_part)


def nt(lhs, rhs):
    return lax.dot_general(lhs, rhs, (((1,), (1,)), ((), ())), preferred_element_type=F32)


def attend_kernel(chunks, q_ref, k_ref, v_ref, row_ref, col_ref, *refs):
    w_refs, refs = refs[:chunks], refs[chunks:]
    mix_ref, lse_ref, even_ref, odd_ref, vt_ref = refs
    kv_width = k_ref.shape[1]
    q_width = q_ref.shape[1]
    head = q_width // lse_ref.shape[0]
    group = q_width // kv_width
    scale = 1.0 / math.sqrt(head)

    @pl.when(pl.program_id(0) == 0)
    def _():
        vt_ref[...] = v_ref[...].astype(F32).T.astype(BF16)

    allowed = col_ref[...] <= row_ref[...]
    for number in range(q_width // head):
        kv = number // group * head
        column = number * head
        scores = jnp.where(
            allowed, nt(k_ref[:, kv : kv + head], q_ref[:, column : column + head]) * scale, MASKED
        )
        top = jnp.max(scores, axis=0, keepdims=True)
        raised = jnp.exp(scores - top)
        total = jnp.sum(raised, axis=0, keepdims=True)
        lse_ref[number : number + 1, :] = top + jnp.log(total)
        probs = (raised * (1.0 / total)).astype(BF16)
        mixed = jnp.dot(vt_ref[kv : kv + head, :], probs, preferred_element_type=F32)
        mix_ref[:, column : column + head] = mixed.T.astype(BF16)
    rows = even_ref.shape[0]
    size = even_ref.shape[1] // chunks
    mix = mix_ref[...]
    for number, w_ref in enumerate(w_refs):
        out = nt(mix, w_ref[...]).astype(BF16)
        even_ref[:, number * size : (number + 1) * size] = out[:rows]
        odd_ref[:, number * size : (number + 1) * size] = out[rows:]


def attend(q, k, v, pos_row, pos_col, weights, head):
    total, q_width = q.shape
    kv_width = k.shape[1]
    width = weights[0].shape[0] * len(weights)
    steps = lax.axis_size(CTX) // 2
    rows = total // (2 * steps)
    heads = q_width // head

    def wide(columns):
        return pl.BlockSpec((2 * rows, columns), lambda step: (step, 0))

    half = pl.BlockSpec((rows, width), lambda step: (step, 0))
    return pl.pallas_call(
        functools.partial(attend_kernel, len(weights)),
        out_shape=[
            jax.ShapeDtypeStruct((total, q_width), BF16),
            jax.ShapeDtypeStruct((heads, total), F32),
            jax.ShapeDtypeStruct((total // 2, width), BF16),
            jax.ShapeDtypeStruct((total // 2, width), BF16),
        ],
        grid=(steps,),
        in_specs=[
            wide(q_width), whole(k), whole(v),
            pl.BlockSpec((1, 2 * rows), lambda step: (0, step)),
            whole(pos_col),
        ]
        + [whole(part) for part in weights],
        out_specs=[
            wide(q_width), pl.BlockSpec((heads, 2 * rows), lambda step: (0, step)), half, half,
        ],
        scratch_shapes=[pltpu.VMEM((kv_width, total), BF16)],
        cost_estimate=pl.CostEstimate(
            flops=4 * total * total * q_width,
            bytes_accessed=8 * total * width,
            transcendentals=total * total * heads,
        ),
    )(q, k, v, pos_row, pos_col, *weights)


def attend_back_kernel(plan, chunks, *refs):
    pieces, refs = refs[: len(plan)], refs[len(plan) :]
    w_refs, refs = refs[:chunks], refs[chunks:]
    q_ref, k_ref, v_ref, row_ref, col_ref, mix_ref, lse_ref = refs[:7]
    raw_ref, qgain_ref, cos_ref, sin_ref = refs[7:11]
    low_ref, dk_ref, dv_ref, dgain_ref, all_ref = refs[11:16]
    buffers, sems, kt_ref = refs[16:18], refs[18], refs[19]
    step = pl.program_id(0)
    head = qgain_ref.shape[1]
    kv_width = k_ref.shape[1]
    q_width = q_ref.shape[1]
    group = q_width // kv_width
    scale = 1.0 / math.sqrt(head)
    rows = q_ref.shape[0] // 2
    size = all_ref.shape[1] // chunks

    @pl.when(pl.program_id(0) == 0)
    def _():
        kt_ref[...] = k_ref[...].astype(F32).T.astype(BF16)
        dk_ref[...] = jnp.zeros_like(dk_ref)
        dv_ref[...] = jnp.zeros_like(dv_ref)
        dgain_ref[...] = jnp.zeros_like(dgain_ref)

    fetch_pieces(step, pieces, plan, buffers, sems, rows)
    grad = here_rows(buffers, step, rows)
    all_ref[...] = grad
    dmix_all = jnp.zeros((2 * rows, q_width), F32)
    for number, w_ref in enumerate(w_refs):
        dmix_all += jnp.dot(
            grad[:, number * size : (number + 1) * size],
            w_ref[...],
            preferred_element_type=F32,
        )
    dmix_all = dmix_all.astype(BF16)
    allowed = col_ref[...] <= row_ref[...]
    for number in range(q_width // head):
        kv = number // group * head
        column = number * head
        q = q_ref[:, column : column + head]
        dmix = dmix_all[:, column : column + head]
        mix = mix_ref[:, column : column + head]
        delta = jnp.sum((dmix.astype(F32) * mix.astype(F32)).T, axis=0, keepdims=True)
        scores = nt(k_ref[:, kv : kv + head], q) * scale
        probs = jnp.exp(jnp.where(allowed, scores - lse_ref[number : number + 1, :], MASKED))
        dv_ref[:, kv : kv + head] += jnp.dot(
            probs.astype(BF16), dmix, preferred_element_type=F32
        )
        prob_grad = nt(v_ref[:, kv : kv + head], dmix)
        score_grad = (probs * (prob_grad - delta) * scale).astype(BF16)
        dk_ref[:, kv : kv + head] += jnp.dot(score_grad, q, preferred_element_type=F32)
        dq = jnp.dot(kt_ref[kv : kv + head, :], score_grad, preferred_element_type=F32).T
        raw_grad, gain_part = head_back(
            dq, raw_ref[:, column : column + head], qgain_ref[...], cos_ref[...], sin_ref[...]
        )
        low_ref[:, column : column + head] = raw_grad.astype(BF16)
        dgain_ref[...] += jnp.sum(gain_part, axis=0, keepdims=True)


def attend_back(pieces, weights, q, k, v, pos_row, pos_col, mix, lse, raw, q_gain, cosine, sine_part):
    total, q_width = q.shape
    kv_width = k.shape[1]
    width = weights[0].shape[0] * len(weights)
    steps = lax.axis_size(CTX) // 2
    rows = total // (2 * steps)
    heads = lse.shape[0]
    head = q_gain.shape[1]

    def wide(columns):
        return pl.BlockSpec((2 * rows, columns), lambda step: (step, 0))

    def fixed(shape):
        return pl.BlockSpec(shape, lambda step: (0, 0))

    return pl.pallas_call(
        functools.partial(attend_back_kernel, piece_plan(pieces), len(weights)),
        out_shape=[
            jax.ShapeDtypeStruct((total, q_width), BF16),
            jax.ShapeDtypeStruct((total, kv_width), F32),
            jax.ShapeDtypeStruct((total, kv_width), F32),
            jax.ShapeDtypeStruct((1, head), F32),
            jax.ShapeDtypeStruct((total, width), BF16),
        ],
        grid=(steps,),
        in_specs=in_place(pieces)
        + [whole(part) for part in weights]
        + [
            wide(q_width), whole(k), whole(v),
            pl.BlockSpec((1, 2 * rows), lambda step: (0, step)),
            whole(pos_col), wide(q_width),
            pl.BlockSpec((heads, 2 * rows), lambda step: (0, step)),
            wide(q_width), whole(q_gain), wide(head), wide(head),
        ],
        out_specs=[
            wide(q_width), fixed((total, kv_width)), fixed((total, kv_width)), fixed((1, head)),
            wide(width),
        ],
        scratch_shapes=piece_scratch(pieces, total // 2, width)
        + [pltpu.VMEM((kv_width, total), BF16)],
        cost_estimate=pl.CostEstimate(
            flops=10 * total * total * q_width,
            bytes_accessed=8 * total * width,
            transcendentals=total * total * heads,
        ),
    )(
        *piece_arrays(pieces), *weights,
        q, k, v, pos_row, pos_col, mix, lse, raw, q_gain, cosine, sine_part,
    )


def project_back_kernel(
    chunks, low_ref, dk_ref, dv_ref, raw_ref, kgain_ref, cos_ref, sin_ref, x_ref, act_ref, *refs
):
    w_refs, d_refs, refs = refs[:chunks], refs[chunks : 2 * chunks], refs[2 * chunks :]
    right_ref, even_ref, odd_ref, again_ref, dgain_ref = refs
    head = kgain_ref.shape[1]
    kv_width = dk_ref.shape[1]
    q_width = low_ref.shape[1]
    rows = even_ref.shape[0]
    width = x_ref.shape[1]
    size = width // chunks

    @pl.when(pl.program_id(0) == 0)
    def _():
        again_ref[...] = jnp.zeros_like(again_ref)
        dgain_ref[...] = jnp.zeros_like(dgain_ref)

    right_ref[:, :q_width] = low_ref[...]
    for column in range(0, kv_width, head):
        raw_grad, gain_part = head_back(
            dk_ref[:, column : column + head],
            raw_ref[:, q_width + column : q_width + column + head],
            kgain_ref[...],
            cos_ref[...],
            sin_ref[...],
        )
        right_ref[:, q_width + column : q_width + column + head] = raw_grad.astype(BF16)
        dgain_ref[...] += jnp.sum(gain_part, axis=0, keepdims=True)
    right_ref[:, q_width + kv_width :] = dv_ref[...].astype(BF16)
    right = right_ref[...]
    x = x_ref[...].astype(F32)
    normed = x * head_scale(x)
    for number, w_ref in enumerate(w_refs):
        side = slice(number * size, (number + 1) * size)
        part = nt(right, w_ref[...])
        again_ref[:, side] += jnp.sum(part * normed[:, side], axis=0, keepdims=True)
        part = part.astype(BF16)
        even_ref[:, side] = part[:rows]
        odd_ref[:, side] = part[rows:]
    act = act_ref[...]
    for number, d_ref in enumerate(d_refs):
        side = slice(width + number * size, width + (number + 1) * size)
        part = nt(act, d_ref[:, d_ref.shape[1] - act.shape[1] :]).astype(BF16)
        even_ref[:, side] = part[:rows]
        odd_ref[:, side] = part[rows:]


def project_back(low, dk, dv, raw, k_gain, cosine, sine_part, both_all, weights, act, mlp_parts):
    total, q_width = low.shape
    kv_width = dk.shape[1]
    width = both_all.shape[1] // 2
    steps = lax.axis_size(CTX) // 2
    rows = total // (2 * steps)
    head = k_gain.shape[1]

    def wide(columns):
        return pl.BlockSpec((2 * rows, columns), lambda step: (step, 0))

    def fixed(shape):
        return pl.BlockSpec(shape, lambda step: (0, 0))

    first_columns = pl.BlockSpec(
        (weights[0].shape[0], q_width + 2 * kv_width), lambda step: (0, 0)
    )
    hidden = act.shape[1]
    if hidden % 128:
        down_columns = whole(mlp_parts[0])
    else:
        down_columns = pl.BlockSpec((mlp_parts[0].shape[0], hidden), lambda step: (0, 2))
    both = pl.BlockSpec((rows, 2 * width), lambda step: (step, 0))
    return pl.pallas_call(
        functools.partial(project_back_kernel, len(weights)),
        out_shape=[
            jax.ShapeDtypeStruct((total, q_width + 2 * kv_width), BF16),
            jax.ShapeDtypeStruct((total // 2, 2 * width), BF16),
            jax.ShapeDtypeStruct((total // 2, 2 * width), BF16),
            jax.ShapeDtypeStruct((1, width), F32),
            jax.ShapeDtypeStruct((1, head), F32),
        ],
        grid=(steps,),
        in_specs=[
            wide(q_width), wide(kv_width), wide(kv_width), wide(q_width + kv_width),
            whole(k_gain), wide(head), wide(head), wide(width), wide(hidden),
        ]
        + [first_columns] * len(weights)
        + [down_columns] * len(weights),
        out_specs=[
            wide(q_width + 2 * kv_width), both, both, fixed((1, width)), fixed((1, head)),
        ],
        cost_estimate=pl.CostEstimate(
            flops=2 * total * width * (q_width + 2 * kv_width),
            bytes_accessed=12 * total * width,
            transcendentals=total,
        ),
    )(low, dk, dv, raw, k_gain, cosine, sine_part, both_all, act, *weights, *mlp_parts)


def on_device_all(
    hidden_in,
    pair_table,
    attn_gain,
    query_proj,
    key_proj,
    value_proj,
    query_gain,
    key_gain,
    output_proj,
    mlp_gain,
    gate_proj,
    up_proj,
    down_proj,
    cotangent,
):
    fsdp_count = lax.axis_size(FSDP)
    fsdp_index = lax.axis_index(FSDP)
    ctx_count = lax.axis_size(CTX)
    ctx_index = lax.axis_index(CTX)
    row_count, width = hidden_in.shape[1:]
    block_len = row_count // 2
    total_rows = ctx_count * row_count
    shard_rows = width // fsdp_count
    head_width = query_gain.shape[0]
    half_head = head_width // 2
    kvhead_total = key_proj.shape[1] // head_width
    kv_count = max(1, kvhead_total // ctx_count)
    kv_share = max(1, ctx_count // kvhead_total)
    query_width = query_proj.shape[1] // ctx_count
    kv_width = kv_count * head_width
    kv_own = key_proj.shape[1] // ctx_count
    hidden_width = gate_proj.shape[1] // ctx_count

    fsdp_order = fsdp_index ^ jnp.arange(fsdp_count, dtype=jnp.int32)

    def block_order(values):
        return jnp.concatenate(
            [
                lax.dynamic_slice_in_dim(
                    values, (fsdp_index ^ number) * shard_rows, shard_rows, axis=values.ndim - 1
                )
                for number in range(fsdp_count)
            ],
            axis=-1,
        )

    def columns(weights, start, size):
        return lax.dynamic_slice_in_dim(weights, start, size, axis=1)

    kv_index = ctx_index // kv_share
    both_own = own_blocks(hidden_in[0], cotangent[0], fsdp_order)
    inputs = both_own[:, :width]
    cot_low = both_own[:, width:]
    gains_rel = block_order(jnp.stack([attn_gain, mlp_gain]))
    attn_gain_rel = gains_rel[0]
    mlp_gain_rel = gains_rel[1]
    fsdp_levels = (fsdp_count - 1).bit_length()
    attn_width = query_width + 2 * kv_width

    both_pieces = gather_ctx(both_own)
    first_shard = pick_columns(
        [
            (query_proj, ctx_index, query_width),
            (key_proj, kv_index, kv_width),
            (value_proj, kv_index, kv_width),
        ]
    )
    first_blocks = {0: first_shard}
    for level in range(1, fsdp_levels + 1):
        first_blocks = gather_fsdp_step(first_blocks, fsdp_count, level)
    first_parts = [first_blocks[number] for number in range(fsdp_count)]
    output_shard = pick_columns([(output_proj, ctx_index, query_width)])
    output_parts = [output_shard] + [
        exchange(output_shard, number, FSDP) for number in range(1, fsdp_count)
    ]
    mlp_shard = pick_columns(
        [(weights, ctx_index, hidden_width) for weights in (gate_proj, up_proj, down_proj)]
    )
    mlp_blocks = gather_fsdp_step({0: mlp_shard}, fsdp_count, 1)

    owner_ids = ctx_index ^ jnp.arange(ctx_count, dtype=jnp.int32)
    picked = owner_ids[:, None] == jnp.arange(ctx_count, dtype=jnp.int32)[None, :]
    block_ids = jnp.sum(jnp.where(picked[:, :, None], pair_table[None], 0), axis=1)
    positions = (
        block_ids[:, :, None] * block_len + jnp.arange(block_len, dtype=jnp.int32)
    ).reshape(total_rows)
    pos_row = positions.reshape(1, total_rows)
    pos_col = positions.reshape(total_rows, 1)
    lanes = jnp.arange(head_width, dtype=jnp.int32)
    frequency = ROPE_BASE ** (-((lanes % half_head).astype(F32) * 2.0 / head_width))
    angles = positions.astype(F32)[:, None] * frequency[None, :]
    cosine = jnp.cos(angles)
    sine_part = jnp.sin(angles) * jnp.where(lanes < half_head, -1.0, 1.0)[None, :]

    query_row = query_gain.reshape(1, head_width)
    key_row = key_gain.reshape(1, head_width)
    attn_in, attn_raw, query_heads, key_heads, value_heads, both_all = project(
        both_pieces, first_parts, attn_gain_rel.reshape(1, width), query_row, key_row,
        cosine, sine_part, query_width, kv_width,
    )
    attn_mix, log_total, mix_even, mix_odd = attend(
        query_heads, key_heads, value_heads, pos_row, pos_col, output_parts, head_width
    )

    resid_sum = scatter_ctx(mix_even, mix_odd)
    resid = inputs.astype(F32) + resid_sum
    mlp_in = rms_norm(resid, mlp_gain_rel).astype(BF16)
    for level in range(2, fsdp_levels + 1):
        mlp_blocks = gather_fsdp_step(mlp_blocks, fsdp_count, level)
    mlp_parts = [mlp_blocks[number] for number in range(fsdp_count)]
    mlp_pieces = gather_ctx(mlp_in)
    mlp_right, hidden_act, part_even, part_odd, mlp_all = mlp_both(
        mlp_pieces, both_all, mlp_parts, ctx_count
    )
    mlp_in_grad = scatter_ctx(part_even, part_odd)
    last = fsdp_count - 1

    def all_grads(*operands):
        sums = {last: weight_grads([last], *operands)[0]}
        if last:
            numbers = list(range(last))
            sums.update(zip(numbers, weight_grads(numbers, *operands)))
        return sums

    mlp_sums = all_grads(mlp_all, mlp_right, both_all, hidden_act, fsdp_count)
    resid_part, mlp_gain_grad = jax.vjp(rms_norm, resid, mlp_gain_rel)[1](mlp_in_grad)
    resid_grad = cot_low.astype(F32) + resid_part
    resid_low = resid_grad.astype(BF16)
    for level in range(fsdp_levels, 1, -1):
        mlp_sums = scatter_fsdp_step(mlp_sums, fsdp_count, level)
    resid_pieces = gather_ctx(resid_low)
    mlp_moved = {
        number: exchange(mlp_sums[number].astype(BF16), number, FSDP)
        for number in range(1, fsdp_count)
        if level_of(number) == 1
    }
    query_low, key_grad, value_grad, query_gain_grad, resid_all = attend_back(
        resid_pieces, output_parts, query_heads, key_heads, value_heads, pos_row, pos_col,
        attn_mix, log_total, attn_raw, query_row, cosine, sine_part,
    )
    bit = 1
    while bit < kv_share:
        moved = exchange(jnp.concatenate([key_grad, value_grad], axis=1), bit, CTX)
        moved = moved.reshape(ctx_count, row_count, 2 * kv_width)
        moved = jnp.concatenate([moved[number ^ bit] for number in range(ctx_count)], axis=0)
        key_grad = key_grad + moved[:, :kv_width]
        value_grad = value_grad + moved[:, kv_width:]
        bit *= 2
    own_parts = first_parts
    own_start = (ctx_index % kv_share) * kv_own
    if kv_share > 1:
        place = jnp.arange(attn_width) - query_width
        owned = (place < 0) | (
            (place % kv_width >= own_start) & (place % kv_width < own_start + kv_own)
        )
        own_parts = [
            jnp.where(owned[None, :], part[:, :attn_width], 0).astype(BF16)
            for part in first_parts
        ]
    attn_right, tail_even, tail_odd, attn_gain_grad, key_gain_grad = project_back(
        query_low, key_grad, value_grad, attn_raw, key_row, cosine, sine_part,
        both_all, own_parts, hidden_act, mlp_parts,
    )
    if kv_share > 1:
        attn_right = jnp.concatenate(
            [
                attn_right[:, :query_width],
                columns(attn_right, query_width + own_start, kv_own),
                columns(attn_right, query_width + kv_width + own_start, kv_own),
            ],
            axis=1,
        )
        key_gain_grad = jnp.where(ctx_index % kv_share == 0, key_gain_grad, 0.0)
    attn_sums = all_grads(attn_in, attn_right, resid_all, attn_mix)
    for level in range(fsdp_levels, 0, -1):
        attn_sums = scatter_fsdp_step(attn_sums, fsdp_count, level)
    attn_grads = attn_sums[0].astype(BF16)
    both_sums = scatter_ctx(tail_even, tail_odd, True)
    attn_in_grad = both_sums[:, :width]
    block_out = (resid + both_sums[:, width:]).astype(BF16)
    mlp_total = mlp_sums[0].astype(F32)
    for moved in mlp_moved.values():
        mlp_total = mlp_total + moved.astype(F32)
    mlp_grads = mlp_total.astype(BF16)
    own_wide = inputs.astype(F32)
    input_part = jax.vjp(lambda values: rms_norm(values, attn_gain_rel), own_wide)[1](
        attn_in_grad
    )[0]
    input_grad = resid_grad + input_part
    gains = join_gains(
        attn_gain_grad, mlp_gain_grad.reshape(1, width), query_gain_grad, key_gain_grad,
        fsdp_order,
    )
    gains = sum_all(gains)[0]
    outs = (
        block_order(block_out)[None],
        block_order(input_grad)[None],
        gains[:width],
        gains[2 * width : 2 * width + head_width],
        gains[2 * width + head_width :],
        gains[width : 2 * width],
    )
    mlp_pieces = gather_ctx(mlp_grads)
    mlp_outs = place_columns(mlp_pieces, (hidden_width,) * 3, ctx_index)
    attn_pieces = gather_ctx(attn_grads)
    last_piece, *outs = tie(attn_pieces[-1][2], *outs)
    attn_pieces[-1] = attn_pieces[-1][:2] + (last_piece,)
    attn_outs = place_columns(attn_pieces, (query_width, kv_own, kv_own, query_width), ctx_index)
    return (
        outs[0],
        outs[1],
        outs[2],
        attn_outs[0],
        attn_outs[1],
        attn_outs[2],
        outs[3],
        outs[4],
        attn_outs[3],
        outs[5],
        mlp_outs[0],
        mlp_outs[1],
        mlp_outs[2],
    )


def solution(mesh):
    in_specs = (
        P(FSDP, CTX, None),
        P(),
        P(),
        P(FSDP, None),
        P(FSDP, None),
        P(FSDP, None),
        P(),
        P(),
        P(FSDP, None),
        P(),
        P(FSDP, None),
        P(FSDP, None),
        P(FSDP, None),
        P(FSDP, CTX, None),
    )
    out_specs = (
        P(FSDP, CTX, None),
        P(FSDP, CTX, None),
        P(),
        P(FSDP, None),
        P(FSDP, None),
        P(FSDP, None),
        P(),
        P(),
        P(FSDP, None),
        P(),
        P(FSDP, None),
        P(FSDP, None),
        P(FSDP, None),
    )
    return jax.shard_map(
        on_device_all, mesh=mesh, in_specs=in_specs, out_specs=out_specs, check_vma=False
    )
```
